32 devices in a mesh: seq: 4 (over y, x), fsdp: 4 (over z), tensor: 2 (over core).
Axes of the slice: x: 2, y: 2, z: 4, core: 2. Of those that a mesh axis runs over, the one named last changes fastest.
Arguments:
- inputs: bfloat16 [8192, 2560], P(('seq', 'fsdp')), may hold values from -6 to 6
- cotangent: bfloat16 [8192, 2560], P(('seq', 'fsdp')), may hold values from -6 to 6
- gain_attn: bfloat16 [2560], P('fsdp'), may hold values from 0.099609375 to 1.8984375
- gain_ffn: bfloat16 [2560], P('fsdp'), may hold values from 0.099609375 to 1.8984375
- w_query: bfloat16 [2560, 2560], P('fsdp', 'tensor'), may hold values from -0.125 to 0.125
- w_key: bfloat16 [2560, 256], P('fsdp'), may hold values from -0.125 to 0.125
- w_value: bfloat16 [2560, 256], P('fsdp'), may hold values from -0.125 to 0.125
- w_out: bfloat16 [2560, 2560], P('tensor', 'fsdp'), may hold values from -3.5 to 3.5
- w_gate: bfloat16 [2560, 7680], P('fsdp', 'tensor'), may hold values from -0.125 to 0.125
- w_up: bfloat16 [2560, 7680], P('fsdp', 'tensor'), may hold values from -0.125 to 0.125
- w_down: bfloat16 [7680, 2560], P('tensor', 'fsdp'), may hold values from -0.0625 to 0.0625
Outputs:
- layer_out: bfloat16 [8192, 2560], P(('seq', 'fsdp'))
- grad_input: float32 [8192, 2560], P(('seq', 'fsdp'))
- grad_gain_attn: float32 [2560], P('fsdp')
- grad_gain_ffn: float32 [2560], P('fsdp')
- grad_w_query: float32 [2560, 2560], P('fsdp', 'tensor')
- grad_w_key: float32 [2560, 256], P('fsdp')
- grad_w_value: float32 [2560, 256], P('fsdp')
- grad_w_out: float32 [2560, 2560], P('tensor', 'fsdp')
- grad_w_gate: float32 [2560, 7680], P('fsdp', 'tensor')
- grad_w_up: float32 [2560, 7680], P('fsdp', 'tensor')
- grad_w_down: float32 [7680, 2560], P('tensor', 'fsdp')
The draws below stay inside these ranges and needn't reach their ends.
All inputs are finite; a program needn't handle non-finite values.
Results may differ from the reference program's by a relative error of at most 0.014.
Values may be sent and summed in bfloat16 or wider, within the bound.
A program may use at most 320 MiB of HBM per device.

```python
import math
import jax
import jax.numpy as jnp
from jax import lax

D = 2560
HEADS = 10
HEAD = 256
FF = 7680
WINDOW = 2048
ROT = 128
SEQ_LEN = 8192


def steps_of(stream_key, shape, pieces, smallest, high):
    level = 1.0
    for dim, blocks in pieces:
        steps = jax.random.uniform(jax.random.fold_in(jax.random.fold_in(stream_key, 6), dim), (blocks,), jnp.float32, smallest / len(pieces), high / len(pieces))
        level = level * jnp.repeat(jnp.exp(steps), shape[dim] // blocks).reshape((-1,) + (1,) * (len(shape) - 1 - dim))
    return level


def centred(stream_key, shape, width, bound, split=(), kind=jnp.bfloat16):
    values = jax.random.normal(stream_key, shape, jnp.float32) * width
    if len(split) > 0:
        values = steps_of(stream_key, shape, split, -0.22, 0.18) * values
    return jnp.clip(values, min=-bound, max=bound).astype(kind)


def setup_inputs(seed: int = 0) -> dict:
    splits = jax.random.split(jax.random.key(seed), 12)
    inputs = centred(splits[0], (SEQ_LEN, D), 1.0, 6.0, ((0, 16),))
    cotangent = centred(splits[1], (SEQ_LEN, D), 1.0, 6.0, ((0, 16),))
    gain_attn = jnp.clip(1.0 + 0.18 * jax.random.normal(splits[2], (D,), jnp.float32), 0.099609375, 1.8984375).astype(jnp.bfloat16)
    gain_ffn = jnp.clip(1.0 + 0.18 * jax.random.normal(splits[3], (D,), jnp.float32), 0.099609375, 1.8984375).astype(jnp.bfloat16)
    w_query = centred(splits[4], (D, HEADS * HEAD), D ** -0.5, 0.125, ((0, 4), (1, 2)))
    w_key = centred(splits[5], (D, HEAD), D ** -0.5, 0.125, ((0, 4),))
    w_value = centred(splits[6], (D, HEAD), D ** -0.5, 0.125, ((0, 4),))
    w_out = centred(splits[7], (HEADS * HEAD, D), (max(1, HEADS * HEAD * 3 // WINDOW)) ** -0.5, 3.5, ((0, 2), (1, 4)))
    w_gate = centred(splits[8], (D, FF), D ** -0.5, 0.125, ((0, 4), (1, 2)))
    w_up = centred(splits[9], (D, FF), D ** -0.5, 0.125, ((0, 4), (1, 2)))
    w_down = centred(splits[10], (FF, D), FF ** -0.5, 0.0625, ((0, 2), (1, 4)))
    return dict(inputs=inputs, cotangent=cotangent, gain_attn=gain_attn, gain_ffn=gain_ffn, w_query=w_query, w_key=w_key, w_value=w_value, w_out=w_out, w_gate=w_gate, w_up=w_up, w_down=w_down)


@jax.custom_vjp
def low(v):
    return lax.optimization_barrier(v.astype(jnp.bfloat16)).astype(jnp.float32)

@jax.custom_vjp
def low_back(v):
    return v

def low_keep(v):
    return (low(v), None)

def low_pass(kept, grad):
    return (grad,)

def back_keep(v):
    return (v, None)

def back_low(kept, grad):
    return (low(grad),)
low.defvjp(low_keep, low_pass)
low_back.defvjp(back_keep, back_low)

def matmul(left, right):
    return jnp.dot(left, right, precision=lax.Precision.HIGHEST, preferred_element_type=jnp.float32)

def rms_norm(values, gain):
    return values * lax.rsqrt(lax.optimization_barrier(jnp.mean(values * values, axis=-1, keepdims=True)) + 1e-06) * gain

def rotate(values, angles, sign):
    half = angles.shape[-1]
    cosine = jnp.cos(angles)
    sine = sign * jnp.sin(angles)
    first_part = values[..., :half]
    second_part = values[..., half:2 * half]
    return jnp.concatenate([first_part * cosine - second_part * sine, second_part * cosine + first_part * sine, values[..., 2 * half:]], axis=-1)

def attend(queries, key_rows, value_rows):
    length = queries.shape[0]
    query_block = math.gcd(length, 512)
    count_blocks = length // query_block
    padding = jnp.zeros((WINDOW, HEAD), jnp.float32)
    key_padded = jnp.concatenate([padding, key_rows], axis=0)
    value_padded = jnp.concatenate([padding, value_rows], axis=0)
    query_at = jnp.arange(query_block, dtype=jnp.int32)[:, None]
    key_at = jnp.arange(query_block + WINDOW, dtype=jnp.int32)[None, :]

    def one_block(index):
        start = (index * query_block).astype(jnp.int32)
        query_part = lax.dynamic_slice_in_dim(queries, start, query_block, 0)
        key_part = lax.dynamic_slice_in_dim(key_padded, start, query_block + WINDOW, 0)
        value_part = lax.dynamic_slice_in_dim(value_padded, start, query_block + WINDOW, 0)
        scores = jnp.einsum('qhd,kd->hqk', query_part, key_part, precision=lax.Precision.HIGHEST)
        scores = low_back(scores)
        allowed = (key_at > query_at) & (key_at <= query_at + WINDOW) & (start - WINDOW + key_at >= 0)
        scores = jnp.where(allowed[None], scores, -1e+30)
        row_max = lax.optimization_barrier(jnp.max(scores, axis=-1, keepdims=True))
        expon = jnp.exp(scores - row_max)
        probability = expon / lax.optimization_barrier(jnp.sum(expon, axis=-1, keepdims=True))
        return jnp.einsum('hqk,kd->qhd', low(probability), value_part, precision=lax.Precision.HIGHEST)
    outputs = lax.map(jax.checkpoint(one_block), jnp.arange(count_blocks, dtype=jnp.int32))
    return outputs.reshape(length, HEADS, HEAD)

def forward(source, gain_attn, gain_ffn, w_query, w_key, w_value, w_out, w_gate, w_up, w_down):
    positions = jnp.arange(SEQ_LEN, dtype=jnp.int32).astype(jnp.float32)
    frequency = 10000.0 ** (-(jnp.arange(ROT // 2, dtype=jnp.float32) * 2.0) / ROT)
    angles = positions[:, None] * frequency[None, :]
    normed_attn = low(rms_norm(source, gain_attn))
    query_proj = low_back(matmul(normed_attn, w_query)).reshape(SEQ_LEN, HEADS, HEAD)
    queries = low(rotate(query_proj, angles[:, None, :], 1.0) * HEAD ** (-0.5))
    key_rows = low(rotate(low_back(matmul(normed_attn, w_key)), angles, 1.0))
    value_rows = low(low_back(matmul(normed_attn, w_value)))
    head_outputs = low(low_back(attend(queries, key_rows, value_rows))).reshape(SEQ_LEN, HEADS * HEAD)
    hidden_in = source + low_back(matmul(head_outputs, w_out))
    normed_ffn = low(rms_norm(hidden_in, gain_ffn))
    gate_pre = low_back(matmul(normed_ffn, w_gate))
    up_proj = low_back(matmul(normed_ffn, w_up))
    activation = low(jax.nn.gelu(gate_pre) * up_proj)
    return hidden_in + low_back(matmul(activation, w_down))

def reference(inputs, cotangent, gain_attn, gain_ffn, w_query, w_key, w_value, w_out, w_gate, w_up, w_down):
    primals = (inputs, gain_attn, gain_ffn, w_query, w_key, w_value, w_out, w_gate, w_up, w_down)
    primals = tuple((item.astype(jnp.float32) for item in primals))
    result, pullback = jax.vjp(forward, *primals)
    grads = pullback(cotangent.astype(jnp.float32))
    return (result.astype(jnp.bfloat16), grads[0], grads[1], grads[2], grads[3], grads[4], grads[5], grads[6], grads[7], grads[8], grads[9])
```

```python
import jax
import jax.numpy as jnp
from jax import lax
from jax.sharding import PartitionSpec as P

WINDOW = 2048
EPSILON = 1e-06
F32 = jnp.float32
BF16 = jnp.bfloat16


def exchange(value, step):
    count = lax.axis_size("seq")
    return lax.ppermute(value, "seq", [(at, at ^ step) for at in range(count)])


def swap(value):
    return lax.ppermute(value, "tensor", [(0, 1), (1, 0)])


def seq_shift(value, steps):
    count = lax.axis_size("seq")
    leading, last = (max(0, -steps), min(count, count - steps))
    return lax.ppermute(value, "seq", [(at, at + steps) for at in range(leading, last)])


def plane_gather(value):
    count = lax.axis_size("seq")
    if count != 4:
        return [value] + [exchange(value, step) for step in range(1, count)]
    half = value.shape[0] // 2
    near_one, near_two = exchange(value, 1), exchange(value, 2)
    far = jnp.concatenate([exchange(near_two[:half], 1), exchange(near_one[half:], 2)], axis=0)
    return [value, near_one, near_two, far]


def plane_scatter(own, others):
    total = own.astype(F32)
    for step, part in enumerate(others, 1):
        total = total + exchange(part.astype(BF16), step).astype(F32)
    return total


def times_transpose(left, right):
    return lax.dot_general(left, right, (((1,), (1,)), ((), ())), preferred_element_type=F32)


def rows_product(left, right):
    return lax.dot_general(left, right, (((0,), (0,)), ((), ())), preferred_element_type=F32)


def rotate(values, cosine, sine):
    half = cosine.shape[-1]
    first_part = values[..., :half]
    second_part = values[..., half : 2 * half]
    return jnp.concatenate(
        [
            first_part * cosine - second_part * sine,
            second_part * cosine + first_part * sine,
            values[..., 2 * half :],
        ],
        axis=-1,
    )


def inverse_rms(values):
    return lax.rsqrt(jnp.mean(values * values, axis=-1, keepdims=True) + EPSILON)


def norm_pull(values, inverse, grad):
    unit = values * inverse
    return inverse * (grad - unit * jnp.mean(grad * unit, axis=-1, keepdims=True))


def gated_unit(gate_pre, up_proj):
    return jax.nn.gelu(gate_pre) * up_proj


def pick(stacked, at):
    return lax.dynamic_index_in_dim(stacked, at, 0, keepdims=False)


def after(value, *others):
    return lax.optimization_barrier((value, *others))[0]


def part_of(value, at, size, axis):
    return lax.dynamic_slice_in_dim(value, at * size, size, axis)


def local(
    inputs, cotangent, gain_attn, gain_ffn, w_query, w_key, w_value, w_out, w_gate, w_up, w_down
):
    rows, width = inputs.shape
    half = rows // 2
    head_size = w_key.shape[1]
    head_cols = w_query.shape[1]
    heads_here = head_cols // head_size
    seqs, shards = lax.axis_size("seq"), lax.axis_size("fsdp")
    assert rows * shards == WINDOW and lax.axis_size("tensor") == 2
    seq_at, shard_at, core = (lax.axis_index(name) for name in ("seq", "fsdp", "tensor"))
    first = core == 0
    key_span = rows + WINDOW
    first_pos = (seq_at * shards + shard_at) * rows
    scale = head_size ** (-0.5)
    rot_half = head_size // 4
    frequency = 10000.0 ** (-(jnp.arange(rot_half, dtype=F32) * 2.0) / (2 * rot_half))
    angles = (first_pos + jnp.arange(rows, dtype=jnp.int32)).astype(F32)[:, None] * frequency[None]
    cosine, sine = jnp.cos(angles), jnp.sin(angles)

    def my_half(value):
        return part_of(value, core, half, 0)

    def other_half(value):
        return part_of(value, 1 - core, half, 0)

    def whole_rows(own):
        other = swap(own)
        return jnp.where(first, jnp.stack([own, other]), jnp.stack([other, own])).reshape(
            rows, own.shape[1]
        )

    def plane_rows(own, other=None):
        near = plane_gather(own)
        far = [swap(piece) if at or other is None else other for at, piece in enumerate(near)]
        return jnp.concatenate(near + far, axis=0)

    def plane_sum(partial):
        count = seqs * half
        cores = partial[:count].astype(F32) + swap(partial[count:].astype(BF16)).astype(F32)
        return plane_scatter(cores[:half], [cores[j * half : (j + 1) * half] for j in range(1, seqs)])

    def order_cols(pieces):
        stacked = jnp.stack(pieces)
        return [pick(stacked, seq_at ^ at) for at in range(seqs)]

    gain_one, gain_two = gain_attn.astype(F32)[:, None], gain_ffn.astype(F32)[:, None]
    gains = jnp.stack([gain_attn, gain_ffn])
    gains = jnp.stack(
        [gains]
        + [
            lax.ppermute(gains, "fsdp", [((at + by) % shards, at) for at in range(shards)])
            for by in range(1, shards)
        ]
    )
    gains = jnp.concatenate(
        [pick(gains, (at - shard_at) % shards) for at in range(shards)], axis=1
    ).astype(F32)
    pair_shard = jnp.where(first, w_key, w_value)
    proj_shard = jnp.concatenate([w_query, pair_shard], axis=1)
    proj_cols = proj_shard.shape[1] // seqs
    proj_weight = lax.all_gather(
        part_of(proj_shard, seq_at, proj_cols, 1), "fsdp", axis=0, tiled=True
    )
    out_rows = head_cols // seqs
    out_quarter = lax.all_gather(
        part_of(w_out, seq_at, out_rows, 0), "fsdp", axis=1, tiled=True
    )
    hidden = w_gate.shape[1] // seqs
    pair_in = jnp.concatenate(
        [part_of(w_gate, seq_at, hidden, 1), part_of(w_up, seq_at, hidden, 1)], axis=1
    )
    in_weight = lax.all_gather(pair_in, "fsdp", axis=0, tiled=True)
    down_weight = lax.all_gather(
        part_of(w_down, seq_at, hidden, 0), "fsdp", axis=1, tiled=True
    )

    source = inputs.astype(F32)
    inverse_one = inverse_rms(source)
    unit_one = (source * inverse_one * gains[0]).astype(BF16)
    rows_one = plane_rows(my_half(unit_one), other_half(unit_one))
    proj = jnp.dot(rows_one, proj_weight, preferred_element_type=F32)
    rotate_first = proj_cols % (2 * rot_half) == 0
    if rotate_first:
        halves_at = jnp.where(first, jnp.arange(2), 1 - jnp.arange(2))[:, None, None]
        seqs_at = (seq_at ^ jnp.arange(seqs))[None, :, None]
        row_pos = (
            (seqs_at * shards + shard_at) * rows + halves_at * half + jnp.arange(half)[None, None]
        ).reshape(-1)
        row_angles = row_pos.astype(F32)[:, None] * frequency[None]
        units = proj_cols // (2 * rot_half)
        unit_at = seq_at * units + jnp.arange(units)
        head_units = head_cols // (2 * rot_half)
        turned = (unit_at % 2 == 0) & (first | (unit_at < head_units))
        unit_scale = jnp.where(unit_at < head_units, scale, 1.0)[None, :, None]
        turned = turned[None, :, None]
        row_cos = jnp.where(turned, jnp.cos(row_angles)[:, None], 1.0) * unit_scale
        row_sin = jnp.where(turned, jnp.sin(row_angles)[:, None], 0.0) * unit_scale
        proj = rotate(proj.reshape(-1, units, 2 * rot_half), row_cos, row_sin)
    proj = proj.astype(BF16).reshape(2, seqs, half, proj_cols)
    proj = jnp.where(first, proj, proj[::-1])
    proj_parts = [proj[:, 0].reshape(rows, proj_cols)] + [
        exchange(proj[:, at].reshape(rows, proj_cols), at) for at in range(1, seqs)
    ]
    proj_here = jnp.concatenate(order_cols(proj_parts), axis=1)
    queries = proj_here[:, :head_cols].reshape(rows, heads_here, head_size)
    pair_here = proj_here[:, head_cols:]
    if not rotate_first:
        queries = (rotate(queries.astype(F32), cosine[:, None], sine[:, None]) * scale).astype(BF16)
        pair_here = jnp.where(first, rotate(pair_here.astype(F32), cosine, sine), pair_here)
        pair_here = pair_here.astype(BF16)

    earlier = seq_shift(pair_here, 1)
    slots = [
        lax.ppermute(
            jnp.where(shard_at >= at, earlier, pair_here),
            "fsdp", [(source_at, (source_at - at) % shards) for source_at in range(shards)],
        )
        for at in range(1, shards)
    ]
    window_here = jnp.concatenate([earlier] + slots + [pair_here], axis=0)
    window_other = swap(window_here)
    key_rows = jnp.where(first, window_here, window_other)
    value_rows = jnp.where(first, window_other, window_here)

    query_at = jnp.arange(rows, dtype=jnp.int32)[:, None]
    key_at = jnp.arange(key_span, dtype=jnp.int32)[None, :]
    allowed = (
        (key_at > query_at) & (key_at <= query_at + WINDOW) & (first_pos - WINDOW + key_at >= 0)
    )

    def score_all():
        raw_scores = jnp.einsum("rhd,kd->hrk", queries, key_rows, preferred_element_type=F32)
        return jnp.where(allowed[None], raw_scores, -1e30)

    scores = score_all()
    row_max = jnp.max(scores, axis=-1, keepdims=True)
    expon = jnp.exp(scores - row_max)
    denominator = jnp.sum(expon, axis=-1, keepdims=True)
    probability = expon / denominator
    log_total = row_max + jnp.log(denominator)
    attended = jnp.einsum(
        "hrk,kd->rhd", probability.astype(BF16), value_rows, preferred_element_type=F32
    )
    head_outputs = attended.reshape(rows, head_cols).astype(BF16)

    out_weight = jnp.zeros((head_cols, width), BF16)
    for at, piece in enumerate(plane_gather(out_quarter)):
        out_weight = lax.dynamic_update_slice_in_dim(
            out_weight, piece, (seq_at ^ at) * out_rows, 0
        )
    out_part = jnp.dot(head_outputs, out_weight, preferred_element_type=F32)
    hidden_in = my_half(source) + my_half(out_part) + swap(other_half(out_part))
    inverse_two = inverse_rms(hidden_in)
    unit_two = (hidden_in * inverse_two * gains[1]).astype(BF16)
    rows_two = plane_rows(unit_two)
    cot_later = after(cotangent, window_here)
    rows_cot = plane_rows(my_half(cot_later), other_half(cot_later))

    in_proj = jnp.dot(rows_two, in_weight, preferred_element_type=F32)
    gate_pre, up_proj = in_proj[:, :hidden], in_proj[:, hidden:]
    activation = gated_unit(gate_pre, up_proj).astype(BF16)
    grad_activation = times_transpose(rows_cot, down_weight)
    grad_gate, grad_up = jax.vjp(gated_unit, gate_pre, up_proj)[1](grad_activation)
    grad_in = jnp.concatenate([grad_gate.astype(BF16), grad_up.astype(BF16)], axis=1)
    grad_unit_two = plane_sum(times_transpose(grad_in, in_weight))
    grad_hidden = my_half(cotangent).astype(F32) + norm_pull(
        hidden_in, inverse_two, grad_unit_two * gains[1]
    )
    ffn_out = plane_sum(
        jnp.dot(after(activation, grad_unit_two), down_weight, preferred_element_type=F32)
    )
    layer_out = whole_rows((hidden_in + ffn_out).astype(BF16))

    in_term = rows_product(rows_two, grad_in).astype(BF16)
    down_term = rows_product(activation, rows_cot).astype(BF16)
    in_shard = lax.psum_scatter(in_term, "fsdp", scatter_dimension=0, tiled=True)
    down_shard = lax.psum_scatter(down_term, "fsdp", scatter_dimension=1, tiled=True)
    in_parts = order_cols(plane_gather(in_shard))
    gate_grad = jnp.concatenate([piece[:, :hidden] for piece in in_parts], axis=1).astype(F32)
    up_grad = jnp.concatenate([piece[:, hidden:] for piece in in_parts], axis=1).astype(F32)
    down_grad = jnp.concatenate(order_cols(plane_gather(down_shard)), axis=0).astype(F32)
    gain_two_half = jnp.sum(
        gate_grad * w_gate.astype(F32) + up_grad * w_up.astype(F32), axis=1
    ) / gain_two[:, 0]

    grad_attn_out = after(whole_rows(grad_hidden.astype(BF16)), in_term, down_term)
    grad_heads = (
        times_transpose(grad_attn_out, out_weight)
        .reshape(rows, heads_here, head_size)
        .astype(BF16)
    )
    out_term = rows_product(head_outputs, grad_attn_out).astype(BF16)
    out_sum = plane_scatter(
        part_of(out_term, seq_at, out_rows, 0),
        [part_of(out_term, seq_at ^ at, out_rows, 0) for at in range(1, seqs)],
    ).astype(BF16)
    out_shard = lax.psum_scatter(out_sum, "fsdp", scatter_dimension=1, tiled=True)
    out_grad = jnp.concatenate(order_cols(plane_gather(out_shard)), axis=0).astype(F32)

    probability_again = jnp.exp(score_all() - log_total)
    grad_probability = jnp.einsum(
        "rhd,kd->hrk", grad_heads, value_rows, preferred_element_type=F32
    )
    inner = jnp.sum(probability_again * grad_probability, axis=-1, keepdims=True)
    grad_scores = (probability_again * (grad_probability - inner)).astype(BF16)
    grad_queries = jnp.einsum("hrk,kd->rhd", grad_scores, key_rows, preferred_element_type=F32)
    grad_query_proj = (
        rotate(grad_queries * scale, cosine[:, None], -sine[:, None])
        .astype(BF16)
        .reshape(rows, head_cols)
    )
    grad_keys = jnp.einsum("hrk,rhd->kd", grad_scores, queries, preferred_element_type=F32)
    grad_values = jnp.einsum(
        "hrk,rhd->kd", probability_again.astype(BF16), grad_heads, preferred_element_type=F32
    )
    pair_grads = jnp.where(first, grad_keys, grad_values) + swap(
        jnp.where(first, grad_values, grad_keys)
    )
    returned = [
        lax.ppermute(
            pair_grads[at * rows : (at + 1) * rows].astype(BF16),
            "fsdp", [((source_at - at) % shards, source_at) for source_at in range(shards)],
        ).astype(F32)
        for at in range(1, shards)
    ]
    own_total = pair_grads[shards * rows :]
    earlier_total = pair_grads[:rows]
    for at, piece in enumerate(returned, 1):
        own_total = own_total + jnp.where(shard_at >= at, 0.0, piece)
        earlier_total = earlier_total + jnp.where(shard_at >= at, piece, 0.0)
    own_total = own_total + seq_shift(earlier_total.astype(BF16), -1).astype(F32)
    grad_pair = jnp.where(first, rotate(own_total, cosine, -sine), own_total).astype(BF16)
    grad_proj = jnp.concatenate([grad_query_proj, grad_pair], axis=1)
    grad_parts = [part_of(grad_proj, seq_at, proj_cols, 1)] + [
        exchange(part_of(grad_proj, seq_at ^ at, proj_cols, 1), at) for at in range(1, seqs)
    ]
    grad_rows = jnp.stack(grad_parts).reshape(seqs, 2, half, proj_cols).swapaxes(0, 1)
    grad_rows = jnp.where(first, grad_rows, grad_rows[::-1]).reshape(2 * seqs * half, proj_cols)

    proj_term = rows_product(rows_one, grad_rows).astype(BF16)
    grad_unit_one = plane_sum(times_transpose(grad_rows, proj_weight))
    grad_input = whole_rows(
        grad_hidden + norm_pull(my_half(source), my_half(inverse_one), grad_unit_one * gains[0])
    )
    proj_sum = lax.psum_scatter(proj_term, "fsdp", scatter_dimension=0, tiled=True)
    proj_grad = jnp.concatenate(order_cols(plane_gather(proj_sum)), axis=1).astype(F32)
    gain_one_half = jnp.sum(proj_grad * proj_shard.astype(F32), axis=1) / gain_one[:, 0]
    query_grad = proj_grad[:, :head_cols]
    pair_grad = proj_grad[:, head_cols:]
    pair_other = swap(pair_grad)
    gain_grads = jnp.stack([gain_one_half, gain_two_half])
    gain_grads = gain_grads + swap(gain_grads)
    return (
        layer_out,
        grad_input,
        gain_grads[0],
        gain_grads[1],
        query_grad,
        jnp.where(first, pair_grad, pair_other),
        jnp.where(first, pair_other, pair_grad),
        out_grad,
        gate_grad,
        up_grad,
        down_grad,
    )


def solution(mesh):
    rows = P(("seq", "fsdp"), None)
    specs = (
        P("fsdp"),
        P("fsdp"),
        P("fsdp", "tensor"),
        P("fsdp", None),
        P("fsdp", None),
        P("tensor", "fsdp"),
        P("fsdp", "tensor"),
        P("fsdp", "tensor"),
        P("tensor", "fsdp"),
    )
    return jax.shard_map(
        local, mesh=mesh, in_specs=(rows, rows) + specs, out_specs=(rows, rows) + specs,
        check_vma=False,
    )
```

```python
import jax
import jax.numpy as jnp
from jax import lax
from jax.experimental import pallas as pl
from jax.experimental.pallas import tpu as pltpu
from jax.sharding import PartitionSpec as P

WINDOW = 2048
EPSILON = 1e-06
F32 = jnp.float32
BF16 = jnp.bfloat16


def exchange(value, step):
    count = lax.axis_size("seq")
    return lax.ppermute(value, "seq", [(at, at ^ step) for at in range(count)])


def swap(value):
    return lax.ppermute(value, "tensor", [(0, 1), (1, 0)])


def seq_shift(value, steps):
    count = lax.axis_size("seq")
    leading, last = (max(0, -steps), min(count, count - steps))
    return lax.ppermute(value, "seq", [(at, at + steps) for at in range(leading, last)])


def plane_gather(value):
    count = lax.axis_size("seq")
    if count != 4:
        return [value] + [exchange(value, step) for step in range(1, count)]
    half = value.shape[0] // 2
    near_one, near_two = exchange(value, 1), exchange(value, 2)
    far = jnp.concatenate([exchange(near_two[:half], 1), exchange(near_one[half:], 2)], axis=0)
    return [value, near_one, near_two, far]


def plane_scatter(own, others, gate=None):
    total = own.astype(F32)
    parts = [exchange(part.astype(BF16), step) for step, part in enumerate(others, 1)]
    if gate is not None:
        parts = lax.optimization_barrier((*parts, gate))[:-1]
    for part in parts:
        total = total + part.astype(F32)
    return total


def times_transpose(left, right):
    return lax.dot_general(left, right, (((1,), (1,)), ((), ())), preferred_element_type=F32)


def rows_product(left, right):
    return lax.dot_general(left, right, (((0,), (0,)), ((), ())), preferred_element_type=F32)


def rotate(values, cosine, sine):
    half = cosine.shape[-1]
    first_part = values[..., :half]
    second_part = values[..., half : 2 * half]
    return jnp.concatenate(
        [
            first_part * cosine - second_part * sine,
            second_part * cosine + first_part * sine,
            values[..., 2 * half :],
        ],
        axis=-1,
    )


def inverse_rms(values):
    return lax.rsqrt(jnp.mean(values * values, axis=-1, keepdims=True) + EPSILON)


def norm_pull(values, inverse, grad):
    unit = values * inverse
    return inverse * (grad - unit * jnp.mean(grad * unit, axis=-1, keepdims=True))


def gated_unit(gate_pre, up_proj):
    return jax.nn.gelu(gate_pre) * up_proj


def pick(stacked, at):
    return lax.dynamic_index_in_dim(stacked, at, 0, keepdims=False)


def after(value, *others):
    return lax.optimization_barrier((value, *others))[0]


def part_of(value, at, size, axis):
    return lax.dynamic_slice_in_dim(value, at * size, size, axis)


MESH = pl.DeviceIdType.MESH


def greet(partners):
    barrier = pltpu.get_barrier_semaphore()
    for partner in partners:
        pl.semaphore_signal(barrier, inc=1, device_id=partner, device_id_type=MESH)
    pl.semaphore_wait(barrier, len(partners))


def plane_partners():
    seq_at, core = lax.axis_index("seq"), lax.axis_index("tensor")
    return {"seq": seq_at ^ 1}, {"seq": seq_at ^ 2}, {"tensor": 1 - core}


def send(source, target, sems, at, partner):
    copy = pltpu.make_async_remote_copy(
        src_ref=source, dst_ref=target, send_sem=sems.at[0, at], recv_sem=sems.at[1, at],
        device_id=partner, device_id_type=MESH,
    )
    copy.start()
    return copy


def rows_kernel(own_ref, out_ref, sems, local_sem):
    half = own_ref.shape[0]
    one, two, core = plane_partners()
    greet((one, two, core))

    def block(at, first=0, count=half):
        return out_ref.at[pl.ds(at * half + first, count), :]

    here = pltpu.make_async_copy(own_ref, block(0), local_sem)
    here.start()
    from_one = send(own_ref, block(1), sems, 0, one)
    from_two = send(own_ref, block(2), sems, 1, two)
    copies = [from_one, from_two, send(own_ref, block(4), sems, 2, core)]
    cut = half // 2
    from_one.wait_recv()
    far_low = send(block(1, cut, cut), block(3, cut, cut), sems, 3, two)
    copies.append(send(block(1), block(5), sems, 4, core))
    from_two.wait_recv()
    far_top = send(block(2, 0, cut), block(3, 0, cut), sems, 5, one)
    copies.append(send(block(2), block(6), sems, 6, core))
    far_low.wait_recv()
    far_top.wait_recv()
    copies.append(send(block(3), block(7), sems, 7, core))
    for copy in copies[2:]:
        copy.wait_recv()
    for copy in copies + [far_low, far_top]:
        copy.wait_send()
    here.wait()


def gather_rows(own, collective_id):
    half, width = own.shape
    return pl.pallas_call(
        rows_kernel,
        out_shape=jax.ShapeDtypeStruct((8 * half, width), own.dtype),
        in_specs=[pl.BlockSpec(memory_space=pl.ANY)],
        out_specs=pl.BlockSpec(memory_space=pl.ANY),
        scratch_shapes=[pltpu.SemaphoreType.DMA((2, 8)), pltpu.SemaphoreType.DMA],
        compiler_params=pltpu.CompilerParams(collective_id=collective_id, has_side_effects=True),
        cost_estimate=pl.CostEstimate(flops=1000, bytes_accessed=1000, transcendentals=0),
        name="gather_rows",
    )(own)


def sum_kernel(
    part_ref, out_ref, own_ref, land_ref, total_ref, near_ref, sems, local_sems
):
    half = out_ref.shape[0]
    cut = half // 2
    chunk = 32
    one, two, core = plane_partners()
    greet((one, two, core))
    order = (3, 1, 2, 0)
    loads, lands = {}, {}
    for at in order:
        loads[at] = pltpu.make_async_copy(
            part_ref.at[pl.ds(at * half, half), :], own_ref.at[at], local_sems.at[at]
        )
        loads[at].start()
        lands[at] = send(
            part_ref.at[pl.ds((4 + at) * half, half), :], land_ref.at[at], sems, at, core
        )
    sent = []
    for at in order:
        loads[at].wait()
        lands[at].wait_recv()

        @pl.loop(0, half // chunk)
        def _(step):
            rows = pl.ds(pl.multiple_of(step * chunk, chunk), chunk)
            value = own_ref[at, rows, :].astype(F32) + land_ref[at, rows, :].astype(F32)
            if at:
                total_ref[at - 1, rows, :] = value.astype(BF16)
            else:
                out_ref[rows, :] = value

        top, low = (total_ref.at[at - 1, pl.ds(first, cut), :] for first in (0, cut))
        if at == 3:
            far_top = send(top, near_ref.at[1], sems, 4, one)
            far_low = send(low, near_ref.at[3], sems, 5, two)
        if at == 1:
            near_top = send(top, near_ref.at[0], sems, 6, one)
        if at == 2:
            near_low = send(low, near_ref.at[2], sems, 7, two)

    def add_in(at, first, from_at):
        @pl.loop(0, cut // chunk)
        def _(step):
            rows = pl.ds(pl.multiple_of(step * chunk, chunk), chunk)
            there = pl.ds(pl.multiple_of(first + step * chunk, chunk), chunk)
            value = total_ref[at, there, :].astype(F32) + near_ref[from_at, rows, :].astype(F32)
            total_ref[at, there, :] = value.astype(BF16)

    far_top.wait_recv()
    add_in(1, 0, 1)
    last_top = send(total_ref.at[1, pl.ds(0, cut), :], near_ref.at[4], sems, 8, two)
    far_low.wait_recv()
    add_in(0, cut, 3)
    last_low = send(total_ref.at[0, pl.ds(cut, cut), :], near_ref.at[5], sems, 9, one)

    for first, near, last, near_at, last_at in (
        (0, near_top, last_top, 0, 4), (cut, near_low, last_low, 2, 5),
    ):
        near.wait_recv()
        last.wait_recv()

        @pl.loop(0, cut // chunk)
        def _(step):
            rows = pl.ds(pl.multiple_of(step * chunk, chunk), chunk)
            there = pl.ds(pl.multiple_of(first + step * chunk, chunk), chunk)
            out_ref[there, :] += near_ref[near_at, rows, :].astype(F32) + near_ref[
                last_at, rows, :
            ].astype(F32)

    for copy in (*lands.values(), far_top, far_low, near_top, near_low, last_top, last_low):
        copy.wait_send()


def scatter_rows(part, collective_id):
    count, width = part.shape
    half = count // 8
    return pl.pallas_call(
        sum_kernel,
        out_shape=jax.ShapeDtypeStruct((half, width), F32),
        in_specs=[pl.BlockSpec(memory_space=pl.ANY)],
        out_specs=pl.BlockSpec(memory_space=pltpu.VMEM),
        scratch_shapes=[
            pltpu.VMEM((4, half, width), BF16),
            pltpu.VMEM((4, half, width), BF16),
            pltpu.VMEM((3, half, width), BF16),
            pltpu.VMEM((6, half // 2, width), BF16),
            pltpu.SemaphoreType.DMA((2, 10)),
            pltpu.SemaphoreType.DMA((4,)),
        ],
        compiler_params=pltpu.CompilerParams(
            collective_id=collective_id, has_side_effects=True, vmem_limit_bytes=40 * 2**20
        ),
        cost_estimate=pl.CostEstimate(flops=1000, bytes_accessed=1000, transcendentals=0),
        name="scatter_rows",
    )(part)


TILE = 256
NT = (((1,), (1,)), ((), ()))
LOWEST = -1e30


def masked_tile(scores, at, tiles, shift):
    scores = scores + shift
    if at in (0, tiles - 1):
        key_at = lax.broadcasted_iota(jnp.int32, scores.shape, 0)
        query_at = lax.broadcasted_iota(jnp.int32, scores.shape, 1)
        allowed = key_at > query_at if at == 0 else key_at <= query_at
        scores = jnp.where(allowed, scores, LOWEST)
    return scores

def tile_shifts(pos_ref, start, tiles):
    return [
        jnp.where(pos_ref[0] - WINDOW + start + at * TILE >= 0, 0.0, LOWEST).astype(F32)
        for at in range(tiles)
    ]

def attend_kernel(pos_ref, q_ref, k_ref, v_ref, out_ref, log_ref, turned_ref, score_ref):
    tiles = WINDOW // TILE + 1

    @pl.when(pl.program_id(0) == 0)
    def _():
        turned_ref[...] = v_ref[...].T

    for start in range(0, q_ref.shape[0], TILE):
        shifts = tile_shifts(pos_ref, start, tiles)
        queries = q_ref[start : start + TILE, :]
        top = jnp.full((1, TILE), LOWEST, F32)
        for at in range(tiles):
            keys = k_ref[start + at * TILE : start + (at + 1) * TILE, :]
            scores = lax.dot_general(keys, queries, NT, preferred_element_type=F32)
            scores = masked_tile(scores, at, tiles, shifts[at])
            score_ref[at] = scores
            top = jnp.maximum(top, jnp.max(scores, axis=0, keepdims=True))
        total = jnp.zeros((1, TILE), F32)
        for at in range(tiles):
            expon = jnp.exp(score_ref[at] - top)
            score_ref[at] = expon
            total = total + jnp.sum(expon, axis=0, keepdims=True)
        inverse = 1.0 / total
        attended = jnp.zeros((v_ref.shape[1], TILE), F32)
        for at in range(tiles):
            probability = (score_ref[at] * inverse).astype(BF16)
            values = turned_ref[:, start + at * TILE : start + (at + 1) * TILE]
            attended = attended + jnp.dot(values, probability, preferred_element_type=F32)
        out_ref[start : start + TILE, :] = attended.T.astype(BF16)
        log_ref[0, :, start : start + TILE] = top + jnp.log(total)

def attend(first_pos, queries, key_rows, value_rows):
    rows, cols = queries.shape
    span, size = key_rows.shape
    heads = cols // size
    return pl.pallas_call(
        attend_kernel,
        out_shape=(
            jax.ShapeDtypeStruct((rows, cols), BF16),
            jax.ShapeDtypeStruct((heads, 1, rows), F32),
        ),
        grid=(heads,),
        in_specs=[
            pl.BlockSpec(memory_space=pltpu.SMEM),
            pl.BlockSpec((rows, size), lambda head: (0, head)),
            pl.BlockSpec((span, size), lambda head: (0, 0)),
            pl.BlockSpec((span, size), lambda head: (0, 0)),
        ],
        out_specs=(
            pl.BlockSpec((rows, size), lambda head: (0, head)),
            pl.BlockSpec((1, 1, rows), lambda head: (head, 0, 0)),
        ),
        scratch_shapes=[
            pltpu.VMEM((size, span), BF16),
            pltpu.VMEM((WINDOW // TILE + 1, TILE, TILE), F32),
        ],
        compiler_params=pltpu.CompilerParams(vmem_limit_bytes=40 * 2**20),
        cost_estimate=pl.CostEstimate(flops=1000, bytes_accessed=1000, transcendentals=0),
        name="attend",
    )(first_pos.reshape(1), queries, key_rows, value_rows)

def attend_back_kernel(
    pos_ref, q_ref, g_ref, k_ref, v_ref, log_ref, cos_ref, sin_ref,
    q_grad_ref, k_grad_ref, v_grad_ref, turned_ref, p_ref, gp_ref,
):
    tiles = WINDOW // TILE + 1
    size = k_ref.shape[1]

    @pl.when(pl.program_id(0) == 0)
    def _():
        turned_ref[...] = k_ref[...].T
        k_grad_ref[...] = jnp.zeros_like(k_grad_ref)
        v_grad_ref[...] = jnp.zeros_like(v_grad_ref)

    for start in range(0, q_ref.shape[0], TILE):
        shifts = tile_shifts(pos_ref, start, tiles)
        block = slice(start, start + TILE)
        queries, grads = q_ref[block, :], g_ref[block, :]
        log_total = log_ref[0, :, block]
        inner = jnp.zeros((1, TILE), F32)
        for at in range(tiles):
            span = slice(start + at * TILE, start + (at + 1) * TILE)
            scores = lax.dot_general(k_ref[span, :], queries, NT, preferred_element_type=F32)
            scores = masked_tile(scores, at, tiles, shifts[at])
            probability = jnp.exp(scores - log_total)
            grad = lax.dot_general(v_ref[span, :], grads, NT, preferred_element_type=F32)
            inner = inner + jnp.sum(probability * grad, axis=0, keepdims=True)
            p_ref[at] = probability
            gp_ref[at] = grad
        query_grad = jnp.zeros((size, TILE), F32)
        for at in range(tiles):
            span = slice(start + at * TILE, start + (at + 1) * TILE)
            probability = p_ref[at]
            score_grad = (probability * (gp_ref[at] - inner)).astype(BF16)
            k_grad_ref[span, :] += jnp.dot(score_grad, queries, preferred_element_type=F32)
            v_grad_ref[span, :] += jnp.dot(
                probability.astype(BF16), grads, preferred_element_type=F32
            )
            query_grad = query_grad + jnp.dot(
                turned_ref[:, span], score_grad, preferred_element_type=F32
            )
        query_grad = query_grad.T * size ** (-0.5)
        turn = cos_ref.shape[1]
        rotated = query_grad[:, :turn]
        rotated = (
            rotated * cos_ref[block, :] + pltpu.roll(rotated, turn // 2, 1) * sin_ref[block, :]
        )
        q_grad_ref[block, :turn] = rotated.astype(BF16)
        q_grad_ref[block, turn:] = query_grad[:, turn:].astype(BF16)

def attend_back(first_pos, queries, grads, key_rows, value_rows, log_total, cosine, sine):
    rows, cols = queries.shape
    span, size = key_rows.shape
    heads = cols // size
    by_head = pl.BlockSpec((rows, size), lambda head: (0, head))
    whole = pl.BlockSpec((span, size), lambda head: (0, 0))
    tile_shape = (WINDOW // TILE + 1, TILE, TILE)
    return pl.pallas_call(
        attend_back_kernel,
        out_shape=(
            jax.ShapeDtypeStruct((rows, cols), BF16),
            jax.ShapeDtypeStruct((span, size), F32),
            jax.ShapeDtypeStruct((span, size), F32),
        ),
        grid=(heads,),
        in_specs=[
            pl.BlockSpec(memory_space=pltpu.SMEM), by_head, by_head, whole, whole,
            pl.BlockSpec((1, 1, rows), lambda head: (head, 0, 0)),
            pl.BlockSpec(cosine.shape, lambda head: (0, 0)),
            pl.BlockSpec(sine.shape, lambda head: (0, 0)),
        ],
        out_specs=(by_head, whole, whole),
        scratch_shapes=[
            pltpu.VMEM((size, span), BF16),
            pltpu.VMEM(tile_shape, F32),
            pltpu.VMEM(tile_shape, F32),
        ],
        compiler_params=pltpu.CompilerParams(vmem_limit_bytes=48 * 2**20),
        cost_estimate=pl.CostEstimate(flops=1000, bytes_accessed=1000, transcendentals=0),
        name="attend_back",
    )(first_pos.reshape(1), queries, grads, key_rows, value_rows, log_total, cosine, sine)

def gelu_parts(gate):
    root = 0.7978845608028654
    square = gate * gate
    tanh = jnp.tanh(root * gate * (1.0 + 0.044715 * square))
    half = 0.5 * (1.0 + tanh)
    slope = half + 0.5 * gate * (1.0 - tanh * tanh) * root * (1.0 + 3 * 0.044715 * square)
    return gate * half, slope

def ffn_kernel(x_ref, w_ref, act_ref, a_ref, b_ref, total_ref):
    steps = 5
    depth = w_ref.shape[0] // steps
    total_ref[...] = jnp.dot(x_ref[:, :depth], w_ref[:depth, :], preferred_element_type=F32)
    for step in range(1, steps):
        part = slice(step * depth, (step + 1) * depth)
        total_ref[...] += jnp.dot(x_ref[:, part], w_ref[part, :], preferred_element_type=F32)
    hidden = act_ref.shape[1]
    main = hidden // 128 * 128
    for start in range(0, main, 128):
        cols = slice(start, start + 128)
        gate, up = total_ref[:, cols], total_ref[:, main + start : main + start + 128]
        gelu, slope = gelu_parts(gate)
        act_ref[:, cols] = (gelu * up).astype(BF16)
        a_ref[:, cols] = (slope * up).astype(BF16)
        b_ref[:, cols] = gelu.astype(BF16)
    last = total_ref[:, 2 * main :]
    up = pltpu.roll(last, 64, 1)
    gelu, slope = gelu_parts(last)
    act_ref[:, main:] = (gelu * up)[:, :64].astype(BF16)
    a_ref[:, main:] = (slope * up)[:, :64].astype(BF16)
    b_ref[:, main:] = gelu[:, :64].astype(BF16)

def ffn(x, w, rows=512):
    count, width = x.shape
    hidden = w.shape[1] // 2
    tile = pl.BlockSpec((rows, hidden), lambda i: (i, 0))
    return pl.pallas_call(
        ffn_kernel,
        out_shape=(jax.ShapeDtypeStruct((count, hidden), BF16),) * 3,
        grid=(count // rows,),
        in_specs=[
            pl.BlockSpec((rows, width), lambda i: (i, 0)),
            pl.BlockSpec(w.shape, lambda i: (0, 0), pipeline_mode=pl.Buffered(1)),
        ],
        out_specs=(tile,) * 3,
        scratch_shapes=[pltpu.VMEM((rows, 2 * hidden), F32)],
        compiler_params=pltpu.CompilerParams(vmem_limit_bytes=56 * 2**20),
        cost_estimate=pl.CostEstimate(flops=1000, bytes_accessed=1000, transcendentals=0),
        name="ffn",
    )(x, w)

def ffn_back_kernel(c_ref, d_ref, a_ref, b_ref, w_ref, g_ref, out_ref):
    hidden = a_ref.shape[1]
    main = hidden // 128 * 128
    act_grad = lax.dot_general(c_ref[...], d_ref[...], NT, preferred_element_type=F32)
    g_ref[:, :main] = (act_grad[:, :main] * a_ref[:, :main].astype(F32)).astype(BF16)
    g_ref[:, main : 2 * main] = (act_grad[:, :main] * b_ref[:, :main].astype(F32)).astype(BF16)
    last = act_grad[:, main:]
    g_ref[:, 2 * main :] = jnp.concatenate(
        [last * a_ref[:, main:].astype(F32), last * b_ref[:, main:].astype(F32)], axis=1
    ).astype(BF16)
    out_ref[...] = lax.dot_general(
        g_ref[...], w_ref[...], NT, preferred_element_type=F32
    ).astype(BF16)

def ffn_back(cot, down, a, b, w, rows=256):
    count, width = cot.shape
    hidden = a.shape[1]
    by_rows = lambda cols: pl.BlockSpec((rows, cols), lambda i: (i, 0))
    once = lambda v: pl.BlockSpec(v.shape, lambda i: (0, 0), pipeline_mode=pl.Buffered(1))
    return pl.pallas_call(
        ffn_back_kernel,
        out_shape=(
            jax.ShapeDtypeStruct((count, 2 * hidden), BF16),
            jax.ShapeDtypeStruct((count, width), BF16),
        ),
        grid=(count // rows,),
        in_specs=[by_rows(width), once(down), by_rows(hidden), by_rows(hidden), once(w)],
        out_specs=(by_rows(2 * hidden), by_rows(width)),
        compiler_params=pltpu.CompilerParams(vmem_limit_bytes=56 * 2**20),
        cost_estimate=pl.CostEstimate(flops=1000, bytes_accessed=1000, transcendentals=0),
        name="ffn_back",
    )(cot, down, a, b, w)


def local(
    inputs, cotangent, gain_attn, gain_ffn, w_query, w_key, w_value, w_out, w_gate, w_up, w_down
):
    rows, width = inputs.shape
    half = rows // 2
    head_size = w_key.shape[1]
    head_cols = w_query.shape[1]
    heads_here = head_cols // head_size
    seqs, shards = lax.axis_size("seq"), lax.axis_size("fsdp")
    assert rows * shards == WINDOW and lax.axis_size("tensor") == 2
    seq_at, shard_at, core = (lax.axis_index(name) for name in ("seq", "fsdp", "tensor"))
    first = core == 0
    key_span = rows + WINDOW
    first_pos = (seq_at * shards + shard_at) * rows
    scale = head_size ** (-0.5)
    rot_half = head_size // 4
    frequency = 10000.0 ** (-(jnp.arange(rot_half, dtype=F32) * 2.0) / (2 * rot_half))
    angles = (first_pos + jnp.arange(rows, dtype=jnp.int32)).astype(F32)[:, None] * frequency[None]
    cosine, sine = jnp.cos(angles), jnp.sin(angles)

    def my_half(value):
        return part_of(value, core, half, 0)

    def other_half(value):
        return part_of(value, 1 - core, half, 0)

    def whole_rows(own):
        other = swap(own)
        return jnp.where(first, jnp.stack([own, other]), jnp.stack([other, own])).reshape(
            rows, own.shape[1]
        )

    def plane_rows(own, other=None):
        near = plane_gather(own)
        far = [swap(piece) if at or other is None else other for at, piece in enumerate(near)]
        return jnp.concatenate(near + far, axis=0)

    def plane_sum(partial, gate=None):
        count = seqs * half
        cores = partial[:count].astype(F32) + swap(partial[count:].astype(BF16)).astype(F32)
        others = [cores[j * half : (j + 1) * half] for j in range(1, seqs)]
        return plane_scatter(cores[:half], others, gate)

    def order_cols(pieces):
        stacked = jnp.stack(pieces)
        return [pick(stacked, seq_at ^ at) for at in range(seqs)]

    gain_one, gain_two = gain_attn.astype(F32)[:, None], gain_ffn.astype(F32)[:, None]
    gains = jnp.stack([gain_attn, gain_ffn])
    gains = jnp.stack(
        [gains]
        + [
            lax.ppermute(gains, "fsdp", [((at + by) % shards, at) for at in range(shards)])
            for by in range(1, shards)
        ]
    )
    gains = jnp.concatenate(
        [pick(gains, (at - shard_at) % shards) for at in range(shards)], axis=1
    ).astype(F32)
    pair_shard = jnp.where(first, w_key, w_value)
    proj_shard = jnp.concatenate([w_query, pair_shard], axis=1)
    proj_cols = proj_shard.shape[1] // seqs
    proj_weight = lax.all_gather(
        part_of(proj_shard, seq_at, proj_cols, 1), "fsdp", axis=0, tiled=True
    )
    out_rows = head_cols // seqs
    hidden = w_gate.shape[1] // seqs
    kernels = hidden % 128 == 64
    main = hidden // 128 * 128 if kernels else hidden
    gate_mine, up_mine = (part_of(value, seq_at, hidden, 1) for value in (w_gate, w_up))
    pair_in = jnp.concatenate(
        [gate_mine[:, :main], up_mine[:, :main], gate_mine[:, main:], up_mine[:, main:]], axis=1
    )
    in_weight = lax.all_gather(pair_in, "fsdp", axis=0, tiled=True)
    down_weight = lax.all_gather(
        part_of(w_down, seq_at, hidden, 0), "fsdp", axis=1, tiled=True
    )

    source = inputs.astype(F32)
    inverse_one = inverse_rms(source)
    unit_one = (source * inverse_one * gains[0]).astype(BF16)
    square = seqs == 4
    unit_one_half = my_half(unit_one)
    rows_one = (
        gather_rows(unit_one_half, 1) if square
        else plane_rows(unit_one_half, other_half(unit_one))
    )
    out_quarter = lax.all_gather(
        part_of(after(w_out, rows_one), seq_at, out_rows, 0), "fsdp", axis=1, tiled=True
    )
    proj = jnp.dot(rows_one, proj_weight, preferred_element_type=F32)
    rotate_first = proj_cols % (2 * rot_half) == 0
    if rotate_first:
        halves_at = jnp.where(first, jnp.arange(2), 1 - jnp.arange(2))[:, None, None]
        seqs_at = (seq_at ^ jnp.arange(seqs))[None, :, None]
        row_pos = (
            (seqs_at * shards + shard_at) * rows + halves_at * half + jnp.arange(half)[None, None]
        ).reshape(-1)
        row_angles = row_pos.astype(F32)[:, None] * frequency[None]
        units = proj_cols // (2 * rot_half)
        unit_at = seq_at * units + jnp.arange(units)
        head_units = head_cols // (2 * rot_half)
        turned = (unit_at % 2 == 0) & (first | (unit_at < head_units))
        unit_scale = jnp.where(unit_at < head_units, scale, 1.0)[None, :, None]
        turned = turned[None, :, None]
        row_cos = jnp.where(turned, jnp.cos(row_angles)[:, None], 1.0) * unit_scale
        row_sin = jnp.where(turned, jnp.sin(row_angles)[:, None], 0.0) * unit_scale
        proj = rotate(proj.reshape(-1, units, 2 * rot_half), row_cos, row_sin)
    proj = proj.astype(BF16).reshape(2, seqs, half, proj_cols)
    proj = jnp.where(first, proj, proj[::-1])
    proj_parts = [proj[:, 0].reshape(rows, proj_cols)] + [
        exchange(proj[:, at].reshape(rows, proj_cols), at) for at in range(1, seqs)
    ]
    proj_here = jnp.concatenate(order_cols(proj_parts), axis=1)
    queries = proj_here[:, :head_cols]
    pair_here = proj_here[:, head_cols:]
    if not rotate_first:
        queries = queries.reshape(rows, heads_here, head_size).astype(F32)
        queries = (rotate(queries, cosine[:, None], sine[:, None]) * scale).astype(BF16)
        queries = queries.reshape(rows, head_cols)
        pair_here = jnp.where(first, rotate(pair_here.astype(F32), cosine, sine), pair_here)
        pair_here = pair_here.astype(BF16)

    pair_here, out_quarter = lax.optimization_barrier((pair_here, out_quarter))
    earlier = seq_shift(pair_here, 1)
    slots = [
        lax.ppermute(
            jnp.where(shard_at >= at, earlier, pair_here),
            "fsdp", [(source_at, (source_at - at) % shards) for source_at in range(shards)],
        )
        for at in range(1, shards)
    ]
    window_here = jnp.concatenate([earlier] + slots + [pair_here], axis=0)
    window_other = swap(window_here)
    key_rows = jnp.where(first, window_here, window_other)
    value_rows = jnp.where(first, window_other, window_here)

    out_weight = jnp.zeros((head_cols, width), BF16)
    for at, piece in enumerate(plane_gather(out_quarter)):
        out_weight = lax.dynamic_update_slice_in_dim(
            out_weight, piece, (seq_at ^ at) * out_rows, 0
        )

    head_outputs, log_total = attend(first_pos, queries, key_rows, value_rows)

    out_part = jnp.dot(head_outputs, out_weight, preferred_element_type=F32)
    hidden_in = my_half(source) + my_half(out_part) + swap(other_half(out_part))
    inverse_two = inverse_rms(hidden_in)
    unit_two = (hidden_in * inverse_two * gains[1]).astype(BF16)
    rows_two = gather_rows(unit_two, 2) if square else plane_rows(unit_two)
    cot_later = after(cotangent, out_weight)
    rows_cot = plane_rows(my_half(cot_later), other_half(cot_later))

    if kernels:
        activation, gate_factor, up_factor = ffn(rows_two, in_weight)
        down_term = rows_product(rows_cot, activation).astype(BF16)
        gate_factor = after(gate_factor, down_term)
        grad_in, back_part = ffn_back(rows_cot, down_weight, gate_factor, up_factor, in_weight)
    else:
        in_proj = jnp.dot(rows_two, in_weight, preferred_element_type=F32)
        gate_pre, up_proj = in_proj[:, :hidden], in_proj[:, hidden:]
        activation = gated_unit(gate_pre, up_proj).astype(BF16)
        down_term = rows_product(rows_cot, activation).astype(BF16)
        grad_activation = times_transpose(rows_cot, down_weight)
        grad_gate, grad_up = jax.vjp(gated_unit, gate_pre, up_proj)[1](grad_activation)
        grad_in = jnp.concatenate([grad_gate.astype(BF16), grad_up.astype(BF16)], axis=1)
        back_part = times_transpose(grad_in, in_weight)
    in_term = rows_product(rows_two, grad_in).astype(BF16)
    back_part = after(back_part, in_term)
    grad_unit_two = scatter_rows(back_part, 3) if square else plane_sum(back_part)
    grad_hidden = my_half(cotangent).astype(F32) + norm_pull(
        hidden_in, inverse_two, grad_unit_two * gains[1]
    )
    out_rows_part = jnp.dot(
        after(activation, grad_unit_two), down_weight, preferred_element_type=F32
    )
    down_shard = lax.psum_scatter(down_term, "fsdp", scatter_dimension=0, tiled=True).T
    in_shard = lax.psum_scatter(in_term, "fsdp", scatter_dimension=0, tiled=True)

    grad_attn_out = whole_rows(grad_hidden.astype(BF16))
    grad_heads = times_transpose(grad_attn_out, out_weight).astype(BF16)
    grad_heads, out_rows_part, down_shard = lax.optimization_barrier(
        (grad_heads, out_rows_part, down_shard)
    )
    grad_query_proj, grad_keys, grad_values = attend_back(
        first_pos, queries, grad_heads, key_rows, value_rows, log_total,
        jnp.concatenate([cosine, cosine], axis=1), jnp.concatenate([sine, -sine], axis=1),
    )
    pair_grads = jnp.where(first, grad_keys, grad_values) + swap(
        jnp.where(first, grad_values, grad_keys)
    )
    returned = [
        lax.ppermute(
            pair_grads[at * rows : (at + 1) * rows].astype(BF16),
            "fsdp", [((source_at - at) % shards, source_at) for source_at in range(shards)],
        ).astype(F32)
        for at in range(1, shards)
    ]
    own_total = pair_grads[shards * rows :]
    earlier_total = pair_grads[:rows]
    for at, piece in enumerate(returned, 1):
        own_total = own_total + jnp.where(shard_at >= at, 0.0, piece)
        earlier_total = earlier_total + jnp.where(shard_at >= at, piece, 0.0)
    own_total = own_total + seq_shift(earlier_total.astype(BF16), -1).astype(F32)
    grad_pair = jnp.where(first, rotate(own_total, cosine, -sine), own_total).astype(BF16)
    grad_pair, in_shard = lax.optimization_barrier((grad_pair, in_shard))
    grad_proj = jnp.concatenate([grad_query_proj, grad_pair], axis=1)
    grad_parts = [part_of(grad_proj, seq_at, proj_cols, 1)] + [
        exchange(part_of(grad_proj, seq_at ^ at, proj_cols, 1), at) for at in range(1, seqs)
    ]
    grad_rows = jnp.stack(grad_parts).reshape(seqs, 2, half, proj_cols).swapaxes(0, 1)
    grad_rows = jnp.where(first, grad_rows, grad_rows[::-1]).reshape(2 * seqs * half, proj_cols)

    ffn_out = plane_sum(after(out_rows_part, pair_grads), grad_pair)
    layer_out = whole_rows((hidden_in + ffn_out).astype(BF16))
    down_parts = lax.optimization_barrier((*plane_gather(down_shard), pair_grads))[:-1]
    down_grad = jnp.concatenate(order_cols(down_parts), axis=0).astype(F32)
    in_parts = order_cols(plane_gather(in_shard))
    rest = hidden - main
    gate_grad, up_grad = (
        jnp.concatenate(
            [
                piece[:, first_at : first_at + count]
                for piece in in_parts
                for first_at, count in spans
                if count
            ],
            axis=1,
        ).astype(F32)
        for spans in (((0, main), (2 * main, rest)), ((main, main), (2 * main + rest, rest)))
    )
    gain_two_half = jnp.sum(
        gate_grad * w_gate.astype(F32) + up_grad * w_up.astype(F32), axis=1
    ) / gain_two[:, 0]
    out_term = rows_product(after(head_outputs, grad_rows), grad_attn_out).astype(BF16)
    out_sum = plane_scatter(
        part_of(out_term, seq_at, out_rows, 0),
        [part_of(out_term, seq_at ^ at, out_rows, 0) for at in range(1, seqs)],
    ).astype(BF16)
    out_shard = lax.psum_scatter(out_sum, "fsdp", scatter_dimension=1, tiled=True)
    out_grad = jnp.concatenate(order_cols(plane_gather(out_shard)), axis=0).astype(F32)

    proj_term = rows_product(rows_one, grad_rows).astype(BF16)
    grad_unit_one = times_transpose(grad_rows, proj_weight)
    if square:
        grad_unit_one = scatter_rows(after(grad_unit_one.astype(BF16), proj_term), 4)
    else:
        grad_unit_one = plane_sum(grad_unit_one)
    grad_input = whole_rows(
        grad_hidden + norm_pull(my_half(source), my_half(inverse_one), grad_unit_one * gains[0])
    )
    proj_sum = lax.psum_scatter(proj_term, "fsdp", scatter_dimension=0, tiled=True)
    proj_grad = jnp.concatenate(order_cols(plane_gather(proj_sum)), axis=1).astype(F32)
    gain_one_half = jnp.sum(proj_grad * proj_shard.astype(F32), axis=1) / gain_one[:, 0]
    query_grad = proj_grad[:, :head_cols]
    pair_grad = proj_grad[:, head_cols:]
    pair_other = swap(pair_grad)
    gain_grads = jnp.stack([gain_one_half, gain_two_half])
    gain_grads = gain_grads + swap(gain_grads)
    return (
        layer_out,
        grad_input,
        gain_grads[0],
        gain_grads[1],
        query_grad,
        jnp.where(first, pair_grad, pair_other),
        jnp.where(first, pair_other, pair_grad),
        out_grad,
        gate_grad,
        up_grad,
        down_grad,
    )


def solution(mesh):
    rows = P(("seq", "fsdp"), None)
    specs = (
        P("fsdp"),
        P("fsdp"),
        P("fsdp", "tensor"),
        P("fsdp", None),
        P("fsdp", None),
        P("tensor", "fsdp"),
        P("fsdp", "tensor"),
        P("fsdp", "tensor"),
        P("tensor", "fsdp"),
    )
    return jax.shard_map(
        local, mesh=mesh, in_specs=(rows, rows) + specs, out_specs=(rows, rows) + specs,
        check_vma=False,
    )
```

```python
import functools

import jax
import jax.numpy as jnp
from jax import lax
from jax.experimental import pallas as pl
from jax.experimental.pallas import tpu as pltpu
from jax.sharding import PartitionSpec as P

WINDOW = 2048
EPSILON = 1e-06
F32 = jnp.float32
BF16 = jnp.bfloat16


def exchange(value, step):
    count = lax.axis_size("seq")
    return lax.ppermute(value, "seq", [(at, at ^ step) for at in range(count)])


def swap(value):
    return lax.ppermute(value, "tensor", [(0, 1), (1, 0)])


def seq_shift(value, steps):
    count = lax.axis_size("seq")
    leading, last = (max(0, -steps), min(count, count - steps))
    return lax.ppermute(value, "seq", [(at, at + steps) for at in range(leading, last)])


def gather_near(value):
    count = lax.axis_size("seq")
    steps = (1, 2) if count == 4 else range(1, count)
    return [exchange(value, step) for step in steps]


def gather_far(value, near):
    if lax.axis_size("seq") != 4:
        return [value, *near]
    half = value.shape[0] // 2
    far = jnp.concatenate([exchange(near[1][:half], 1), exchange(near[0][half:], 2)], axis=0)
    return [value, *near, far]


def plane_gather(value):
    return gather_far(value, gather_near(value))


def scatter_near(parts):
    if len(parts) != 4:
        return [exchange(part.astype(BF16), step) for step, part in enumerate(parts[1:], 1)]
    cut = parts[0].shape[0] // 2
    by_one = jnp.concatenate([parts[1][:cut], parts[3][:cut]]).astype(BF16)
    by_two = jnp.concatenate([parts[2][cut:], parts[3][cut:]]).astype(BF16)
    return [exchange(by_one, 1), exchange(by_two, 2)]


def scatter_far(parts, near):
    if len(parts) != 4:
        return sum((part.astype(F32) for part in near), parts[0].astype(F32)), []
    cut = parts[0].shape[0] // 2
    by_one, by_two = near
    last_top = (parts[2][:cut].astype(F32) + by_one[cut:].astype(F32)).astype(BF16)
    last_low = (parts[1][cut:].astype(F32) + by_two[cut:].astype(F32)).astype(BF16)
    total = parts[0].astype(F32) + jnp.concatenate([by_one[:cut], by_two[:cut]]).astype(F32)
    return total, [exchange(last_top, 2), exchange(last_low, 1)]


def scatter_end(total, far):
    return total + jnp.concatenate(far).astype(F32) if far else total


def times_transpose(left, right):
    return lax.dot_general(left, right, (((1,), (1,)), ((), ())), preferred_element_type=F32)


def rows_product(left, right):
    return lax.dot_general(left, right, (((0,), (0,)), ((), ())), preferred_element_type=F32)


def rotate(values, cosine, sine):
    half = cosine.shape[-1]
    first_part = values[..., :half]
    second_part = values[..., half : 2 * half]
    return jnp.concatenate(
        [
            first_part * cosine - second_part * sine,
            second_part * cosine + first_part * sine,
            values[..., 2 * half :],
        ],
        axis=-1,
    )


def inverse_rms(values):
    return lax.rsqrt(jnp.mean(values * values, axis=-1, keepdims=True) + EPSILON)


def norm_pull(values, inverse, grad):
    unit = values * inverse
    return inverse * (grad - unit * jnp.mean(grad * unit, axis=-1, keepdims=True))


def gated_unit(gate_pre, up_proj):
    return jax.nn.gelu(gate_pre) * up_proj


def pick(stacked, at):
    return lax.dynamic_index_in_dim(stacked, at, 0, keepdims=False)


def after(value, *others):
    return lax.optimization_barrier((value, *others))[0]


def part_of(value, at, size, axis):
    return lax.dynamic_slice_in_dim(value, at * size, size, axis)


MESH = pl.DeviceIdType.MESH


def greet(partners):
    barrier = pltpu.get_barrier_semaphore()
    for partner in partners:
        pl.semaphore_signal(barrier, inc=1, device_id=partner, device_id_type=MESH)
    pl.semaphore_wait(barrier, len(partners))


def plane_partners():
    seq_at, core = lax.axis_index("seq"), lax.axis_index("tensor")
    return {"seq": seq_at ^ 1}, {"seq": seq_at ^ 2}, {"tensor": 1 - core}


def send(source, target, sems, at, partner):
    copy = pltpu.make_async_remote_copy(
        src_ref=source, dst_ref=target, send_sem=sems.at[0, at], recv_sem=sems.at[1, at],
        device_id=partner, device_id_type=MESH,
    )
    copy.start()
    return copy


def rows_kernel(own_ref, out_ref, sems, local_sem):
    half = own_ref.shape[0]
    one, two, core = plane_partners()
    greet((one, two, core))

    def block(at, first=0, count=half):
        return out_ref.at[pl.ds(at * half + first, count), :]

    here = pltpu.make_async_copy(own_ref, block(0), local_sem)
    here.start()
    from_one = send(own_ref, block(1), sems, 0, one)
    from_two = send(own_ref, block(2), sems, 1, two)
    copies = [from_one, from_two, send(own_ref, block(4), sems, 2, core)]
    cut = half // 2
    from_one.wait_recv()
    far_low = send(block(1, cut, cut), block(3, cut, cut), sems, 3, two)
    copies.append(send(block(1), block(5), sems, 4, core))
    from_two.wait_recv()
    far_top = send(block(2, 0, cut), block(3, 0, cut), sems, 5, one)
    copies.append(send(block(2), block(6), sems, 6, core))
    far_low.wait_recv()
    far_top.wait_recv()
    copies.append(send(block(3), block(7), sems, 7, core))
    for copy in copies[2:]:
        copy.wait_recv()
    for copy in copies + [far_low, far_top]:
        copy.wait_send()
    here.wait()


def gather_rows(own, collective_id):
    half, width = own.shape
    return pl.pallas_call(
        rows_kernel,
        out_shape=jax.ShapeDtypeStruct((8 * half, width), own.dtype),
        in_specs=[pl.BlockSpec(memory_space=pl.ANY)],
        out_specs=pl.BlockSpec(memory_space=pl.ANY),
        scratch_shapes=[pltpu.SemaphoreType.DMA((2, 8)), pltpu.SemaphoreType.DMA],
        compiler_params=pltpu.CompilerParams(collective_id=collective_id, has_side_effects=True),
        cost_estimate=pl.CostEstimate(flops=1000, bytes_accessed=1000, transcendentals=0),
        name="gather_rows",
    )(own)


def unit_kernel(seq_ref, grad_ref, *refs):
    weights, out_ref = refs[:-1], refs[-1]
    cols = weights[0].shape[1]
    for at, weight_ref in enumerate(weights):
        part = pl.ds(pl.multiple_of((seq_ref[0] ^ at) * cols, 128), cols)
        term = lax.dot_general(
            grad_ref[:, part], weight_ref[...], NT, preferred_element_type=F32
        )
        if at:
            out_ref[...] += term
        else:
            out_ref[...] = term


def unit_grads(seq_at, grads, weights):
    vmem = pl.BlockSpec(memory_space=pltpu.VMEM)
    return pl.pallas_call(
        unit_kernel,
        out_shape=jax.ShapeDtypeStruct((grads.shape[0], weights[0].shape[0]), F32),
        in_specs=[pl.BlockSpec(memory_space=pltpu.SMEM), vmem] + [vmem] * len(weights),
        out_specs=vmem,
        compiler_params=pltpu.CompilerParams(vmem_limit_bytes=40 * 2**20),
        cost_estimate=pl.CostEstimate(flops=1000, bytes_accessed=1000, transcendentals=0),
        name="unit_grads",
    )(seq_at.reshape(1), grads, *weights)


def trade_kernel(to_rows, value_ref, out_ref, sems, local_sems):
    seq_at, core = lax.axis_index("seq"), lax.axis_index("tensor")
    plane_ref, chip_ref = (out_ref, value_ref) if to_rows else (value_ref, out_ref)
    cols, half = plane_ref.shape[1], plane_ref.shape[0] // 8
    greet([{"seq": seq_at ^ step} for step in range(1, 4)])
    copies = []
    for step in (3, 1, 2, 0):
        for at in range(2):
            plane = plane_ref.at[pl.ds((at * 4 + step) * half, half), :]
            rows = pl.ds(pl.multiple_of((core if at == 0 else 1 - core) * half, half), half)
            owner = seq_at ^ step if to_rows else seq_at
            chip = chip_ref.at[rows, pl.ds(pl.multiple_of(owner * cols, 128), cols)]
            source, target = (chip, plane) if to_rows else (plane, chip)
            if step:
                sem_at = 2 * (step - 1) + at
                copies.append(send(source, target, sems, sem_at, {"seq": seq_at ^ step}))
            else:
                here = pltpu.make_async_copy(source, target, local_sems.at[at])
                here.start()
                copies.append(here)
    for copy in copies:
        copy.wait()


def trade(value, to_rows, collective_id):
    rows, cols = value.shape
    return pl.pallas_call(
        functools.partial(trade_kernel, to_rows),
        out_shape=jax.ShapeDtypeStruct(
            (rows * 4, cols // 4) if to_rows else (rows // 4, cols * 4), value.dtype
        ),
        in_specs=[pl.BlockSpec(memory_space=pl.ANY)],
        out_specs=pl.BlockSpec(memory_space=pl.ANY),
        scratch_shapes=[pltpu.SemaphoreType.DMA((2, 6)), pltpu.SemaphoreType.DMA((2,))],
        compiler_params=pltpu.CompilerParams(collective_id=collective_id, has_side_effects=True),
        cost_estimate=pl.CostEstimate(flops=1000, bytes_accessed=1000, transcendentals=0),
        name="trade",
    )(value)


def sum_kernel(
    part_ref, out_ref, own_ref, land_ref, total_ref, near_ref, sems, local_sems
):
    half = out_ref.shape[0]
    cut = half // 2
    chunk = 32
    one, two, core = plane_partners()
    greet((one, two, core))
    order = (3, 1, 2, 0)
    loads, lands = {}, {}
    for at in order:
        loads[at] = pltpu.make_async_copy(
            part_ref.at[pl.ds(at * half, half), :], own_ref.at[at], local_sems.at[at]
        )
        loads[at].start()
        lands[at] = send(
            part_ref.at[pl.ds((4 + at) * half, half), :], land_ref.at[at], sems, at, core
        )
    sent = []
    for at in order:
        loads[at].wait()
        lands[at].wait_recv()

        @pl.loop(0, half // chunk)
        def _(step):
            rows = pl.ds(pl.multiple_of(step * chunk, chunk), chunk)
            value = own_ref[at, rows, :].astype(F32) + land_ref[at, rows, :].astype(F32)
            if at:
                total_ref[at - 1, rows, :] = value.astype(BF16)
            else:
                out_ref[rows, :] = value

        top, low = (total_ref.at[at - 1, pl.ds(first, cut), :] for first in (0, cut))
        if at == 3:
            far_top = send(top, near_ref.at[1], sems, 4, one)
            far_low = send(low, near_ref.at[3], sems, 5, two)
        if at == 1:
            near_top = send(top, near_ref.at[0], sems, 6, one)
        if at == 2:
            near_low = send(low, near_ref.at[2], sems, 7, two)

    def add_in(at, first, from_at):
        @pl.loop(0, cut // chunk)
        def _(step):
            rows = pl.ds(pl.multiple_of(step * chunk, chunk), chunk)
            there = pl.ds(pl.multiple_of(first + step * chunk, chunk), chunk)
            value = total_ref[at, there, :].astype(F32) + near_ref[from_at, rows, :].astype(F32)
            total_ref[at, there, :] = value.astype(BF16)

    far_top.wait_recv()
    add_in(1, 0, 1)
    last_top = send(total_ref.at[1, pl.ds(0, cut), :], near_ref.at[4], sems, 8, two)
    far_low.wait_recv()
    add_in(0, cut, 3)
    last_low = send(total_ref.at[0, pl.ds(cut, cut), :], near_ref.at[5], sems, 9, one)

    for first, near, last, near_at, last_at in (
        (0, near_top, last_top, 0, 4), (cut, near_low, last_low, 2, 5),
    ):
        near.wait_recv()
        last.wait_recv()

        @pl.loop(0, cut // chunk)
        def _(step):
            rows = pl.ds(pl.multiple_of(step * chunk, chunk), chunk)
            there = pl.ds(pl.multiple_of(first + step * chunk, chunk), chunk)
            out_ref[there, :] += near_ref[near_at, rows, :].astype(F32) + near_ref[
                last_at, rows, :
            ].astype(F32)

    for copy in (*lands.values(), far_top, far_low, near_top, near_low, last_top, last_low):
        copy.wait_send()


def scatter_rows(part, collective_id):
    count, width = part.shape
    half = count // 8
    return pl.pallas_call(
        sum_kernel,
        out_shape=jax.ShapeDtypeStruct((half, width), F32),
        in_specs=[pl.BlockSpec(memory_space=pl.ANY)],
        out_specs=pl.BlockSpec(memory_space=pltpu.VMEM),
        scratch_shapes=[
            pltpu.VMEM((4, half, width), BF16),
            pltpu.VMEM((4, half, width), BF16),
            pltpu.VMEM((3, half, width), BF16),
            pltpu.VMEM((6, half // 2, width), BF16),
            pltpu.SemaphoreType.DMA((2, 10)),
            pltpu.SemaphoreType.DMA((4,)),
        ],
        compiler_params=pltpu.CompilerParams(
            collective_id=collective_id, has_side_effects=True, vmem_limit_bytes=40 * 2**20
        ),
        cost_estimate=pl.CostEstimate(flops=1000, bytes_accessed=1000, transcendentals=0),
        name="scatter_rows",
    )(part)


TILE = 256
NT = (((1,), (1,)), ((), ()))
LOWEST = -1e30


def masked_tile(scores, at, tiles, shift):
    scores = scores + shift
    if at in (0, tiles - 1):
        key_at = lax.broadcasted_iota(jnp.int32, scores.shape, 0)
        query_at = lax.broadcasted_iota(jnp.int32, scores.shape, 1)
        allowed = key_at > query_at if at == 0 else key_at <= query_at
        scores = jnp.where(allowed, scores, LOWEST)
    return scores

def tile_shifts(pos_ref, start, tiles):
    return [
        jnp.where(pos_ref[0] - WINDOW + start + at * TILE >= 0, 0.0, LOWEST).astype(F32)
        for at in range(tiles)
    ]

def attend_kernel(pos_ref, q_ref, k_ref, v_ref, out_ref, log_ref, turned_ref, score_ref):
    tiles = WINDOW // TILE + 1

    @pl.when(pl.program_id(0) == 0)
    def _():
        turned_ref[...] = v_ref[...].T

    for start in range(0, q_ref.shape[0], TILE):
        shifts = tile_shifts(pos_ref, start, tiles)
        queries = q_ref[start : start + TILE, :]
        top = jnp.full((1, TILE), LOWEST, F32)
        for at in range(tiles):
            keys = k_ref[start + at * TILE : start + (at + 1) * TILE, :]
            scores = lax.dot_general(keys, queries, NT, preferred_element_type=F32)
            scores = masked_tile(scores, at, tiles, shifts[at])
            score_ref[at] = scores
            top = jnp.maximum(top, jnp.max(scores, axis=0, keepdims=True))
        total = jnp.zeros((1, TILE), F32)
        for at in range(tiles):
            expon = jnp.exp(score_ref[at] - top)
            score_ref[at] = expon
            total = total + jnp.sum(expon, axis=0, keepdims=True)
        inverse = 1.0 / total
        attended = jnp.zeros((v_ref.shape[1], TILE), F32)
        for at in range(tiles):
            probability = (score_ref[at] * inverse).astype(BF16)
            values = turned_ref[:, start + at * TILE : start + (at + 1) * TILE]
            attended = attended + jnp.dot(values, probability, preferred_element_type=F32)
        out_ref[start : start + TILE, :] = attended.T.astype(BF16)
        log_ref[0, :, start : start + TILE] = top + jnp.log(total)

def attend(first_pos, queries, key_rows, value_rows):
    rows, cols = queries.shape
    span, size = key_rows.shape
    heads = cols // size
    return pl.pallas_call(
        attend_kernel,
        out_shape=(
            jax.ShapeDtypeStruct((rows, cols), BF16),
            jax.ShapeDtypeStruct((heads, 1, rows), F32),
        ),
        grid=(heads,),
        in_specs=[
            pl.BlockSpec(memory_space=pltpu.SMEM),
            pl.BlockSpec((rows, size), lambda head: (0, head)),
            pl.BlockSpec((span, size), lambda head: (0, 0)),
            pl.BlockSpec((span, size), lambda head: (0, 0)),
        ],
        out_specs=(
            pl.BlockSpec((rows, size), lambda head: (0, head)),
            pl.BlockSpec((1, 1, rows), lambda head: (head, 0, 0)),
        ),
        scratch_shapes=[
            pltpu.VMEM((size, span), BF16),
            pltpu.VMEM((WINDOW // TILE + 1, TILE, TILE), F32),
        ],
        compiler_params=pltpu.CompilerParams(vmem_limit_bytes=40 * 2**20),
        cost_estimate=pl.CostEstimate(flops=1000, bytes_accessed=1000, transcendentals=0),
        name="attend",
    )(first_pos.reshape(1), queries, key_rows, value_rows)

def attend_back_kernel(
    pos_ref, q_ref, g_ref, k_ref, v_ref, log_ref, cos_ref, sin_ref,
    q_grad_ref, keep_ref, sent_ref, turned_ref, p_ref, gp_ref, k_grad_ref, v_grad_ref,
):
    tiles = WINDOW // TILE + 1
    size = k_ref.shape[1]

    @pl.when(pl.program_id(0) == 0)
    def _():
        turned_ref[...] = k_ref[...].T
        k_grad_ref[...] = jnp.zeros_like(k_grad_ref)
        v_grad_ref[...] = jnp.zeros_like(v_grad_ref)

    for start in range(0, q_ref.shape[0], TILE):
        shifts = tile_shifts(pos_ref, start, tiles)
        block = slice(start, start + TILE)
        queries, grads = q_ref[block, :], g_ref[block, :]
        log_total = log_ref[0, :, block]
        inner = jnp.zeros((1, TILE), F32)
        for at in range(tiles):
            span = slice(start + at * TILE, start + (at + 1) * TILE)
            scores = lax.dot_general(k_ref[span, :], queries, NT, preferred_element_type=F32)
            scores = masked_tile(scores, at, tiles, shifts[at])
            probability = jnp.exp(scores - log_total)
            grad = lax.dot_general(v_ref[span, :], grads, NT, preferred_element_type=F32)
            inner = inner + jnp.sum(probability * grad, axis=0, keepdims=True)
            p_ref[at] = probability
            gp_ref[at] = grad
        query_grad = jnp.zeros((size, TILE), F32)
        for at in range(tiles):
            span = slice(start + at * TILE, start + (at + 1) * TILE)
            probability = p_ref[at]
            score_grad = (probability * (gp_ref[at] - inner)).astype(BF16)
            k_grad_ref[span, :] += jnp.dot(score_grad, queries, preferred_element_type=F32)
            v_grad_ref[span, :] += jnp.dot(
                probability.astype(BF16), grads, preferred_element_type=F32
            )
            query_grad = query_grad + jnp.dot(
                turned_ref[:, span], score_grad, preferred_element_type=F32
            )
        query_grad = query_grad.T * size ** (-0.5)
        turn = cos_ref.shape[1]
        rotated = query_grad[:, :turn]
        rotated = (
            rotated * cos_ref[block, :] + pltpu.roll(rotated, turn // 2, 1) * sin_ref[block, :]
        )
        q_grad_ref[block, :turn] = rotated.astype(BF16)
        q_grad_ref[block, turn:] = query_grad[:, turn:].astype(BF16)

    @pl.when(pl.program_id(0) == pl.num_programs(0) - 1)
    def _():
        first = pos_ref[1] == 0
        for start in range(0, k_ref.shape[0], TILE):
            block = slice(start, start + TILE)
            k_grad, v_grad = k_grad_ref[block, :], v_grad_ref[block, :]
            keep_ref[block, :] = jnp.where(first, k_grad, v_grad)
            sent_ref[block, :] = jnp.where(first, v_grad, k_grad).astype(BF16)


def attend_back(first_pos, core, queries, grads, key_rows, value_rows, log_total, cosine, sine):
    rows, cols = queries.shape
    span, size = key_rows.shape
    heads = cols // size
    by_head = pl.BlockSpec((rows, size), lambda head: (0, head))
    whole = pl.BlockSpec((span, size), lambda head: (0, 0))
    tile_shape = (WINDOW // TILE + 1, TILE, TILE)
    return pl.pallas_call(
        attend_back_kernel,
        out_shape=(
            jax.ShapeDtypeStruct((rows, cols), BF16),
            jax.ShapeDtypeStruct((span, size), F32),
            jax.ShapeDtypeStruct((span, size), BF16),
        ),
        grid=(heads,),
        in_specs=[
            pl.BlockSpec(memory_space=pltpu.SMEM), by_head, by_head, whole, whole,
            pl.BlockSpec((1, 1, rows), lambda head: (head, 0, 0)),
            pl.BlockSpec(cosine.shape, lambda head: (0, 0)),
            pl.BlockSpec(sine.shape, lambda head: (0, 0)),
        ],
        out_specs=(by_head, whole, whole),
        scratch_shapes=[
            pltpu.VMEM((size, span), BF16),
            pltpu.VMEM(tile_shape, F32),
            pltpu.VMEM(tile_shape, F32),
            pltpu.VMEM((span, size), F32),
            pltpu.VMEM((span, size), F32),
        ],
        compiler_params=pltpu.CompilerParams(vmem_limit_bytes=48 * 2**20),
        cost_estimate=pl.CostEstimate(flops=1000, bytes_accessed=1000, transcendentals=0),
        name="attend_back",
    )(jnp.stack([first_pos, core]), queries, grads, key_rows, value_rows, log_total, cosine, sine)

def gelu_parts(gate):
    root = 0.7978845608028654
    square = gate * gate
    tanh = jnp.tanh(root * gate * (1.0 + 0.044715 * square))
    half = 0.5 * (1.0 + tanh)
    slope = half + 0.5 * gate * (1.0 - tanh * tanh) * root * (1.0 + 3 * 0.044715 * square)
    return gate * half, slope

def ffn_kernel(x_ref, w_ref, act_ref, a_ref, b_ref, total_ref):
    steps = 5
    depth = w_ref.shape[0] // steps
    total_ref[...] = jnp.dot(x_ref[:, :depth], w_ref[:depth, :], preferred_element_type=F32)
    for step in range(1, steps):
        part = slice(step * depth, (step + 1) * depth)
        total_ref[...] += jnp.dot(x_ref[:, part], w_ref[part, :], preferred_element_type=F32)
    hidden = act_ref.shape[1]
    main = hidden // 128 * 128
    for start in range(0, main, 128):
        cols = slice(start, start + 128)
        gate, up = total_ref[:, cols], total_ref[:, main + start : main + start + 128]
        gelu, slope = gelu_parts(gate)
        act_ref[:, cols] = (gelu * up).astype(BF16)
        a_ref[:, cols] = (slope * up).astype(BF16)
        b_ref[:, cols] = gelu.astype(BF16)
    last = total_ref[:, 2 * main :]
    up = pltpu.roll(last, 64, 1)
    gelu, slope = gelu_parts(last)
    act_ref[:, main:] = (gelu * up)[:, :64].astype(BF16)
    a_ref[:, main:] = (slope * up)[:, :64].astype(BF16)
    b_ref[:, main:] = gelu[:, :64].astype(BF16)

def ffn(x, w, rows=512):
    count, width = x.shape
    hidden = w.shape[1] // 2
    tile = pl.BlockSpec((rows, hidden), lambda i: (i, 0))
    return pl.pallas_call(
        ffn_kernel,
        out_shape=(jax.ShapeDtypeStruct((count, hidden), BF16),) * 3,
        grid=(count // rows,),
        in_specs=[
            pl.BlockSpec((rows, width), lambda i: (i, 0)),
            pl.BlockSpec(w.shape, lambda i: (0, 0), pipeline_mode=pl.Buffered(1)),
        ],
        out_specs=(tile,) * 3,
        scratch_shapes=[pltpu.VMEM((rows, 2 * hidden), F32)],
        compiler_params=pltpu.CompilerParams(vmem_limit_bytes=56 * 2**20),
        cost_estimate=pl.CostEstimate(flops=1000, bytes_accessed=1000, transcendentals=0),
        name="ffn",
    )(x, w)

def ffn_back_kernel(c_ref, d_ref, a_ref, b_ref, w_ref, g_ref, out_ref):
    hidden = a_ref.shape[1]
    main = hidden // 128 * 128
    act_grad = lax.dot_general(c_ref[...], d_ref[...], NT, preferred_element_type=F32)
    g_ref[:, :main] = (act_grad[:, :main] * a_ref[:, :main].astype(F32)).astype(BF16)
    g_ref[:, main : 2 * main] = (act_grad[:, :main] * b_ref[:, :main].astype(F32)).astype(BF16)
    last = act_grad[:, main:]
    g_ref[:, 2 * main :] = jnp.concatenate(
        [last * a_ref[:, main:].astype(F32), last * b_ref[:, main:].astype(F32)], axis=1
    ).astype(BF16)
    out_ref[...] = lax.dot_general(
        g_ref[...], w_ref[...], NT, preferred_element_type=F32
    ).astype(BF16)

def ffn_back(cot, down, a, b, w, rows=256):
    count, width = cot.shape
    hidden = a.shape[1]
    by_rows = lambda cols: pl.BlockSpec((rows, cols), lambda i: (i, 0))
    once = lambda v: pl.BlockSpec(v.shape, lambda i: (0, 0), pipeline_mode=pl.Buffered(1))
    return pl.pallas_call(
        ffn_back_kernel,
        out_shape=(
            jax.ShapeDtypeStruct((count, 2 * hidden), BF16),
            jax.ShapeDtypeStruct((count, width), BF16),
        ),
        grid=(count // rows,),
        in_specs=[by_rows(width), once(down), by_rows(hidden), by_rows(hidden), once(w)],
        out_specs=(by_rows(2 * hidden), by_rows(width)),
        compiler_params=pltpu.CompilerParams(vmem_limit_bytes=56 * 2**20),
        cost_estimate=pl.CostEstimate(flops=1000, bytes_accessed=1000, transcendentals=0),
        name="ffn_back",
    )(cot, down, a, b, w)


def join_kernel(seq_ref, *refs):
    pieces, (gate_w_ref, up_w_ref, gate_ref, up_ref, gain_ref) = refs[:4], refs[4:]
    hidden = pieces[0].shape[1] // 2
    main, rest = hidden // 128 * 128, hidden % 128
    for seq_at in range(4):

        @pl.when(seq_ref[0] == seq_at)
        def _():
            gain = jnp.zeros((gate_ref.shape[0], 1), F32)
            for out_ref, w_ref, spans in (
                (gate_ref, gate_w_ref, ((0, main), (2 * main, rest))),
                (up_ref, up_w_ref, ((main, main), (2 * main + rest, rest))),
            ):
                grad = jnp.concatenate(
                    [
                        pieces[at ^ seq_at][:, start : start + count].astype(F32)
                        for at in range(4)
                        for start, count in spans
                    ],
                    axis=1,
                )
                out_ref[...] = grad
                gain += jnp.sum(grad * w_ref[...].astype(F32), axis=1, keepdims=True)
            gain_ref[...] = gain


def join_columns(seq_at, pieces, w_gate, w_up):
    rows, cols = w_gate.shape
    tile = 64
    by_rows = lambda width: pl.BlockSpec((tile, width), lambda i: (i, 0))
    whole = jax.ShapeDtypeStruct((rows, cols), F32)
    gate, up, gain = pl.pallas_call(
        join_kernel,
        out_shape=(whole, whole, jax.ShapeDtypeStruct((rows, 1), F32)),
        grid=(rows // tile,),
        in_specs=[pl.BlockSpec(memory_space=pltpu.SMEM)]
        + [by_rows(pieces[0].shape[1])] * 4 + [by_rows(cols)] * 2,
        out_specs=(by_rows(cols), by_rows(cols), by_rows(1)),
        compiler_params=pltpu.CompilerParams(vmem_limit_bytes=40 * 2**20),
        cost_estimate=pl.CostEstimate(flops=1000, bytes_accessed=1000, transcendentals=0),
        name="join_columns",
    )(seq_at.reshape(1), *pieces, w_gate, w_up)
    return gate, up, gain[:, 0]


def local(
    inputs, cotangent, gain_attn, gain_ffn, w_query, w_key, w_value, w_out, w_gate, w_up, w_down
):
    rows, width = inputs.shape
    half = rows // 2
    head_size = w_key.shape[1]
    head_cols = w_query.shape[1]
    heads_here = head_cols // head_size
    seqs, shards = lax.axis_size("seq"), lax.axis_size("fsdp")
    assert rows * shards == WINDOW and lax.axis_size("tensor") == 2
    seq_at, shard_at, core = (lax.axis_index(name) for name in ("seq", "fsdp", "tensor"))
    first = core == 0
    key_span = rows + WINDOW
    first_pos = (seq_at * shards + shard_at) * rows
    scale = head_size ** (-0.5)
    rot_half = head_size // 4
    frequency = 10000.0 ** (-(jnp.arange(rot_half, dtype=F32) * 2.0) / (2 * rot_half))
    angles = (first_pos + jnp.arange(rows, dtype=jnp.int32)).astype(F32)[:, None] * frequency[None]
    cosine, sine = jnp.cos(angles), jnp.sin(angles)

    def my_half(value):
        return part_of(value, core, half, 0)

    def other_half(value):
        return part_of(value, 1 - core, half, 0)

    def whole_rows(own):
        other = swap(own)
        return jnp.where(first, jnp.stack([own, other]), jnp.stack([other, own])).reshape(
            rows, own.shape[1]
        )

    def plane_rows(own, other=None):
        near = plane_gather(own)
        far = [swap(piece) if at or other is None else other for at, piece in enumerate(near)]
        return jnp.concatenate(near + far, axis=0)

    def core_sum(partial):
        count = seqs * half
        cores = partial[:count].astype(F32) + swap(partial[count:].astype(BF16)).astype(F32)
        return [cores[j * half : (j + 1) * half] for j in range(seqs)]

    def plane_sum(partial):
        parts = core_sum(partial)
        return scatter_end(*scatter_far(parts, scatter_near(parts)))

    def order_cols(pieces):
        stacked = jnp.stack(pieces)
        return [pick(stacked, seq_at ^ at) for at in range(seqs)]

    gain_one, gain_two = gain_attn.astype(F32)[:, None], gain_ffn.astype(F32)[:, None]
    gains = jnp.stack([gain_attn, gain_ffn])
    gains = jnp.stack(
        [gains]
        + [
            lax.ppermute(gains, "fsdp", [((at + by) % shards, at) for at in range(shards)])
            for by in range(1, shards)
        ]
    )
    gains = jnp.concatenate(
        [pick(gains, (at - shard_at) % shards) for at in range(shards)], axis=1
    ).astype(F32)
    pair_shard = jnp.where(first, w_key, w_value)
    proj_shard = jnp.concatenate([w_query, pair_shard], axis=1)
    proj_cols = proj_shard.shape[1] // seqs
    out_rows = head_cols // seqs
    proj_weight = lax.all_gather(
        part_of(proj_shard, seq_at, proj_cols, 1), "fsdp", axis=0, tiled=True
    )
    hidden = w_gate.shape[1] // seqs
    kernels = hidden % 128 == 64
    main = hidden // 128 * 128 if kernels else hidden
    gate_mine, up_mine = (part_of(value, seq_at, hidden, 1) for value in (w_gate, w_up))
    pair_in = jnp.concatenate(
        [gate_mine[:, :main], up_mine[:, :main], gate_mine[:, main:], up_mine[:, main:]], axis=1
    )
    in_weight = lax.all_gather(pair_in, "fsdp", axis=0, tiled=True)
    down_weight = lax.all_gather(
        part_of(w_down, seq_at, hidden, 0), "fsdp", axis=1, tiled=True
    )

    source = my_half(inputs).astype(F32)
    inverse_one = inverse_rms(source)
    unit_one = (source * inverse_one * gains[0]).astype(BF16)
    square = seqs == 4
    out_quarter = lax.all_gather(
        part_of(w_out, seq_at, out_rows, 0), "fsdp", axis=1, tiled=True
    )
    rows_one = gather_rows(unit_one, 1) if square else plane_rows(unit_one)
    proj = jnp.dot(rows_one, proj_weight, preferred_element_type=F32)
    rotate_first = proj_cols % (2 * rot_half) == 0
    if rotate_first:
        halves_at = jnp.where(first, jnp.arange(2), 1 - jnp.arange(2))[:, None, None]
        seqs_at = (seq_at ^ jnp.arange(seqs))[None, :, None]
        row_pos = (
            (seqs_at * shards + shard_at) * rows + halves_at * half + jnp.arange(half)[None, None]
        ).reshape(-1)
        row_angles = row_pos.astype(F32)[:, None] * frequency[None]
        units = proj_cols // (2 * rot_half)
        unit_at = seq_at * units + jnp.arange(units)
        head_units = head_cols // (2 * rot_half)
        turned = (unit_at % 2 == 0) & (first | (unit_at < head_units))
        unit_scale = jnp.where(unit_at < head_units, scale, 1.0)[None, :, None]
        turned = turned[None, :, None]
        row_cos = jnp.where(turned, jnp.cos(row_angles)[:, None], 1.0) * unit_scale
        row_sin = jnp.where(turned, jnp.sin(row_angles)[:, None], 0.0) * unit_scale
        proj = rotate(proj.reshape(-1, units, 2 * rot_half), row_cos, row_sin)
    proj = proj.astype(BF16).reshape(2 * seqs * half, proj_cols)
    if square and rotate_first:
        proj_here = trade(proj, False, 5)
    else:
        proj = proj.reshape(2, seqs, half, proj_cols)
        proj = jnp.where(first, proj, proj[::-1])
        proj_parts = [proj[:, 0].reshape(rows, proj_cols)] + [
            exchange(proj[:, at].reshape(rows, proj_cols), at) for at in range(1, seqs)
        ]
        proj_here = jnp.concatenate(order_cols(proj_parts), axis=1)
    queries = proj_here[:, :head_cols]
    pair_here = proj_here[:, head_cols:]
    if not rotate_first:
        queries = queries.reshape(rows, heads_here, head_size).astype(F32)
        queries = (rotate(queries, cosine[:, None], sine[:, None]) * scale).astype(BF16)
        queries = queries.reshape(rows, head_cols)
        pair_here = jnp.where(first, rotate(pair_here.astype(F32), cosine, sine), pair_here)
        pair_here = pair_here.astype(BF16)

    earlier = seq_shift(pair_here, 1)
    slots = [
        lax.ppermute(
            jnp.where(shard_at >= at, earlier, pair_here),
            "fsdp", [(source_at, (source_at - at) % shards) for source_at in range(shards)],
        )
        for at in range(1, shards)
    ]
    window_here = jnp.concatenate([earlier] + slots + [pair_here], axis=0)
    window_here, *out_pieces = lax.optimization_barrier((window_here, *plane_gather(out_quarter)))
    window_other = swap(window_here)
    key_rows = jnp.where(first, window_here, window_other)
    value_rows = jnp.where(first, window_other, window_here)

    out_weight = jnp.zeros((head_cols, width), BF16)
    for at, piece in enumerate(out_pieces):
        out_weight = lax.dynamic_update_slice_in_dim(
            out_weight, piece, (seq_at ^ at) * out_rows, 0
        )

    head_outputs, log_total = attend(first_pos, queries, key_rows, value_rows)

    out_part = jnp.dot(head_outputs, out_weight, preferred_element_type=F32)
    hidden_in = source + my_half(out_part) + swap(other_half(out_part))
    inverse_two = inverse_rms(hidden_in)
    unit_two = (hidden_in * inverse_two * gains[1]).astype(BF16)
    rows_two = gather_rows(unit_two, 2) if square else plane_rows(unit_two)
    cot_later = after(cotangent, out_weight)
    rows_cot = plane_rows(my_half(cot_later), other_half(cot_later))

    if kernels:
        activation, gate_factor, up_factor = ffn(rows_two, in_weight)
        down_term = rows_product(rows_cot, activation).astype(BF16)
        gate_factor, proj_later, _ = lax.optimization_barrier(
            (gate_factor, proj_weight, down_term)
        )
        grad_in, back_part = ffn_back(rows_cot, down_weight, gate_factor, up_factor, in_weight)
    else:
        in_proj = jnp.dot(rows_two, in_weight, preferred_element_type=F32)
        gate_pre, up_proj = in_proj[:, :hidden], in_proj[:, hidden:]
        activation = gated_unit(gate_pre, up_proj).astype(BF16)
        down_term = rows_product(rows_cot, activation).astype(BF16)
        grad_activation = times_transpose(rows_cot, down_weight)
        grad_gate, grad_up = jax.vjp(gated_unit, gate_pre, up_proj)[1](grad_activation)
        grad_in = jnp.concatenate([grad_gate.astype(BF16), grad_up.astype(BF16)], axis=1)
        back_part = times_transpose(grad_in, in_weight)
        proj_later = after(proj_weight, down_term)
    grad_in, proj_near = lax.optimization_barrier((grad_in, gather_near(proj_later)))
    proj_pieces = gather_far(proj_later, proj_near)
    in_term = rows_product(rows_two, grad_in).astype(BF16)
    back_part, proj_pieces, in_term = lax.optimization_barrier((back_part, proj_pieces, in_term))
    grad_unit_two = scatter_rows(back_part, 3) if square else plane_sum(back_part)
    grad_hidden = my_half(cotangent).astype(F32) + norm_pull(
        hidden_in, inverse_two, grad_unit_two * gains[1]
    )
    down_shard = lax.psum_scatter(down_term, "fsdp", scatter_dimension=0, tiled=True).T
    in_shard = lax.psum_scatter(in_term, "fsdp", scatter_dimension=0, tiled=True)

    grad_attn_out = whole_rows(grad_hidden.astype(BF16))
    grad_heads = times_transpose(grad_attn_out, out_weight).astype(BF16)
    ffn_part = jnp.dot(
        after(activation, grad_unit_two), down_weight, preferred_element_type=F32
    ).astype(BF16)
    out_term = rows_product(head_outputs, grad_attn_out).astype(BF16)
    down_near = gather_near(down_shard)
    grad_heads, down_near, ffn_part, out_term = lax.optimization_barrier(
        (grad_heads, down_near, ffn_part, out_term)
    )
    out_parts = [part_of(out_term, seq_at ^ at, out_rows, 0) for at in range(seqs)]
    out_near = scatter_near(out_parts)
    grad_query_proj, pair_keep, pair_sent = attend_back(
        first_pos, core, queries, grad_heads, key_rows, value_rows, log_total,
        jnp.concatenate([cosine, cosine], axis=1), jnp.concatenate([sine, -sine], axis=1),
    )
    pair_grads = pair_keep + swap(pair_sent).astype(F32)
    pair_grads, down_near = lax.optimization_barrier((pair_grads, down_near))
    returned = [
        lax.ppermute(
            pair_grads[at * rows : (at + 1) * rows].astype(BF16),
            "fsdp", [((source_at - at) % shards, source_at) for source_at in range(shards)],
        )
        for at in range(1, shards)
    ]
    ffn_cores = core_sum(ffn_part)
    returned, out_near, ffn_cores = lax.optimization_barrier((returned, out_near, ffn_cores))
    out_sum, out_far = scatter_far(out_parts, out_near)
    own_total = pair_grads[shards * rows :]
    earlier_total = pair_grads[:rows]
    for at, piece in enumerate(returned, 1):
        own_total = own_total + jnp.where(shard_at >= at, 0.0, piece.astype(F32))
        earlier_total = earlier_total + jnp.where(shard_at >= at, piece.astype(F32), 0.0)
    own_total = own_total + seq_shift(earlier_total.astype(BF16), -1).astype(F32)
    grad_pair = jnp.where(first, rotate(own_total, cosine, -sine), own_total).astype(BF16)
    ffn_near = scatter_near(ffn_cores)
    grad_pair, in_shard, out_far, ffn_near, down_parts = lax.optimization_barrier(
        (grad_pair, in_shard, out_far, ffn_near, gather_far(down_shard, down_near))
    )
    out_sum = scatter_end(out_sum, out_far)
    grad_proj = jnp.concatenate([grad_query_proj, grad_pair], axis=1)
    if square:
        grad_rows = trade(grad_proj, True, 6)
    else:
        grad_parts = [part_of(grad_proj, seq_at, proj_cols, 1)] + [
            exchange(part_of(grad_proj, seq_at ^ at, proj_cols, 1), at) for at in range(1, seqs)
        ]
        grad_rows = jnp.stack(grad_parts).reshape(seqs, 2, half, proj_cols).swapaxes(0, 1)
        grad_rows = jnp.where(first, grad_rows, grad_rows[::-1])
        grad_rows = grad_rows.reshape(2 * seqs * half, proj_cols)
    proj_term = rows_product(rows_one, grad_rows).astype(BF16)

    out_shard = lax.psum_scatter(out_sum.astype(BF16), "fsdp", scatter_dimension=1, tiled=True)
    proj_sum = lax.psum_scatter(proj_term, "fsdp", scatter_dimension=0, tiled=True)
    in_parts = plane_gather(after(in_shard, grad_rows))
    grad_proj = after(grad_proj, proj_term)
    if square:
        unit_part = unit_grads(seq_at, grad_proj, proj_pieces)
    else:
        unit_part = sum(
            times_transpose(part_of(grad_proj, seq_at ^ at, proj_cols, 1), proj_pieces[at])
            for at in range(seqs)
        )
    grad_unit_one = my_half(unit_part) + swap(other_half(unit_part))
    grad_unit_one, proj_sum = lax.optimization_barrier((grad_unit_one, proj_sum))
    ffn_sum, ffn_far = scatter_far(ffn_cores, after(ffn_near, proj_term))
    ffn_out = scatter_end(ffn_sum, after(ffn_far, grad_unit_one))
    layer_out = whole_rows((hidden_in + ffn_out).astype(BF16))
    down_parts = lax.optimization_barrier((*down_parts, grad_unit_one))[:-1]
    down_grad = jnp.concatenate(order_cols(down_parts), axis=0).astype(F32)
    grad_input = whole_rows(
        grad_hidden + norm_pull(source, inverse_one, grad_unit_one * gains[0])
    )
    if kernels and square:
        in_parts, down_grad, grad_input, layer_out = lax.optimization_barrier(
            (in_parts, down_grad, grad_input, layer_out)
        )
        gate_grad, up_grad, gain_two_half = join_columns(seq_at, in_parts, w_gate, w_up)
    else:
        in_parts = order_cols(in_parts)
        rest = hidden - main
        gate_grad, up_grad = (
            jnp.concatenate(
                [
                    piece[:, first_at : first_at + count]
                    for piece in in_parts
                    for first_at, count in spans
                    if count
                ],
                axis=1,
            ).astype(F32)
            for spans in (((0, main), (2 * main, rest)), ((main, main), (2 * main + rest, rest)))
        )
        gain_two_half = jnp.sum(
            gate_grad * w_gate.astype(F32) + up_grad * w_up.astype(F32), axis=1
        )
    gain_two_half = gain_two_half / gain_two[:, 0]
    out_grad = jnp.concatenate(order_cols(plane_gather(out_shard)), axis=0).astype(F32)

    proj_grad = jnp.concatenate(order_cols(plane_gather(proj_sum)), axis=1).astype(F32)
    gain_one_half = jnp.sum(proj_grad * proj_shard.astype(F32), axis=1) / gain_one[:, 0]
    query_grad = proj_grad[:, :head_cols]
    pair_grad = proj_grad[:, head_cols:]
    pair_other = swap(pair_grad)
    gain_grads = jnp.stack([gain_one_half, gain_two_half])
    gain_grads = gain_grads + swap(gain_grads)
    return (
        layer_out,
        grad_input,
        gain_grads[0],
        gain_grads[1],
        query_grad,
        jnp.where(first, pair_grad, pair_other),
        jnp.where(first, pair_other, pair_grad),
        out_grad,
        gate_grad,
        up_grad,
        down_grad,
    )


def solution(mesh):
    rows = P(("seq", "fsdp"), None)
    specs = (
        P("fsdp"),
        P("fsdp"),
        P("fsdp", "tensor"),
        P("fsdp", None),
        P("fsdp", None),
        P("tensor", "fsdp"),
        P("fsdp", "tensor"),
        P("fsdp", "tensor"),
        P("tensor", "fsdp"),
    )
    return jax.shard_map(
        local, mesh=mesh, in_specs=(rows, rows) + specs, out_specs=(rows, rows) + specs,
        check_vma=False,
    )
```

```python
import functools

import jax
import jax.numpy as jnp
from jax import lax
from jax.experimental import pallas as pl
from jax.experimental.pallas import tpu as pltpu
from jax.sharding import PartitionSpec as P

WINDOW = 2048
EPSILON = 1e-06
F32 = jnp.float32
BF16 = jnp.bfloat16


def exchange(value, step):
    count = lax.axis_size("seq")
    return lax.ppermute(value, "seq", [(at, at ^ step) for at in range(count)])


def swap(value):
    return lax.ppermute(value, "tensor", [(0, 1), (1, 0)])


def seq_shift(value, steps):
    count = lax.axis_size("seq")
    leading, last = (max(0, -steps), min(count, count - steps))
    return lax.ppermute(value, "seq", [(at, at + steps) for at in range(leading, last)])


def gather_near(value):
    count = lax.axis_size("seq")
    steps = (1, 2) if count == 4 else range(1, count)
    return [exchange(value, step) for step in steps]


def gather_far(value, near):
    if lax.axis_size("seq") != 4:
        return [value, *near]
    half = value.shape[0] // 2
    far = jnp.concatenate([exchange(near[1][:half], 1), exchange(near[0][half:], 2)], axis=0)
    return [value, *near, far]


def plane_gather(value):
    return gather_far(value, gather_near(value))


def scatter_near(parts):
    if len(parts) != 4:
        return [exchange(part.astype(BF16), step) for step, part in enumerate(parts[1:], 1)]
    cut = parts[0].shape[0] // 2
    by_one = jnp.concatenate([parts[1][:cut], parts[3][:cut]]).astype(BF16)
    by_two = jnp.concatenate([parts[2][cut:], parts[3][cut:]]).astype(BF16)
    return [exchange(by_one, 1), exchange(by_two, 2)]


def scatter_far(parts, near):
    if len(parts) != 4:
        return sum((part.astype(F32) for part in near), parts[0].astype(F32)), []
    cut = parts[0].shape[0] // 2
    by_one, by_two = near
    last_top = (parts[2][:cut].astype(F32) + by_one[cut:].astype(F32)).astype(BF16)
    last_low = (parts[1][cut:].astype(F32) + by_two[cut:].astype(F32)).astype(BF16)
    total = parts[0].astype(F32) + jnp.concatenate([by_one[:cut], by_two[:cut]]).astype(F32)
    return total, [exchange(last_top, 2), exchange(last_low, 1)]


def scatter_end(total, far):
    return total + jnp.concatenate(far).astype(F32) if far else total


def times_transpose(left, right):
    return lax.dot_general(left, right, (((1,), (1,)), ((), ())), preferred_element_type=F32)


def rows_product(left, right):
    return lax.dot_general(left, right, (((0,), (0,)), ((), ())), preferred_element_type=F32)


def rotate(values, cosine, sine):
    half = cosine.shape[-1]
    first_part = values[..., :half]
    second_part = values[..., half : 2 * half]
    return jnp.concatenate(
        [
            first_part * cosine - second_part * sine,
            second_part * cosine + first_part * sine,
            values[..., 2 * half :],
        ],
        axis=-1,
    )


def inverse_rms(values):
    return lax.rsqrt(jnp.mean(values * values, axis=-1, keepdims=True) + EPSILON)


def norm_pull(values, inverse, grad):
    unit = values * inverse
    return inverse * (grad - unit * jnp.mean(grad * unit, axis=-1, keepdims=True))


def gated_unit(gate_pre, up_proj):
    return jax.nn.gelu(gate_pre) * up_proj


def pick(stacked, at):
    return lax.dynamic_index_in_dim(stacked, at, 0, keepdims=False)


def after(value, *others):
    return lax.optimization_barrier((value, *others))[0]


def part_of(value, at, size, axis):
    return lax.dynamic_slice_in_dim(value, at * size, size, axis)


MESH = pl.DeviceIdType.MESH


def greet(partners):
    barrier = pltpu.get_barrier_semaphore()
    for partner in partners:
        pl.semaphore_signal(barrier, inc=1, device_id=partner, device_id_type=MESH)
    pl.semaphore_wait(barrier, len(partners))


def plane_partners():
    seq_at, core = lax.axis_index("seq"), lax.axis_index("tensor")
    return {"seq": seq_at ^ 1}, {"seq": seq_at ^ 2}, {"tensor": 1 - core}


def send(source, target, sems, at, partner):
    copy = pltpu.make_async_remote_copy(
        src_ref=source, dst_ref=target, send_sem=sems.at[0, at], recv_sem=sems.at[1, at],
        device_id=partner, device_id_type=MESH,
    )
    copy.start()
    return copy


def rows_kernel(own_ref, out_ref, sems, local_sem):
    half = own_ref.shape[0]
    one, two, core = plane_partners()
    greet((one, two, core))

    def block(at, first=0, count=half):
        return out_ref.at[pl.ds(at * half + first, count), :]

    here = pltpu.make_async_copy(own_ref, block(0), local_sem)
    here.start()
    from_one = send(own_ref, block(1), sems, 0, one)
    from_two = send(own_ref, block(2), sems, 1, two)
    copies = [from_one, from_two, send(own_ref, block(4), sems, 2, core)]
    cut = half // 2
    from_one.wait_recv()
    far_low = send(block(1, cut, cut), block(3, cut, cut), sems, 3, two)
    copies.append(send(block(1), block(5), sems, 4, core))
    from_two.wait_recv()
    far_top = send(block(2, 0, cut), block(3, 0, cut), sems, 5, one)
    copies.append(send(block(2), block(6), sems, 6, core))
    far_low.wait_recv()
    far_top.wait_recv()
    copies.append(send(block(3), block(7), sems, 7, core))
    for copy in copies[2:]:
        copy.wait_recv()
    for copy in copies + [far_low, far_top]:
        copy.wait_send()
    here.wait()


def gather_rows(own, collective_id):
    half, width = own.shape
    return pl.pallas_call(
        rows_kernel,
        out_shape=jax.ShapeDtypeStruct((8 * half, width), own.dtype),
        in_specs=[pl.BlockSpec(memory_space=pl.ANY)],
        out_specs=pl.BlockSpec(memory_space=pl.ANY),
        scratch_shapes=[pltpu.SemaphoreType.DMA((2, 8)), pltpu.SemaphoreType.DMA],
        compiler_params=pltpu.CompilerParams(collective_id=collective_id, has_side_effects=True),
        cost_estimate=pl.CostEstimate(flops=1000, bytes_accessed=1000, transcendentals=0),
        name="gather_rows",
    )(own)


def unit_kernel(seq_ref, grad_ref, *refs):
    weights, out_ref = refs[:-1], refs[-1]
    cols = weights[0].shape[1]
    for at, weight_ref in enumerate(weights):
        part = pl.ds(pl.multiple_of((seq_ref[0] ^ at) * cols, 128), cols)
        term = lax.dot_general(
            grad_ref[:, part], weight_ref[...], NT, preferred_element_type=F32
        )
        if at:
            out_ref[...] += term
        else:
            out_ref[...] = term


def unit_grads(seq_at, grads, weights):
    vmem = pl.BlockSpec(memory_space=pltpu.VMEM)
    return pl.pallas_call(
        unit_kernel,
        out_shape=jax.ShapeDtypeStruct((grads.shape[0], weights[0].shape[0]), F32),
        in_specs=[pl.BlockSpec(memory_space=pltpu.SMEM), vmem] + [vmem] * len(weights),
        out_specs=vmem,
        compiler_params=pltpu.CompilerParams(vmem_limit_bytes=40 * 2**20),
        cost_estimate=pl.CostEstimate(flops=1000, bytes_accessed=1000, transcendentals=0),
        name="unit_grads",
    )(seq_at.reshape(1), grads, *weights)


def return_kernel(
    keep_ref, sent_ref, out_ref, land_ref, pass_ref, ring_ref, early_ref, back_ref, sems
):
    seqs, shards = lax.axis_size("seq"), lax.axis_size("fsdp")
    seq_at, shard_at = lax.axis_index("seq"), lax.axis_index("fsdp")
    rows = out_ref.shape[0]
    core = {"tensor": 1 - lax.axis_index("tensor")}
    behind, ahead = ({"seq": lax.rem(seq_at + by, seqs)} for by in (seqs - 1, 1))
    ring = [{"fsdp": lax.rem(shard_at + at, shards)} for at in range(1, shards)]
    greet([core, behind, ahead, *ring])
    slots = [pl.ds(at * rows, rows) for at in range(shards + 1)]
    lands = {
        at: send(sent_ref.at[slots[at], :], land_ref.at[slots[at], :], sems, at, core)
        for at in (*range(1, shards), 0, shards)
    }

    def chip_sum(at):
        lands[at].wait_recv()
        return keep_ref[slots[at], :] + land_ref[slots[at], :].astype(F32)

    rings = []
    for at in range(1, shards):
        pass_ref[at - 1] = chip_sum(at).astype(BF16)
        rings.append(send(pass_ref.at[at - 1], ring_ref.at[at - 1], sems, shards + at, ring[at - 1]))
    early, own = chip_sum(0), chip_sum(shards)
    for at, copy in enumerate(rings, 1):
        copy.wait_recv()
        piece = ring_ref[at - 1].astype(F32)
        share = jnp.where(shard_at >= at, 1.0, 0.0).astype(F32)
        early = early + piece * share
        own = own + piece * (1.0 - share)
    early_ref[...] = early.astype(BF16)
    shift = send(early_ref, back_ref, sems, 2 * shards, behind)
    shift.wait_recv()
    share = jnp.where(seq_at < seqs - 1, 1.0, 0.0).astype(F32)
    out_ref[...] = own + back_ref[...].astype(F32) * share
    for copy in (*lands.values(), *rings, shift):
        copy.wait_send()


def return_pairs(keep, sent, rows, shards, collective_id):
    size = keep.shape[1]
    vmem = pl.BlockSpec(memory_space=pltpu.VMEM)
    return pl.pallas_call(
        return_kernel,
        out_shape=jax.ShapeDtypeStruct((rows, size), F32),
        in_specs=[vmem, vmem],
        out_specs=vmem,
        scratch_shapes=[
            pltpu.VMEM(sent.shape, BF16),
            pltpu.VMEM((shards - 1, rows, size), BF16),
            pltpu.VMEM((shards - 1, rows, size), BF16),
            pltpu.VMEM((rows, size), BF16),
            pltpu.VMEM((rows, size), BF16),
            pltpu.SemaphoreType.DMA((2, 2 * shards + 1)),
        ],
        compiler_params=pltpu.CompilerParams(
            collective_id=collective_id, has_side_effects=True, vmem_limit_bytes=24 * 2**20
        ),
        cost_estimate=pl.CostEstimate(flops=1000, bytes_accessed=1000, transcendentals=0),
        name="return_pairs",
    )(keep, sent)


def trade_kernel(to_rows, value_ref, out_ref, sems, local_sems):
    seq_at, core = lax.axis_index("seq"), lax.axis_index("tensor")
    plane_ref, chip_ref = (out_ref, value_ref) if to_rows else (value_ref, out_ref)
    cols, half = plane_ref.shape[1], plane_ref.shape[0] // 8
    greet([{"seq": seq_at ^ step} for step in range(1, 4)])
    copies = []
    for step in (3, 1, 2, 0):
        for at in range(2):
            plane = plane_ref.at[pl.ds((at * 4 + step) * half, half), :]
            rows = pl.ds(pl.multiple_of((core if at == 0 else 1 - core) * half, half), half)
            owner = seq_at ^ step if to_rows else seq_at
            chip = chip_ref.at[rows, pl.ds(pl.multiple_of(owner * cols, 128), cols)]
            source, target = (chip, plane) if to_rows else (plane, chip)
            if step:
                sem_at = 2 * (step - 1) + at
                copies.append(send(source, target, sems, sem_at, {"seq": seq_at ^ step}))
            else:
                here = pltpu.make_async_copy(source, target, local_sems.at[at])
                here.start()
                copies.append(here)
    for copy in copies:
        copy.wait()


def trade(value, to_rows, collective_id):
    rows, cols = value.shape
    return pl.pallas_call(
        functools.partial(trade_kernel, to_rows),
        out_shape=jax.ShapeDtypeStruct(
            (rows * 4, cols // 4) if to_rows else (rows // 4, cols * 4), value.dtype
        ),
        in_specs=[pl.BlockSpec(memory_space=pl.ANY)],
        out_specs=pl.BlockSpec(memory_space=pl.ANY),
        scratch_shapes=[pltpu.SemaphoreType.DMA((2, 6)), pltpu.SemaphoreType.DMA((2,))],
        compiler_params=pltpu.CompilerParams(collective_id=collective_id, has_side_effects=True),
        cost_estimate=pl.CostEstimate(flops=1000, bytes_accessed=1000, transcendentals=0),
        name="trade",
    )(value)


def sum_kernel(
    part_ref, out_ref, own_ref, land_ref, total_ref, near_ref, sems, local_sems
):
    half = out_ref.shape[0]
    cut = half // 2
    chunk = 32
    one, two, core = plane_partners()
    greet((one, two, core))
    order = (3, 1, 2, 0)
    loads, lands = {}, {}
    for at in order:
        loads[at] = pltpu.make_async_copy(
            part_ref.at[pl.ds(at * half, half), :], own_ref.at[at], local_sems.at[at]
        )
        loads[at].start()
        lands[at] = send(
            part_ref.at[pl.ds((4 + at) * half, half), :], land_ref.at[at], sems, at, core
        )
    sent = []
    for at in order:
        loads[at].wait()
        lands[at].wait_recv()

        @pl.loop(0, half // chunk)
        def _(step):
            rows = pl.ds(pl.multiple_of(step * chunk, chunk), chunk)
            value = own_ref[at, rows, :].astype(F32) + land_ref[at, rows, :].astype(F32)
            if at:
                total_ref[at - 1, rows, :] = value.astype(BF16)
            else:
                out_ref[rows, :] = value

        top, low = (total_ref.at[at - 1, pl.ds(first, cut), :] for first in (0, cut))
        if at == 3:
            far_top = send(top, near_ref.at[1], sems, 4, one)
            far_low = send(low, near_ref.at[3], sems, 5, two)
        if at == 1:
            near_top = send(top, near_ref.at[0], sems, 6, one)
        if at == 2:
            near_low = send(low, near_ref.at[2], sems, 7, two)

    def add_in(at, first, from_at):
        @pl.loop(0, cut // chunk)
        def _(step):
            rows = pl.ds(pl.multiple_of(step * chunk, chunk), chunk)
            there = pl.ds(pl.multiple_of(first + step * chunk, chunk), chunk)
            value = total_ref[at, there, :].astype(F32) + near_ref[from_at, rows, :].astype(F32)
            total_ref[at, there, :] = value.astype(BF16)

    far_top.wait_recv()
    add_in(1, 0, 1)
    last_top = send(total_ref.at[1, pl.ds(0, cut), :], near_ref.at[4], sems, 8, two)
    far_low.wait_recv()
    add_in(0, cut, 3)
    last_low = send(total_ref.at[0, pl.ds(cut, cut), :], near_ref.at[5], sems, 9, one)

    for first, near, last, near_at, last_at in (
        (0, near_top, last_top, 0, 4), (cut, near_low, last_low, 2, 5),
    ):
        near.wait_recv()
        last.wait_recv()

        @pl.loop(0, cut // chunk)
        def _(step):
            rows = pl.ds(pl.multiple_of(step * chunk, chunk), chunk)
            there = pl.ds(pl.multiple_of(first + step * chunk, chunk), chunk)
            out_ref[there, :] += near_ref[near_at, rows, :].astype(F32) + near_ref[
                last_at, rows, :
            ].astype(F32)

    for copy in (*lands.values(), far_top, far_low, near_top, near_low, last_top, last_low):
        copy.wait_send()


def scatter_rows(part, collective_id):
    count, width = part.shape
    half = count // 8
    return pl.pallas_call(
        sum_kernel,
        out_shape=jax.ShapeDtypeStruct((half, width), F32),
        in_specs=[pl.BlockSpec(memory_space=pl.ANY)],
        out_specs=pl.BlockSpec(memory_space=pltpu.VMEM),
        scratch_shapes=[
            pltpu.VMEM((4, half, width), BF16),
            pltpu.VMEM((4, half, width), BF16),
            pltpu.VMEM((3, half, width), BF16),
            pltpu.VMEM((6, half // 2, width), BF16),
            pltpu.SemaphoreType.DMA((2, 10)),
            pltpu.SemaphoreType.DMA((4,)),
        ],
        compiler_params=pltpu.CompilerParams(
            collective_id=collective_id, has_side_effects=True, vmem_limit_bytes=40 * 2**20
        ),
        cost_estimate=pl.CostEstimate(flops=1000, bytes_accessed=1000, transcendentals=0),
        name="scatter_rows",
    )(part)


TILE = 256
NT = (((1,), (1,)), ((), ()))
LOWEST = -1e30


def masked_tile(scores, at, tiles, shift):
    scores = scores + shift
    if at in (0, tiles - 1):
        key_at = lax.broadcasted_iota(jnp.int32, scores.shape, 0)
        query_at = lax.broadcasted_iota(jnp.int32, scores.shape, 1)
        allowed = key_at > query_at if at == 0 else key_at <= query_at
        scores = jnp.where(allowed, scores, LOWEST)
    return scores

def tile_shifts(pos_ref, start, tiles):
    return [
        jnp.where(pos_ref[0] - WINDOW + start + at * TILE >= 0, 0.0, LOWEST).astype(F32)
        for at in range(tiles)
    ]

def attend_kernel(pos_ref, q_ref, k_ref, v_ref, out_ref, log_ref, turned_ref, score_ref):
    tiles = WINDOW // TILE + 1

    @pl.when(pl.program_id(0) == 0)
    def _():
        turned_ref[...] = v_ref[...].T

    for start in range(0, q_ref.shape[0], TILE):
        shifts = tile_shifts(pos_ref, start, tiles)
        queries = q_ref[start : start + TILE, :]
        top = jnp.full((1, TILE), LOWEST, F32)
        for at in range(tiles):
            keys = k_ref[start + at * TILE : start + (at + 1) * TILE, :]
            scores = lax.dot_general(keys, queries, NT, preferred_element_type=F32)
            scores = masked_tile(scores, at, tiles, shifts[at])
            score_ref[at] = scores
            top = jnp.maximum(top, jnp.max(scores, axis=0, keepdims=True))
        total = jnp.zeros((1, TILE), F32)
        for at in range(tiles):
            expon = jnp.exp(score_ref[at] - top)
            score_ref[at] = expon
            total = total + jnp.sum(expon, axis=0, keepdims=True)
        inverse = 1.0 / total
        attended = jnp.zeros((v_ref.shape[1], TILE), F32)
        for at in range(tiles):
            probability = (score_ref[at] * inverse).astype(BF16)
            values = turned_ref[:, start + at * TILE : start + (at + 1) * TILE]
            attended = attended + jnp.dot(values, probability, preferred_element_type=F32)
        out_ref[start : start + TILE, :] = attended.T.astype(BF16)
        log_ref[0, :, start : start + TILE] = top + jnp.log(total)

def attend(first_pos, queries, key_rows, value_rows):
    rows, cols = queries.shape
    span, size = key_rows.shape
    heads = cols // size
    return pl.pallas_call(
        attend_kernel,
        out_shape=(
            jax.ShapeDtypeStruct((rows, cols), BF16),
            jax.ShapeDtypeStruct((heads, 1, rows), F32),
        ),
        grid=(heads,),
        in_specs=[
            pl.BlockSpec(memory_space=pltpu.SMEM),
            pl.BlockSpec((rows, size), lambda head: (0, head)),
            pl.BlockSpec((span, size), lambda head: (0, 0)),
            pl.BlockSpec((span, size), lambda head: (0, 0)),
        ],
        out_specs=(
            pl.BlockSpec((rows, size), lambda head: (0, head)),
            pl.BlockSpec((1, 1, rows), lambda head: (head, 0, 0)),
        ),
        scratch_shapes=[
            pltpu.VMEM((size, span), BF16),
            pltpu.VMEM((WINDOW // TILE + 1, TILE, TILE), F32),
        ],
        compiler_params=pltpu.CompilerParams(vmem_limit_bytes=40 * 2**20),
        cost_estimate=pl.CostEstimate(flops=1000, bytes_accessed=1000, transcendentals=0),
        name="attend",
    )(first_pos.reshape(1), queries, key_rows, value_rows)

def attend_back_kernel(
    pos_ref, q_ref, g_ref, k_ref, v_ref, log_ref, cos_ref, sin_ref,
    q_grad_ref, keep_ref, sent_ref, turned_ref, p_ref, gp_ref, k_grad_ref, v_grad_ref,
):
    tiles = WINDOW // TILE + 1
    size = k_ref.shape[1]

    @pl.when(pl.program_id(0) == 0)
    def _():
        turned_ref[...] = k_ref[...].T
        k_grad_ref[...] = jnp.zeros_like(k_grad_ref)
        v_grad_ref[...] = jnp.zeros_like(v_grad_ref)

    for start in range(0, q_ref.shape[0], TILE):
        shifts = tile_shifts(pos_ref, start, tiles)
        block = slice(start, start + TILE)
        queries, grads = q_ref[block, :], g_ref[block, :]
        log_total = log_ref[0, :, block]
        inner = jnp.zeros((1, TILE), F32)
        for at in range(tiles):
            span = slice(start + at * TILE, start + (at + 1) * TILE)
            scores = lax.dot_general(k_ref[span, :], queries, NT, preferred_element_type=F32)
            scores = masked_tile(scores, at, tiles, shifts[at])
            probability = jnp.exp(scores - log_total)
            grad = lax.dot_general(v_ref[span, :], grads, NT, preferred_element_type=F32)
            inner = inner + jnp.sum(probability * grad, axis=0, keepdims=True)
            p_ref[at] = probability
            gp_ref[at] = grad
        query_grad = jnp.zeros((size, TILE), F32)
        for at in range(tiles):
            span = slice(start + at * TILE, start + (at + 1) * TILE)
            probability = p_ref[at]
            score_grad = (probability * (gp_ref[at] - inner)).astype(BF16)
            k_grad_ref[span, :] += jnp.dot(score_grad, queries, preferred_element_type=F32)
            v_grad_ref[span, :] += jnp.dot(
                probability.astype(BF16), grads, preferred_element_type=F32
            )
            query_grad = query_grad + jnp.dot(
                turned_ref[:, span], score_grad, preferred_element_type=F32
            )
        query_grad = query_grad.T * size ** (-0.5)
        turn = cos_ref.shape[1]
        rotated = query_grad[:, :turn]
        rotated = (
            rotated * cos_ref[block, :] + pltpu.roll(rotated, turn // 2, 1) * sin_ref[block, :]
        )
        q_grad_ref[block, :turn] = rotated.astype(BF16)
        q_grad_ref[block, turn:] = query_grad[:, turn:].astype(BF16)

    @pl.when(pl.program_id(0) == pl.num_programs(0) - 1)
    def _():
        first = pos_ref[1] == 0
        for start in range(0, k_ref.shape[0], TILE):
            block = slice(start, start + TILE)
            k_grad, v_grad = k_grad_ref[block, :], v_grad_ref[block, :]
            keep_ref[block, :] = jnp.where(first, k_grad, v_grad)
            sent_ref[block, :] = jnp.where(first, v_grad, k_grad).astype(BF16)


def attend_back(first_pos, core, queries, grads, key_rows, value_rows, log_total, cosine, sine):
    rows, cols = queries.shape
    span, size = key_rows.shape
    heads = cols // size
    by_head = pl.BlockSpec((rows, size), lambda head: (0, head))
    whole = pl.BlockSpec((span, size), lambda head: (0, 0))
    tile_shape = (WINDOW // TILE + 1, TILE, TILE)
    return pl.pallas_call(
        attend_back_kernel,
        out_shape=(
            jax.ShapeDtypeStruct((rows, cols), BF16),
            jax.ShapeDtypeStruct((span, size), F32),
            jax.ShapeDtypeStruct((span, size), BF16),
        ),
        grid=(heads,),
        in_specs=[
            pl.BlockSpec(memory_space=pltpu.SMEM), by_head, by_head, whole, whole,
            pl.BlockSpec((1, 1, rows), lambda head: (head, 0, 0)),
            pl.BlockSpec(cosine.shape, lambda head: (0, 0)),
            pl.BlockSpec(sine.shape, lambda head: (0, 0)),
        ],
        out_specs=(by_head, whole, whole),
        scratch_shapes=[
            pltpu.VMEM((size, span), BF16),
            pltpu.VMEM(tile_shape, F32),
            pltpu.VMEM(tile_shape, F32),
            pltpu.VMEM((span, size), F32),
            pltpu.VMEM((span, size), F32),
        ],
        compiler_params=pltpu.CompilerParams(vmem_limit_bytes=48 * 2**20),
        cost_estimate=pl.CostEstimate(flops=1000, bytes_accessed=1000, transcendentals=0),
        name="attend_back",
    )(jnp.stack([first_pos, core]), queries, grads, key_rows, value_rows, log_total, cosine, sine)

def gelu_parts(gate):
    root = 0.7978845608028654
    square = gate * gate
    tanh = jnp.tanh(root * gate * (1.0 + 0.044715 * square))
    half = 0.5 * (1.0 + tanh)
    slope = half + 0.5 * gate * (1.0 - tanh * tanh) * root * (1.0 + 3 * 0.044715 * square)
    return gate * half, slope

def ffn_kernel(x_ref, w_ref, act_ref, a_ref, b_ref, total_ref):
    steps = 5
    depth = w_ref.shape[0] // steps
    total_ref[...] = jnp.dot(x_ref[:, :depth], w_ref[:depth, :], preferred_element_type=F32)
    for step in range(1, steps):
        part = slice(step * depth, (step + 1) * depth)
        total_ref[...] += jnp.dot(x_ref[:, part], w_ref[part, :], preferred_element_type=F32)
    hidden = act_ref.shape[1]
    main = hidden // 128 * 128
    for start in range(0, main, 128):
        cols = slice(start, start + 128)
        gate, up = total_ref[:, cols], total_ref[:, main + start : main + start + 128]
        gelu, slope = gelu_parts(gate)
        act_ref[:, cols] = (gelu * up).astype(BF16)
        a_ref[:, cols] = (slope * up).astype(BF16)
        b_ref[:, cols] = gelu.astype(BF16)
    last = total_ref[:, 2 * main :]
    up = pltpu.roll(last, 64, 1)
    gelu, slope = gelu_parts(last)
    act_ref[:, main:] = (gelu * up)[:, :64].astype(BF16)
    a_ref[:, main:] = (slope * up)[:, :64].astype(BF16)
    b_ref[:, main:] = gelu[:, :64].astype(BF16)

def ffn(x, w, rows=512):
    count, width = x.shape
    hidden = w.shape[1] // 2
    tile = pl.BlockSpec((rows, hidden), lambda i: (i, 0))
    return pl.pallas_call(
        ffn_kernel,
        out_shape=(jax.ShapeDtypeStruct((count, hidden), BF16),) * 3,
        grid=(count // rows,),
        in_specs=[
            pl.BlockSpec((rows, width), lambda i: (i, 0)),
            pl.BlockSpec(w.shape, lambda i: (0, 0), pipeline_mode=pl.Buffered(1)),
        ],
        out_specs=(tile,) * 3,
        scratch_shapes=[pltpu.VMEM((rows, 2 * hidden), F32)],
        compiler_params=pltpu.CompilerParams(vmem_limit_bytes=56 * 2**20),
        cost_estimate=pl.CostEstimate(flops=1000, bytes_accessed=1000, transcendentals=0),
        name="ffn",
    )(x, w)

def ffn_back_kernel(c_ref, d_ref, a_ref, b_ref, w_ref, g_ref, out_ref):
    hidden = a_ref.shape[1]
    main = hidden // 128 * 128
    act_grad = lax.dot_general(c_ref[...], d_ref[...], NT, preferred_element_type=F32)
    g_ref[:, :main] = (act_grad[:, :main] * a_ref[:, :main].astype(F32)).astype(BF16)
    g_ref[:, main : 2 * main] = (act_grad[:, :main] * b_ref[:, :main].astype(F32)).astype(BF16)
    last = act_grad[:, main:]
    g_ref[:, 2 * main :] = jnp.concatenate(
        [last * a_ref[:, main:].astype(F32), last * b_ref[:, main:].astype(F32)], axis=1
    ).astype(BF16)
    out_ref[...] = lax.dot_general(
        g_ref[...], w_ref[...], NT, preferred_element_type=F32
    ).astype(BF16)

def ffn_back(cot, down, a, b, w, rows=256):
    count, width = cot.shape
    hidden = a.shape[1]
    by_rows = lambda cols: pl.BlockSpec((rows, cols), lambda i: (i, 0))
    once = lambda v: pl.BlockSpec(v.shape, lambda i: (0, 0), pipeline_mode=pl.Buffered(1))
    return pl.pallas_call(
        ffn_back_kernel,
        out_shape=(
            jax.ShapeDtypeStruct((count, 2 * hidden), BF16),
            jax.ShapeDtypeStruct((count, width), BF16),
        ),
        grid=(count // rows,),
        in_specs=[by_rows(width), once(down), by_rows(hidden), by_rows(hidden), once(w)],
        out_specs=(by_rows(2 * hidden), by_rows(width)),
        compiler_params=pltpu.CompilerParams(vmem_limit_bytes=56 * 2**20),
        cost_estimate=pl.CostEstimate(flops=1000, bytes_accessed=1000, transcendentals=0),
        name="ffn_back",
    )(cot, down, a, b, w)


def join_kernel(seq_ref, *refs):
    pieces, (gate_w_ref, up_w_ref, gate_ref, up_ref, gain_ref) = refs[:4], refs[4:]
    hidden = pieces[0].shape[1] // 2
    main, rest = hidden // 128 * 128, hidden % 128
    for seq_at in range(4):

        @pl.when(seq_ref[0] == seq_at)
        def _():
            gain = jnp.zeros((gate_ref.shape[0], 1), F32)
            for out_ref, w_ref, spans in (
                (gate_ref, gate_w_ref, ((0, main), (2 * main, rest))),
                (up_ref, up_w_ref, ((main, main), (2 * main + rest, rest))),
            ):
                grad = jnp.concatenate(
                    [
                        pieces[at ^ seq_at][:, start : start + count].astype(F32)
                        for at in range(4)
                        for start, count in spans
                    ],
                    axis=1,
                )
                out_ref[...] = grad
                gain += jnp.sum(grad * w_ref[...].astype(F32), axis=1, keepdims=True)
            gain_ref[...] = gain


def join_columns(seq_at, pieces, w_gate, w_up):
    rows, cols = w_gate.shape
    tile = 64
    by_rows = lambda width: pl.BlockSpec((tile, width), lambda i: (i, 0))
    whole = jax.ShapeDtypeStruct((rows, cols), F32)
    gate, up, gain = pl.pallas_call(
        join_kernel,
        out_shape=(whole, whole, jax.ShapeDtypeStruct((rows, 1), F32)),
        grid=(rows // tile,),
        in_specs=[pl.BlockSpec(memory_space=pltpu.SMEM)]
        + [by_rows(pieces[0].shape[1])] * 4 + [by_rows(cols)] * 2,
        out_specs=(by_rows(cols), by_rows(cols), by_rows(1)),
        compiler_params=pltpu.CompilerParams(vmem_limit_bytes=40 * 2**20),
        cost_estimate=pl.CostEstimate(flops=1000, bytes_accessed=1000, transcendentals=0),
        name="join_columns",
    )(seq_at.reshape(1), *pieces, w_gate, w_up)
    return gate, up, gain[:, 0]


def local(
    inputs, cotangent, gain_attn, gain_ffn, w_query, w_key, w_value, w_out, w_gate, w_up, w_down
):
    rows, width = inputs.shape
    half = rows // 2
    head_size = w_key.shape[1]
    head_cols = w_query.shape[1]
    heads_here = head_cols // head_size
    seqs, shards = lax.axis_size("seq"), lax.axis_size("fsdp")
    assert rows * shards == WINDOW and lax.axis_size("tensor") == 2
    seq_at, shard_at, core = (lax.axis_index(name) for name in ("seq", "fsdp", "tensor"))
    first = core == 0
    key_span = rows + WINDOW
    first_pos = (seq_at * shards + shard_at) * rows
    scale = head_size ** (-0.5)
    rot_half = head_size // 4
    frequency = 10000.0 ** (-(jnp.arange(rot_half, dtype=F32) * 2.0) / (2 * rot_half))
    angles = (first_pos + jnp.arange(rows, dtype=jnp.int32)).astype(F32)[:, None] * frequency[None]
    cosine, sine = jnp.cos(angles), jnp.sin(angles)

    def my_half(value):
        return part_of(value, core, half, 0)

    def other_half(value):
        return part_of(value, 1 - core, half, 0)

    def whole_rows(own):
        other = swap(own)
        return jnp.where(first, jnp.stack([own, other]), jnp.stack([other, own])).reshape(
            rows, own.shape[1]
        )

    def plane_rows(own, other=None):
        near = plane_gather(own)
        far = [swap(piece) if at or other is None else other for at, piece in enumerate(near)]
        return jnp.concatenate(near + far, axis=0)

    def core_sum(partial):
        count = seqs * half
        cores = partial[:count].astype(F32) + swap(partial[count:].astype(BF16)).astype(F32)
        return [cores[j * half : (j + 1) * half] for j in range(seqs)]

    def plane_sum(partial):
        parts = core_sum(partial)
        return scatter_end(*scatter_far(parts, scatter_near(parts)))

    def order_cols(pieces):
        stacked = jnp.stack(pieces)
        return [pick(stacked, seq_at ^ at) for at in range(seqs)]

    def order_rows(pieces):
        count, width = pieces[0].shape
        rows_all = jnp.zeros((seqs * count, width), F32)
        for at, piece in enumerate(pieces):
            rows_all = lax.dynamic_update_slice_in_dim(
                rows_all, piece.astype(F32), (seq_at ^ at) * count, 0
            )
        return rows_all

    gain_one, gain_two = gain_attn.astype(F32)[:, None], gain_ffn.astype(F32)[:, None]
    gains = jnp.stack([gain_attn, gain_ffn])
    gains = jnp.stack(
        [gains]
        + [
            lax.ppermute(gains, "fsdp", [((at + by) % shards, at) for at in range(shards)])
            for by in range(1, shards)
        ]
    )
    gains = jnp.concatenate(
        [pick(gains, (at - shard_at) % shards) for at in range(shards)], axis=1
    ).astype(F32)
    pair_shard = jnp.where(first, w_key, w_value)
    proj_shard = jnp.concatenate([w_query, pair_shard], axis=1)
    proj_cols = proj_shard.shape[1] // seqs
    out_rows = head_cols // seqs
    proj_weight = lax.all_gather(
        part_of(proj_shard, seq_at, proj_cols, 1), "fsdp", axis=0, tiled=True
    )
    hidden = w_gate.shape[1] // seqs
    kernels = hidden % 128 == 64
    main = hidden // 128 * 128 if kernels else hidden
    gate_mine, up_mine = (part_of(value, seq_at, hidden, 1) for value in (w_gate, w_up))
    pair_in = jnp.concatenate(
        [gate_mine[:, :main], up_mine[:, :main], gate_mine[:, main:], up_mine[:, main:]], axis=1
    )
    in_weight = lax.all_gather(pair_in, "fsdp", axis=0, tiled=True)
    down_weight = lax.all_gather(
        part_of(w_down, seq_at, hidden, 0), "fsdp", axis=1, tiled=True
    )

    source = my_half(inputs).astype(F32)
    inverse_one = inverse_rms(source)
    unit_one = (source * inverse_one * gains[0]).astype(BF16)
    square = seqs == 4
    out_quarter = lax.all_gather(
        part_of(w_out, seq_at, out_rows, 0), "fsdp", axis=1, tiled=True
    )
    rows_one = gather_rows(unit_one, 1) if square else plane_rows(unit_one)
    proj = jnp.dot(rows_one, proj_weight, preferred_element_type=F32)
    rotate_first = proj_cols % (2 * rot_half) == 0
    if rotate_first:
        halves_at = jnp.where(first, jnp.arange(2), 1 - jnp.arange(2))[:, None, None]
        seqs_at = (seq_at ^ jnp.arange(seqs))[None, :, None]
        row_pos = (
            (seqs_at * shards + shard_at) * rows + halves_at * half + jnp.arange(half)[None, None]
        ).reshape(-1)
        row_angles = row_pos.astype(F32)[:, None] * frequency[None]
        units = proj_cols // (2 * rot_half)
        unit_at = seq_at * units + jnp.arange(units)
        head_units = head_cols // (2 * rot_half)
        turned = (unit_at % 2 == 0) & (first | (unit_at < head_units))
        unit_scale = jnp.where(unit_at < head_units, scale, 1.0)[None, :, None]
        turned = turned[None, :, None]
        row_cos = jnp.where(turned, jnp.cos(row_angles)[:, None], 1.0) * unit_scale
        row_sin = jnp.where(turned, jnp.sin(row_angles)[:, None], 0.0) * unit_scale
        proj = rotate(proj.reshape(-1, units, 2 * rot_half), row_cos, row_sin)
    proj = proj.astype(BF16).reshape(2 * seqs * half, proj_cols)
    if square and rotate_first:
        proj_here = trade(proj, False, 5)
    else:
        proj = proj.reshape(2, seqs, half, proj_cols)
        proj = jnp.where(first, proj, proj[::-1])
        proj_parts = [proj[:, 0].reshape(rows, proj_cols)] + [
            exchange(proj[:, at].reshape(rows, proj_cols), at) for at in range(1, seqs)
        ]
        proj_here = jnp.concatenate(order_cols(proj_parts), axis=1)
    queries = proj_here[:, :head_cols]
    pair_here = proj_here[:, head_cols:]
    if not rotate_first:
        queries = queries.reshape(rows, heads_here, head_size).astype(F32)
        queries = (rotate(queries, cosine[:, None], sine[:, None]) * scale).astype(BF16)
        queries = queries.reshape(rows, head_cols)
        pair_here = jnp.where(first, rotate(pair_here.astype(F32), cosine, sine), pair_here)
        pair_here = pair_here.astype(BF16)

    earlier = seq_shift(pair_here, 1)
    slots = [
        lax.ppermute(
            jnp.where(shard_at >= at, earlier, pair_here),
            "fsdp", [(source_at, (source_at - at) % shards) for source_at in range(shards)],
        )
        for at in range(1, shards)
    ]
    window_here = jnp.concatenate([earlier] + slots + [pair_here], axis=0)
    window_here, *out_pieces = lax.optimization_barrier((window_here, *plane_gather(out_quarter)))
    window_other = swap(window_here)
    key_rows = jnp.where(first, window_here, window_other)
    value_rows = jnp.where(first, window_other, window_here)

    out_weight = jnp.zeros((head_cols, width), BF16)
    for at, piece in enumerate(out_pieces):
        out_weight = lax.dynamic_update_slice_in_dim(
            out_weight, piece, (seq_at ^ at) * out_rows, 0
        )

    head_outputs, log_total = attend(first_pos, queries, key_rows, value_rows)

    out_part = jnp.dot(head_outputs, out_weight, preferred_element_type=F32)
    hidden_in = source + my_half(out_part) + swap(other_half(out_part))
    inverse_two = inverse_rms(hidden_in)
    unit_two = (hidden_in * inverse_two * gains[1]).astype(BF16)
    rows_two = gather_rows(unit_two, 2) if square else plane_rows(unit_two)
    cot_later = after(cotangent, out_weight)
    rows_cot = plane_rows(my_half(cot_later), other_half(cot_later))

    if kernels:
        activation, gate_factor, up_factor = ffn(rows_two, in_weight)
        down_term = rows_product(rows_cot, activation).astype(BF16)
        gate_factor, proj_later, _ = lax.optimization_barrier(
            (gate_factor, proj_weight, down_term)
        )
        grad_in, back_part = ffn_back(rows_cot, down_weight, gate_factor, up_factor, in_weight)
    else:
        in_proj = jnp.dot(rows_two, in_weight, preferred_element_type=F32)
        gate_pre, up_proj = in_proj[:, :hidden], in_proj[:, hidden:]
        activation = gated_unit(gate_pre, up_proj).astype(BF16)
        down_term = rows_product(rows_cot, activation).astype(BF16)
        grad_activation = times_transpose(rows_cot, down_weight)
        grad_gate, grad_up = jax.vjp(gated_unit, gate_pre, up_proj)[1](grad_activation)
        grad_in = jnp.concatenate([grad_gate.astype(BF16), grad_up.astype(BF16)], axis=1)
        back_part = times_transpose(grad_in, in_weight)
        proj_later = after(proj_weight, down_term)
    grad_in, proj_near = lax.optimization_barrier((grad_in, gather_near(proj_later)))
    proj_pieces = gather_far(proj_later, proj_near)
    in_term = rows_product(rows_two, grad_in).astype(BF16)
    back_part, proj_pieces, in_term = lax.optimization_barrier((back_part, proj_pieces, in_term))
    grad_unit_two = scatter_rows(back_part, 3) if square else plane_sum(back_part)
    grad_hidden = my_half(cotangent).astype(F32) + norm_pull(
        hidden_in, inverse_two, grad_unit_two * gains[1]
    )
    down_shard = lax.psum_scatter(down_term, "fsdp", scatter_dimension=0, tiled=True).T
    in_shard = lax.psum_scatter(in_term, "fsdp", scatter_dimension=0, tiled=True)

    grad_attn_out = whole_rows(grad_hidden.astype(BF16))
    grad_heads = times_transpose(grad_attn_out, out_weight).astype(BF16)
    grad_heads, down_shard = lax.optimization_barrier((grad_heads, down_shard))
    grad_query_proj, pair_keep, pair_sent = attend_back(
        first_pos, core, queries, grad_heads, key_rows, value_rows, log_total,
        jnp.concatenate([cosine, cosine], axis=1), jnp.concatenate([sine, -sine], axis=1),
    )
    pair_sent, down_near = lax.optimization_barrier((pair_sent, gather_near(down_shard)))
    out_term = rows_product(after(head_outputs, pair_sent), grad_attn_out).astype(BF16)
    out_parts = [part_of(out_term, seq_at ^ at, out_rows, 0) for at in range(seqs)]
    out_near = scatter_near(out_parts)
    count = seqs * half
    activation = after(activation, out_term)
    ffn_other = jnp.dot(activation[count:], down_weight, preferred_element_type=F32)
    ffn_part = jnp.dot(
        after(activation[:count], ffn_other), down_weight, preferred_element_type=F32
    )
    ffn_part = (ffn_part + swap(ffn_other.astype(BF16)).astype(F32)).astype(BF16)
    ffn_cores = [ffn_part[j * half : (j + 1) * half] for j in range(seqs)]
    ffn_near = scatter_near(ffn_cores)
    pair_keep, pair_sent, _ = lax.optimization_barrier((pair_keep, pair_sent, ffn_part))
    if square:
        own_total = return_pairs(pair_keep, pair_sent, rows, shards, 1 + 6)
    else:
        pair_grads = pair_keep + swap(pair_sent).astype(F32)
        own_total = pair_grads[shards * rows :]
        earlier_total = pair_grads[:rows]
        for at in range(1, shards):
            piece = lax.ppermute(
                pair_grads[at * rows : (at + 1) * rows].astype(BF16),
                "fsdp",
                [((source_at - at) % shards, source_at) for source_at in range(shards)],
            ).astype(F32)
            own_total = own_total + jnp.where(shard_at >= at, 0.0, piece)
            earlier_total = earlier_total + jnp.where(shard_at >= at, piece, 0.0)
        own_total = own_total + seq_shift(earlier_total.astype(BF16), -1).astype(F32)
    own_total, out_near, ffn_near, down_near = lax.optimization_barrier(
        (own_total, out_near, ffn_near, down_near)
    )
    out_sum, out_far = scatter_far(out_parts, out_near)
    grad_pair = jnp.where(first, rotate(own_total, cosine, -sine), own_total).astype(BF16)
    grad_pair, in_shard, out_far, down_parts = lax.optimization_barrier(
        (grad_pair, in_shard, out_far, gather_far(down_shard, down_near))
    )
    grad_proj = jnp.concatenate([grad_query_proj, grad_pair], axis=1)
    if square:
        grad_rows = trade(grad_proj, True, 6)
    else:
        grad_parts = [part_of(grad_proj, seq_at, proj_cols, 1)] + [
            exchange(part_of(grad_proj, seq_at ^ at, proj_cols, 1), at) for at in range(1, seqs)
        ]
        grad_rows = jnp.stack(grad_parts).reshape(seqs, 2, half, proj_cols).swapaxes(0, 1)
        grad_rows = jnp.where(first, grad_rows, grad_rows[::-1])
        grad_rows = grad_rows.reshape(2 * seqs * half, proj_cols)
    proj_term = rows_product(rows_one, grad_rows).astype(BF16)

    out_sum = scatter_end(out_sum, after(out_far, proj_term))
    last_term = jnp.concatenate([proj_term, out_sum.astype(BF16).T], axis=1)
    last_sum = lax.psum_scatter(last_term, "fsdp", scatter_dimension=0, tiled=True)
    in_near = gather_near(after(in_shard, grad_rows))
    grad_proj = after(grad_proj, proj_term)
    if square:
        unit_part = unit_grads(seq_at, grad_proj, proj_pieces)
    else:
        unit_part = sum(
            times_transpose(part_of(grad_proj, seq_at ^ at, proj_cols, 1), proj_pieces[at])
            for at in range(seqs)
        )
    down_grad = order_rows(after(down_parts, grad_rows))
    ffn_sum, ffn_far = scatter_far(ffn_cores, after(ffn_near, proj_term))
    in_near, unit_part, down_grad = lax.optimization_barrier((in_near, unit_part, down_grad))
    in_parts = gather_far(in_shard, in_near)
    grad_unit_one = my_half(unit_part) + swap(other_half(unit_part))
    layer_half = (hidden_in + scatter_end(ffn_sum, ffn_far)).astype(BF16)
    grad_half = grad_hidden + norm_pull(source, inverse_one, grad_unit_one * gains[0])
    in_parts, grad_half = lax.optimization_barrier((in_parts, grad_half))
    layer_out, grad_input = whole_rows(layer_half), whole_rows(grad_half)
    if kernels and square:
        gate_grad, up_grad, gain_two_half = join_columns(seq_at, in_parts, w_gate, w_up)
    else:
        in_parts = order_cols(in_parts)
        rest = hidden - main
        gate_grad, up_grad = (
            jnp.concatenate(
                [
                    piece[:, first_at : first_at + count]
                    for piece in in_parts
                    for first_at, count in spans
                    if count
                ],
                axis=1,
            ).astype(F32)
            for spans in (((0, main), (2 * main, rest)), ((main, main), (2 * main + rest, rest)))
        )
        gain_two_half = jnp.sum(
            gate_grad * w_gate.astype(F32) + up_grad * w_up.astype(F32), axis=1
        )
    gain_two_half = gain_two_half / gain_two[:, 0]
    last_parts = gather_far(last_sum, after(gather_near(last_sum), gate_grad))
    out_grad = order_rows([piece[:, proj_cols:].T for piece in last_parts])
    proj_grad = jnp.concatenate(
        order_cols([piece[:, :proj_cols] for piece in last_parts]), axis=1
    ).astype(F32)
    gain_one_half = jnp.sum(proj_grad * proj_shard.astype(F32), axis=1) / gain_one[:, 0]
    query_grad = proj_grad[:, :head_cols]
    pair_grad = proj_grad[:, head_cols:]
    pair_other = swap(pair_grad)
    gain_grads = jnp.stack([gain_one_half, gain_two_half])
    gain_grads = gain_grads + swap(gain_grads)
    return (
        layer_out,
        grad_input,
        gain_grads[0],
        gain_grads[1],
        query_grad,
        jnp.where(first, pair_grad, pair_other),
        jnp.where(first, pair_other, pair_grad),
        out_grad,
        gate_grad,
        up_grad,
        down_grad,
    )


def solution(mesh):
    rows = P(("seq", "fsdp"), None)
    specs = (
        P("fsdp"),
        P("fsdp"),
        P("fsdp", "tensor"),
        P("fsdp", None),
        P("fsdp", None),
        P("tensor", "fsdp"),
        P("fsdp", "tensor"),
        P("fsdp", "tensor"),
        P("tensor", "fsdp"),
    )
    return jax.shard_map(
        local, mesh=mesh, in_specs=(rows, rows) + specs, out_specs=(rows, rows) + specs,
        check_vma=False,
    )
```

```python
import functools

import jax
import jax.numpy as jnp
from jax import lax
from jax.experimental import pallas as pl
from jax.experimental.pallas import tpu as pltpu
from jax.sharding import PartitionSpec as P

WINDOW = 2048
EPSILON = 1e-06
F32 = jnp.float32
BF16 = jnp.bfloat16


def exchange(value, step):
    count = lax.axis_size("seq")
    return lax.ppermute(value, "seq", [(at, at ^ step) for at in range(count)])


def swap(value):
    return lax.ppermute(value, "tensor", [(0, 1), (1, 0)])


def seq_shift(value, steps):
    count = lax.axis_size("seq")
    leading, last = (max(0, -steps), min(count, count - steps))
    return lax.ppermute(value, "seq", [(at, at + steps) for at in range(leading, last)])


def gather_near(value):
    count = lax.axis_size("seq")
    steps = (1, 2) if count == 4 else range(1, count)
    return [exchange(value, step) for step in steps]


def gather_far(value, near):
    if lax.axis_size("seq") != 4:
        return [value, *near]
    half = value.shape[0] // 2
    far = jnp.concatenate([exchange(near[1][:half], 1), exchange(near[0][half:], 2)], axis=0)
    return [value, *near, far]


def plane_gather(value):
    return gather_far(value, gather_near(value))


def scatter_near(parts):
    if len(parts) != 4:
        return [exchange(part.astype(BF16), step) for step, part in enumerate(parts[1:], 1)]
    cut = parts[0].shape[0] // 2
    by_one = jnp.concatenate([parts[1][:cut], parts[3][:cut]]).astype(BF16)
    by_two = jnp.concatenate([parts[2][cut:], parts[3][cut:]]).astype(BF16)
    return [exchange(by_one, 1), exchange(by_two, 2)]


def scatter_far(parts, near, send_on=True):
    if len(parts) != 4:
        return sum((part.astype(F32) for part in near), parts[0].astype(F32)), []
    cut = parts[0].shape[0] // 2
    by_one, by_two = near
    last_top = (parts[2][:cut].astype(F32) + by_one[cut:].astype(F32)).astype(BF16)
    last_low = (parts[1][cut:].astype(F32) + by_two[cut:].astype(F32)).astype(BF16)
    total = parts[0].astype(F32) + jnp.concatenate([by_one[:cut], by_two[:cut]]).astype(F32)
    if not send_on:
        return total, [last_top, last_low]
    return total, [exchange(last_top, 2), exchange(last_low, 1)]


def scatter_end(total, far):
    return total + jnp.concatenate(far).astype(F32) if far else total


def times_transpose(left, right):
    return lax.dot_general(left, right, (((1,), (1,)), ((), ())), preferred_element_type=F32)


def rows_product(left, right):
    return lax.dot_general(left, right, (((0,), (0,)), ((), ())), preferred_element_type=F32)


def rotate(values, cosine, sine):
    half = cosine.shape[-1]
    first_part = values[..., :half]
    second_part = values[..., half : 2 * half]
    return jnp.concatenate(
        [
            first_part * cosine - second_part * sine,
            second_part * cosine + first_part * sine,
            values[..., 2 * half :],
        ],
        axis=-1,
    )


def inverse_rms(values):
    return lax.rsqrt(jnp.mean(values * values, axis=-1, keepdims=True) + EPSILON)


def norm_pull(values, inverse, grad):
    unit = values * inverse
    return inverse * (grad - unit * jnp.mean(grad * unit, axis=-1, keepdims=True))


def gated_unit(gate_pre, up_proj):
    return jax.nn.gelu(gate_pre) * up_proj


def pick(stacked, at):
    return lax.dynamic_index_in_dim(stacked, at, 0, keepdims=False)


def after(value, *others):
    return lax.optimization_barrier((value, *others))[0]


def part_of(value, at, size, axis):
    return lax.dynamic_slice_in_dim(value, at * size, size, axis)


MESH = pl.DeviceIdType.MESH


def greet(partners):
    barrier = pltpu.get_barrier_semaphore()
    for partner in partners:
        pl.semaphore_signal(barrier, inc=1, device_id=partner, device_id_type=MESH)
    pl.semaphore_wait(barrier, len(partners))


def plane_partners():
    seq_at, core = lax.axis_index("seq"), lax.axis_index("tensor")
    return {"seq": seq_at ^ 1}, {"seq": seq_at ^ 2}, {"tensor": 1 - core}


def send(source, target, sems, at, partner):
    copy = pltpu.make_async_remote_copy(
        src_ref=source, dst_ref=target, send_sem=sems.at[0, at], recv_sem=sems.at[1, at],
        device_id=partner, device_id_type=MESH,
    )
    copy.start()
    return copy


def rows_kernel(own_ref, out_ref, sems, local_sem):
    half = own_ref.shape[0]
    one, two, core = plane_partners()
    greet((one, two, core))

    def block(at, first=0, count=half):
        return out_ref.at[pl.ds(at * half + first, count), :]

    here = pltpu.make_async_copy(own_ref, block(0), local_sem)
    here.start()
    from_one = send(own_ref, block(1), sems, 0, one)
    from_two = send(own_ref, block(2), sems, 1, two)
    copies = [from_one, from_two, send(own_ref, block(4), sems, 2, core)]
    cut = half // 2
    from_one.wait_recv()
    far_low = send(block(1, cut, cut), block(3, cut, cut), sems, 3, two)
    copies.append(send(block(1), block(5), sems, 4, core))
    from_two.wait_recv()
    far_top = send(block(2, 0, cut), block(3, 0, cut), sems, 5, one)
    copies.append(send(block(2), block(6), sems, 6, core))
    far_low.wait_recv()
    far_top.wait_recv()
    copies.append(send(block(3), block(7), sems, 7, core))
    for copy in copies[2:]:
        copy.wait_recv()
    for copy in copies + [far_low, far_top]:
        copy.wait_send()
    here.wait()


def gather_rows(own, collective_id):
    half, width = own.shape
    return pl.pallas_call(
        rows_kernel,
        out_shape=jax.ShapeDtypeStruct((8 * half, width), own.dtype),
        in_specs=[pl.BlockSpec(memory_space=pl.ANY)],
        out_specs=pl.BlockSpec(memory_space=pl.ANY),
        scratch_shapes=[pltpu.SemaphoreType.DMA((2, 8)), pltpu.SemaphoreType.DMA],
        compiler_params=pltpu.CompilerParams(collective_id=collective_id, has_side_effects=True),
        cost_estimate=pl.CostEstimate(flops=1000, bytes_accessed=1000, transcendentals=0),
        name="gather_rows",
    )(own)


def unit_kernel(seq_ref, grad_ref, *refs):
    weights, out_ref = refs[:-1], refs[-1]
    cols = weights[0].shape[1]
    for at, weight_ref in enumerate(weights):
        part = pl.ds(pl.multiple_of((seq_ref[0] ^ at) * cols, 128), cols)
        term = lax.dot_general(
            grad_ref[:, part], weight_ref[...], NT, preferred_element_type=F32
        )
        if at:
            out_ref[...] += term
        else:
            out_ref[...] = term


def unit_grads(seq_at, grads, weights):
    vmem = pl.BlockSpec(memory_space=pltpu.VMEM)
    return pl.pallas_call(
        unit_kernel,
        out_shape=jax.ShapeDtypeStruct((grads.shape[0], weights[0].shape[0]), F32),
        in_specs=[pl.BlockSpec(memory_space=pltpu.SMEM), vmem] + [vmem] * len(weights),
        out_specs=vmem,
        compiler_params=pltpu.CompilerParams(vmem_limit_bytes=40 * 2**20),
        cost_estimate=pl.CostEstimate(flops=1000, bytes_accessed=1000, transcendentals=0),
        name="unit_grads",
    )(seq_at.reshape(1), grads, *weights)


def return_kernel(steps, keep_ref, sent_ref, *refs):
    extras, (out_ref, *refs) = refs[: len(steps)], refs[len(steps) :]
    extra_outs, refs = refs[: len(steps)], refs[len(steps) :]
    land_ref, pass_ref, ring_ref, early_ref, back_ref, sems, extra_sems = refs
    seqs, shards = lax.axis_size("seq"), lax.axis_size("fsdp")
    seq_at, shard_at = lax.axis_index("seq"), lax.axis_index("fsdp")
    rows = out_ref.shape[0]
    core = {"tensor": 1 - lax.axis_index("tensor")}
    behind = {"seq": lax.rem(seq_at + seqs - 1, seqs)}
    ring = [{"fsdp": lax.rem(shard_at + at, shards)} for at in range(1, shards)]
    greet([core, *({"seq": seq_at ^ step} for step in range(1, 4)), *ring])
    slots = [pl.ds(at * rows, rows) for at in range(shards + 1)]
    lands = {
        at: send(sent_ref.at[slots[at], :], land_ref.at[slots[at], :], sems, at, core)
        for at in (*range(1, shards), 0, shards)
    }

    traded = [
        send(source, target, extra_sems, at, {"seq": seq_at ^ step})
        for at, (source, target, step) in enumerate(zip(extras, extra_outs, steps))
    ]

    def chip_sum(at):
        lands[at].wait_recv()
        return keep_ref[slots[at], :] + land_ref[slots[at], :].astype(F32)

    rings = []
    for at in range(1, shards):
        pass_ref[at - 1] = chip_sum(at).astype(BF16)
        rings.append(send(pass_ref.at[at - 1], ring_ref.at[at - 1], sems, shards + at, ring[at - 1]))
    early, own = chip_sum(0), chip_sum(shards)
    for at, copy in enumerate(rings, 1):
        copy.wait_recv()
        piece = ring_ref[at - 1].astype(F32)
        share = jnp.where(shard_at >= at, 1.0, 0.0).astype(F32)
        early = early + piece * share
        own = own + piece * (1.0 - share)
    early_ref[...] = early.astype(BF16)
    shift = send(early_ref, back_ref, sems, 2 * shards, behind)
    shift.wait_recv()
    share = jnp.where(seq_at < seqs - 1, 1.0, 0.0).astype(F32)
    out_ref[...] = own + back_ref[...].astype(F32) * share
    for copy in (*lands.values(), *rings, shift):
        copy.wait_send()
    for copy in traded:
        copy.wait()


def return_pairs(keep, sent, extras, steps, rows, shards, collective_id):
    size = keep.shape[1]
    any_place = [pl.BlockSpec(memory_space=pl.ANY)] * len(steps)
    vmem = pl.BlockSpec(memory_space=pltpu.VMEM)
    return pl.pallas_call(
        functools.partial(return_kernel, steps),
        out_shape=[jax.ShapeDtypeStruct((rows, size), F32)]
        + [jax.ShapeDtypeStruct(value.shape, value.dtype) for value in extras],
        in_specs=[vmem, vmem] + any_place,
        out_specs=[vmem] + any_place,
        scratch_shapes=[
            pltpu.VMEM(sent.shape, BF16),
            pltpu.VMEM((shards - 1, rows, size), BF16),
            pltpu.VMEM((shards - 1, rows, size), BF16),
            pltpu.VMEM((rows, size), BF16),
            pltpu.VMEM((rows, size), BF16),
            pltpu.SemaphoreType.DMA((2, 2 * shards + 1)),
            pltpu.SemaphoreType.DMA((2, len(steps))),
        ],
        compiler_params=pltpu.CompilerParams(
            collective_id=collective_id, has_side_effects=True, vmem_limit_bytes=24 * 2**20
        ),
        cost_estimate=pl.CostEstimate(flops=1000, bytes_accessed=1000, transcendentals=0),
        name="return_pairs",
    )(keep, sent, *extras)


def trade_kernel(to_rows, value_ref, out_ref, sems, local_sems):
    seq_at, core = lax.axis_index("seq"), lax.axis_index("tensor")
    plane_ref, chip_ref = (out_ref, value_ref) if to_rows else (value_ref, out_ref)
    cols, half = plane_ref.shape[1], plane_ref.shape[0] // 8
    greet([{"seq": seq_at ^ step} for step in range(1, 4)])
    copies = []
    for step in (3, 1, 2, 0):
        for at in range(2):
            plane = plane_ref.at[pl.ds((at * 4 + step) * half, half), :]
            rows = pl.ds(pl.multiple_of((core if at == 0 else 1 - core) * half, half), half)
            owner = seq_at ^ step if to_rows else seq_at
            chip = chip_ref.at[rows, pl.ds(pl.multiple_of(owner * cols, 128), cols)]
            source, target = (chip, plane) if to_rows else (plane, chip)
            if step:
                sem_at = 2 * (step - 1) + at
                copies.append(send(source, target, sems, sem_at, {"seq": seq_at ^ step}))
            else:
                here = pltpu.make_async_copy(source, target, local_sems.at[at])
                here.start()
                copies.append(here)
    for copy in copies:
        copy.wait()


def trade(value, to_rows, collective_id):
    rows, cols = value.shape
    return pl.pallas_call(
        functools.partial(trade_kernel, to_rows),
        out_shape=jax.ShapeDtypeStruct(
            (rows * 4, cols // 4) if to_rows else (rows // 4, cols * 4), value.dtype
        ),
        in_specs=[pl.BlockSpec(memory_space=pl.ANY)],
        out_specs=pl.BlockSpec(memory_space=pl.ANY),
        scratch_shapes=[pltpu.SemaphoreType.DMA((2, 6)), pltpu.SemaphoreType.DMA((2,))],
        compiler_params=pltpu.CompilerParams(collective_id=collective_id, has_side_effects=True),
        cost_estimate=pl.CostEstimate(flops=1000, bytes_accessed=1000, transcendentals=0),
        name="trade",
    )(value)


def sum_kernel(
    part_ref, out_ref, own_ref, land_ref, total_ref, near_ref, sems, local_sems
):
    half = out_ref.shape[0]
    cut = half // 2
    chunk = 32
    one, two, core = plane_partners()
    greet((one, two, core))
    order = (3, 1, 2, 0)
    loads, lands = {}, {}
    for at in order:
        loads[at] = pltpu.make_async_copy(
            part_ref.at[pl.ds(at * half, half), :], own_ref.at[at], local_sems.at[at]
        )
        loads[at].start()
        lands[at] = send(
            part_ref.at[pl.ds((4 + at) * half, half), :], land_ref.at[at], sems, at, core
        )
    sent = []
    for at in order:
        loads[at].wait()
        lands[at].wait_recv()

        @pl.loop(0, half // chunk)
        def _(step):
            rows = pl.ds(pl.multiple_of(step * chunk, chunk), chunk)
            value = own_ref[at, rows, :].astype(F32) + land_ref[at, rows, :].astype(F32)
            if at:
                total_ref[at - 1, rows, :] = value.astype(BF16)
            else:
                out_ref[rows, :] = value

        top, low = (total_ref.at[at - 1, pl.ds(first, cut), :] for first in (0, cut))
        if at == 3:
            far_top = send(top, near_ref.at[1], sems, 4, one)
            far_low = send(low, near_ref.at[3], sems, 5, two)
        if at == 1:
            near_top = send(top, near_ref.at[0], sems, 6, one)
        if at == 2:
            near_low = send(low, near_ref.at[2], sems, 7, two)

    def add_in(at, first, from_at):
        @pl.loop(0, cut // chunk)
        def _(step):
            rows = pl.ds(pl.multiple_of(step * chunk, chunk), chunk)
            there = pl.ds(pl.multiple_of(first + step * chunk, chunk), chunk)
            value = total_ref[at, there, :].astype(F32) + near_ref[from_at, rows, :].astype(F32)
            total_ref[at, there, :] = value.astype(BF16)

    far_top.wait_recv()
    add_in(1, 0, 1)
    last_top = send(total_ref.at[1, pl.ds(0, cut), :], near_ref.at[4], sems, 8, two)
    far_low.wait_recv()
    add_in(0, cut, 3)
    last_low = send(total_ref.at[0, pl.ds(cut, cut), :], near_ref.at[5], sems, 9, one)

    for first, near, last, near_at, last_at in (
        (0, near_top, last_top, 0, 4), (cut, near_low, last_low, 2, 5),
    ):
        near.wait_recv()
        last.wait_recv()

        @pl.loop(0, cut // chunk)
        def _(step):
            rows = pl.ds(pl.multiple_of(step * chunk, chunk), chunk)
            there = pl.ds(pl.multiple_of(first + step * chunk, chunk), chunk)
            out_ref[there, :] += near_ref[near_at, rows, :].astype(F32) + near_ref[
                last_at, rows, :
            ].astype(F32)

    for copy in (*lands.values(), far_top, far_low, near_top, near_low, last_top, last_low):
        copy.wait_send()


def scatter_rows(part, collective_id):
    count, width = part.shape
    half = count // 8
    return pl.pallas_call(
        sum_kernel,
        out_shape=jax.ShapeDtypeStruct((half, width), F32),
        in_specs=[pl.BlockSpec(memory_space=pl.ANY)],
        out_specs=pl.BlockSpec(memory_space=pltpu.VMEM),
        scratch_shapes=[
            pltpu.VMEM((4, half, width), BF16),
            pltpu.VMEM((4, half, width), BF16),
            pltpu.VMEM((3, half, width), BF16),
            pltpu.VMEM((6, half // 2, width), BF16),
            pltpu.SemaphoreType.DMA((2, 10)),
            pltpu.SemaphoreType.DMA((4,)),
        ],
        compiler_params=pltpu.CompilerParams(
            collective_id=collective_id, has_side_effects=True, vmem_limit_bytes=40 * 2**20
        ),
        cost_estimate=pl.CostEstimate(flops=1000, bytes_accessed=1000, transcendentals=0),
        name="scatter_rows",
    )(part)


TILE = 256
NT = (((1,), (1,)), ((), ()))
LOWEST = -1e30


def masked_tile(scores, at, tiles, shift):
    scores = scores + shift
    if at in (0, tiles - 1):
        key_at = lax.broadcasted_iota(jnp.int32, scores.shape, 0)
        query_at = lax.broadcasted_iota(jnp.int32, scores.shape, 1)
        allowed = key_at > query_at if at == 0 else key_at <= query_at
        scores = jnp.where(allowed, scores, LOWEST)
    return scores

def tile_shifts(pos_ref, start, tiles):
    return [
        jnp.where(pos_ref[0] - WINDOW + start + at * TILE >= 0, 0.0, LOWEST).astype(F32)
        for at in range(tiles)
    ]

def attend_kernel(pos_ref, q_ref, k_ref, v_ref, out_ref, log_ref, turned_ref, score_ref):
    tiles = WINDOW // TILE + 1

    @pl.when(pl.program_id(0) == 0)
    def _():
        turned_ref[...] = v_ref[...].T

    for start in range(0, q_ref.shape[0], TILE):
        shifts = tile_shifts(pos_ref, start, tiles)
        queries = q_ref[start : start + TILE, :]
        top = jnp.full((1, TILE), LOWEST, F32)
        for at in range(tiles):
            keys = k_ref[start + at * TILE : start + (at + 1) * TILE, :]
            scores = lax.dot_general(keys, queries, NT, preferred_element_type=F32)
            scores = masked_tile(scores, at, tiles, shifts[at])
            score_ref[at] = scores
            top = jnp.maximum(top, jnp.max(scores, axis=0, keepdims=True))
        total = jnp.zeros((1, TILE), F32)
        for at in range(tiles):
            expon = jnp.exp(score_ref[at] - top)
            score_ref[at] = expon
            total = total + jnp.sum(expon, axis=0, keepdims=True)
        inverse = 1.0 / total
        attended = jnp.zeros((v_ref.shape[1], TILE), F32)
        for at in range(tiles):
            probability = (score_ref[at] * inverse).astype(BF16)
            values = turned_ref[:, start + at * TILE : start + (at + 1) * TILE]
            attended = attended + jnp.dot(values, probability, preferred_element_type=F32)
        out_ref[start : start + TILE, :] = attended.T.astype(BF16)
        log_ref[0, :, start : start + TILE] = top + jnp.log(total)

def attend(first_pos, queries, key_rows, value_rows):
    rows, cols = queries.shape
    span, size = key_rows.shape
    heads = cols // size
    return pl.pallas_call(
        attend_kernel,
        out_shape=(
            jax.ShapeDtypeStruct((rows, cols), BF16),
            jax.ShapeDtypeStruct((heads, 1, rows), F32),
        ),
        grid=(heads,),
        in_specs=[
            pl.BlockSpec(memory_space=pltpu.SMEM),
            pl.BlockSpec((rows, size), lambda head: (0, head)),
            pl.BlockSpec((span, size), lambda head: (0, 0)),
            pl.BlockSpec((span, size), lambda head: (0, 0)),
        ],
        out_specs=(
            pl.BlockSpec((rows, size), lambda head: (0, head)),
            pl.BlockSpec((1, 1, rows), lambda head: (head, 0, 0)),
        ),
        scratch_shapes=[
            pltpu.VMEM((size, span), BF16),
            pltpu.VMEM((WINDOW // TILE + 1, TILE, TILE), F32),
        ],
        compiler_params=pltpu.CompilerParams(vmem_limit_bytes=40 * 2**20),
        cost_estimate=pl.CostEstimate(flops=1000, bytes_accessed=1000, transcendentals=0),
        name="attend",
    )(first_pos.reshape(1), queries, key_rows, value_rows)

def attend_back_kernel(
    pos_ref, q_ref, g_ref, k_ref, v_ref, log_ref, cos_ref, sin_ref,
    q_grad_ref, keep_ref, sent_ref, turned_ref, p_ref, gp_ref, k_grad_ref, v_grad_ref,
):
    tiles = WINDOW // TILE + 1
    size = k_ref.shape[1]

    @pl.when(pl.program_id(0) == 0)
    def _():
        turned_ref[...] = k_ref[...].T
        k_grad_ref[...] = jnp.zeros_like(k_grad_ref)
        v_grad_ref[...] = jnp.zeros_like(v_grad_ref)

    for start in range(0, q_ref.shape[0], TILE):
        shifts = tile_shifts(pos_ref, start, tiles)
        block = slice(start, start + TILE)
        queries, grads = q_ref[block, :], g_ref[block, :]
        log_total = log_ref[0, :, block]
        inner = jnp.zeros((1, TILE), F32)
        for at in range(tiles):
            span = slice(start + at * TILE, start + (at + 1) * TILE)
            scores = lax.dot_general(k_ref[span, :], queries, NT, preferred_element_type=F32)
            scores = masked_tile(scores, at, tiles, shifts[at])
            probability = jnp.exp(scores - log_total)
            grad = lax.dot_general(v_ref[span, :], grads, NT, preferred_element_type=F32)
            inner = inner + jnp.sum(probability * grad, axis=0, keepdims=True)
            p_ref[at] = probability
            gp_ref[at] = grad
        query_grad = jnp.zeros((size, TILE), F32)
        for at in range(tiles):
            span = slice(start + at * TILE, start + (at + 1) * TILE)
            probability = p_ref[at]
            score_grad = (probability * (gp_ref[at] - inner)).astype(BF16)
            k_grad_ref[span, :] += jnp.dot(score_grad, queries, preferred_element_type=F32)
            v_grad_ref[span, :] += jnp.dot(
                probability.astype(BF16), grads, preferred_element_type=F32
            )
            query_grad = query_grad + jnp.dot(
                turned_ref[:, span], score_grad, preferred_element_type=F32
            )
        query_grad = query_grad.T * size ** (-0.5)
        turn = cos_ref.shape[1]
        rotated = query_grad[:, :turn]
        rotated = (
            rotated * cos_ref[block, :] + pltpu.roll(rotated, turn // 2, 1) * sin_ref[block, :]
        )
        q_grad_ref[block, :turn] = rotated.astype(BF16)
        q_grad_ref[block, turn:] = query_grad[:, turn:].astype(BF16)

    @pl.when(pl.program_id(0) == pl.num_programs(0) - 1)
    def _():
        first = pos_ref[1] == 0
        for start in range(0, k_ref.shape[0], TILE):
            block = slice(start, start + TILE)
            k_grad, v_grad = k_grad_ref[block, :], v_grad_ref[block, :]
            keep_ref[block, :] = jnp.where(first, k_grad, v_grad)
            sent_ref[block, :] = jnp.where(first, v_grad, k_grad).astype(BF16)


def attend_back(first_pos, core, queries, grads, key_rows, value_rows, log_total, cosine, sine):
    rows, cols = queries.shape
    span, size = key_rows.shape
    heads = cols // size
    by_head = pl.BlockSpec((rows, size), lambda head: (0, head))
    whole = pl.BlockSpec((span, size), lambda head: (0, 0))
    tile_shape = (WINDOW // TILE + 1, TILE, TILE)
    return pl.pallas_call(
        attend_back_kernel,
        out_shape=(
            jax.ShapeDtypeStruct((rows, cols), BF16),
            jax.ShapeDtypeStruct((span, size), F32),
            jax.ShapeDtypeStruct((span, size), BF16),
        ),
        grid=(heads,),
        in_specs=[
            pl.BlockSpec(memory_space=pltpu.SMEM), by_head, by_head, whole, whole,
            pl.BlockSpec((1, 1, rows), lambda head: (head, 0, 0)),
            pl.BlockSpec(cosine.shape, lambda head: (0, 0)),
            pl.BlockSpec(sine.shape, lambda head: (0, 0)),
        ],
        out_specs=(by_head, whole, whole),
        scratch_shapes=[
            pltpu.VMEM((size, span), BF16),
            pltpu.VMEM(tile_shape, F32),
            pltpu.VMEM(tile_shape, F32),
            pltpu.VMEM((span, size), F32),
            pltpu.VMEM((span, size), F32),
        ],
        compiler_params=pltpu.CompilerParams(vmem_limit_bytes=48 * 2**20),
        cost_estimate=pl.CostEstimate(flops=1000, bytes_accessed=1000, transcendentals=0),
        name="attend_back",
    )(jnp.stack([first_pos, core]), queries, grads, key_rows, value_rows, log_total, cosine, sine)

def gelu_parts(gate):
    root = 0.7978845608028654
    square = gate * gate
    tanh = jnp.tanh(root * gate * (1.0 + 0.044715 * square))
    half = 0.5 * (1.0 + tanh)
    slope = half + 0.5 * gate * (1.0 - tanh * tanh) * root * (1.0 + 3 * 0.044715 * square)
    return gate * half, slope

def ffn_kernel(x_ref, w_ref, act_ref, a_ref, b_ref, total_ref):
    steps = 5
    depth = w_ref.shape[0] // steps
    total_ref[...] = jnp.dot(x_ref[:, :depth], w_ref[:depth, :], preferred_element_type=F32)
    for step in range(1, steps):
        part = slice(step * depth, (step + 1) * depth)
        total_ref[...] += jnp.dot(x_ref[:, part], w_ref[part, :], preferred_element_type=F32)
    hidden = act_ref.shape[1]
    main = hidden // 128 * 128
    for start in range(0, main, 128):
        cols = slice(start, start + 128)
        gate, up = total_ref[:, cols], total_ref[:, main + start : main + start + 128]
        gelu, slope = gelu_parts(gate)
        act_ref[:, cols] = (gelu * up).astype(BF16)
        a_ref[:, cols] = (slope * up).astype(BF16)
        b_ref[:, cols] = gelu.astype(BF16)
    last = total_ref[:, 2 * main :]
    up = pltpu.roll(last, 64, 1)
    gelu, slope = gelu_parts(last)
    act_ref[:, main:] = (gelu * up)[:, :64].astype(BF16)
    a_ref[:, main:] = (slope * up)[:, :64].astype(BF16)
    b_ref[:, main:] = gelu[:, :64].astype(BF16)

def ffn(x, w, rows=512):
    count, width = x.shape
    hidden = w.shape[1] // 2
    tile = pl.BlockSpec((rows, hidden), lambda i: (i, 0))
    return pl.pallas_call(
        ffn_kernel,
        out_shape=(jax.ShapeDtypeStruct((count, hidden), BF16),) * 3,
        grid=(count // rows,),
        in_specs=[
            pl.BlockSpec((rows, width), lambda i: (i, 0)),
            pl.BlockSpec(w.shape, lambda i: (0, 0), pipeline_mode=pl.Buffered(1)),
        ],
        out_specs=(tile,) * 3,
        scratch_shapes=[pltpu.VMEM((rows, 2 * hidden), F32)],
        compiler_params=pltpu.CompilerParams(vmem_limit_bytes=56 * 2**20),
        cost_estimate=pl.CostEstimate(flops=1000, bytes_accessed=1000, transcendentals=0),
        name="ffn",
    )(x, w)

def ffn_back_kernel(c_ref, d_ref, a_ref, b_ref, w_ref, g_ref, out_ref):
    hidden = a_ref.shape[1]
    main = hidden // 128 * 128
    act_grad = lax.dot_general(c_ref[...], d_ref[...], NT, preferred_element_type=F32)
    g_ref[:, :main] = (act_grad[:, :main] * a_ref[:, :main].astype(F32)).astype(BF16)
    g_ref[:, main : 2 * main] = (act_grad[:, :main] * b_ref[:, :main].astype(F32)).astype(BF16)
    last = act_grad[:, main:]
    g_ref[:, 2 * main :] = jnp.concatenate(
        [last * a_ref[:, main:].astype(F32), last * b_ref[:, main:].astype(F32)], axis=1
    ).astype(BF16)
    out_ref[...] = lax.dot_general(
        g_ref[...], w_ref[...], NT, preferred_element_type=F32
    ).astype(BF16)

def ffn_back(cot, down, a, b, w, rows=256):
    count, width = cot.shape
    hidden = a.shape[1]
    by_rows = lambda cols: pl.BlockSpec((rows, cols), lambda i: (i, 0))
    once = lambda v: pl.BlockSpec(v.shape, lambda i: (0, 0), pipeline_mode=pl.Buffered(1))
    return pl.pallas_call(
        ffn_back_kernel,
        out_shape=(
            jax.ShapeDtypeStruct((count, 2 * hidden), BF16),
            jax.ShapeDtypeStruct((count, width), BF16),
        ),
        grid=(count // rows,),
        in_specs=[by_rows(width), once(down), by_rows(hidden), by_rows(hidden), once(w)],
        out_specs=(by_rows(2 * hidden), by_rows(width)),
        compiler_params=pltpu.CompilerParams(vmem_limit_bytes=56 * 2**20),
        cost_estimate=pl.CostEstimate(flops=1000, bytes_accessed=1000, transcendentals=0),
        name="ffn_back",
    )(cot, down, a, b, w)


def join_kernel(seq_ref, *refs):
    pieces, (gate_w_ref, up_w_ref, gate_ref, up_ref, gain_ref) = refs[:4], refs[4:]
    hidden = pieces[0].shape[1] // 2
    main, rest = hidden // 128 * 128, hidden % 128
    for seq_at in range(4):

        @pl.when(seq_ref[0] == seq_at)
        def _():
            gain = jnp.zeros((gate_ref.shape[0], 1), F32)
            for out_ref, w_ref, spans in (
                (gate_ref, gate_w_ref, ((0, main), (2 * main, rest))),
                (up_ref, up_w_ref, ((main, main), (2 * main + rest, rest))),
            ):
                grad = jnp.concatenate(
                    [
                        pieces[at ^ seq_at][:, start : start + count].astype(F32)
                        for at in range(4)
                        for start, count in spans
                    ],
                    axis=1,
                )
                out_ref[...] = grad
                gain += jnp.sum(grad * w_ref[...].astype(F32), axis=1, keepdims=True)
            gain_ref[...] = gain


def join_columns(seq_at, pieces, w_gate, w_up):
    rows, cols = w_gate.shape
    tile = 64
    by_rows = lambda width: pl.BlockSpec((tile, width), lambda i: (i, 0))
    whole = jax.ShapeDtypeStruct((rows, cols), F32)
    gate, up, gain = pl.pallas_call(
        join_kernel,
        out_shape=(whole, whole, jax.ShapeDtypeStruct((rows, 1), F32)),
        grid=(rows // tile,),
        in_specs=[pl.BlockSpec(memory_space=pltpu.SMEM)]
        + [by_rows(pieces[0].shape[1])] * 4 + [by_rows(cols)] * 2,
        out_specs=(by_rows(cols), by_rows(cols), by_rows(1)),
        compiler_params=pltpu.CompilerParams(vmem_limit_bytes=40 * 2**20),
        cost_estimate=pl.CostEstimate(flops=1000, bytes_accessed=1000, transcendentals=0),
        name="join_columns",
    )(seq_at.reshape(1), *pieces, w_gate, w_up)
    return gate, up, gain[:, 0]


def local(
    inputs, cotangent, gain_attn, gain_ffn, w_query, w_key, w_value, w_out, w_gate, w_up, w_down
):
    rows, width = inputs.shape
    half = rows // 2
    head_size = w_key.shape[1]
    head_cols = w_query.shape[1]
    heads_here = head_cols // head_size
    seqs, shards = lax.axis_size("seq"), lax.axis_size("fsdp")
    assert rows * shards == WINDOW and lax.axis_size("tensor") == 2
    seq_at, shard_at, core = (lax.axis_index(name) for name in ("seq", "fsdp", "tensor"))
    first = core == 0
    key_span = rows + WINDOW
    first_pos = (seq_at * shards + shard_at) * rows
    scale = head_size ** (-0.5)
    rot_half = head_size // 4
    frequency = 10000.0 ** (-(jnp.arange(rot_half, dtype=F32) * 2.0) / (2 * rot_half))
    angles = (first_pos + jnp.arange(rows, dtype=jnp.int32)).astype(F32)[:, None] * frequency[None]
    cosine, sine = jnp.cos(angles), jnp.sin(angles)

    def my_half(value):
        return part_of(value, core, half, 0)

    def other_half(value):
        return part_of(value, 1 - core, half, 0)

    def whole_rows(own):
        other = swap(own)
        return jnp.where(first, jnp.stack([own, other]), jnp.stack([other, own])).reshape(
            rows, own.shape[1]
        )

    def plane_rows(own, other=None):
        near = plane_gather(own)
        far = [swap(piece) if at or other is None else other for at, piece in enumerate(near)]
        return jnp.concatenate(near + far, axis=0)

    def core_sum(partial):
        count = seqs * half
        cores = partial[:count].astype(F32) + swap(partial[count:].astype(BF16)).astype(F32)
        return [cores[j * half : (j + 1) * half] for j in range(seqs)]

    def plane_sum(partial):
        parts = core_sum(partial)
        return scatter_end(*scatter_far(parts, scatter_near(parts)))

    def order_cols(pieces):
        stacked = jnp.stack(pieces)
        return [pick(stacked, seq_at ^ at) for at in range(seqs)]

    def order_rows(pieces):
        count, width = pieces[0].shape
        rows_all = jnp.zeros((seqs * count, width), F32)
        for at, piece in enumerate(pieces):
            rows_all = lax.dynamic_update_slice_in_dim(
                rows_all, piece.astype(F32), (seq_at ^ at) * count, 0
            )
        return rows_all

    gain_one, gain_two = gain_attn.astype(F32)[:, None], gain_ffn.astype(F32)[:, None]
    gains = jnp.stack([gain_attn, gain_ffn])
    gains = jnp.stack(
        [gains]
        + [
            lax.ppermute(gains, "fsdp", [((at + by) % shards, at) for at in range(shards)])
            for by in range(1, shards)
        ]
    )
    gains = jnp.concatenate(
        [pick(gains, (at - shard_at) % shards) for at in range(shards)], axis=1
    ).astype(F32)
    pair_shard = jnp.where(first, w_key, w_value)
    proj_shard = jnp.concatenate([w_query, pair_shard], axis=1)
    proj_cols = proj_shard.shape[1] // seqs
    out_rows = head_cols // seqs
    proj_weight = lax.all_gather(
        part_of(proj_shard, seq_at, proj_cols, 1), "fsdp", axis=0, tiled=True
    )
    hidden = w_gate.shape[1] // seqs
    kernels = hidden % 128 == 64
    main = hidden // 128 * 128 if kernels else hidden
    gate_mine, up_mine = (part_of(value, seq_at, hidden, 1) for value in (w_gate, w_up))
    pair_in = jnp.concatenate(
        [gate_mine[:, :main], up_mine[:, :main], gate_mine[:, main:], up_mine[:, main:]], axis=1
    )
    in_weight = lax.all_gather(pair_in, "fsdp", axis=0, tiled=True)
    down_weight = lax.all_gather(
        part_of(w_down, seq_at, hidden, 0), "fsdp", axis=1, tiled=True
    )

    source = my_half(inputs).astype(F32)
    inverse_one = inverse_rms(source)
    unit_one = (source * inverse_one * gains[0]).astype(BF16)
    square = seqs == 4
    out_quarter = lax.all_gather(
        part_of(w_out, seq_at, out_rows, 0), "fsdp", axis=1, tiled=True
    )
    rows_one = gather_rows(unit_one, 1) if square else plane_rows(unit_one)
    proj = jnp.dot(rows_one, proj_weight, preferred_element_type=F32)
    rotate_first = proj_cols % (2 * rot_half) == 0
    if rotate_first:
        halves_at = jnp.where(first, jnp.arange(2), 1 - jnp.arange(2))[:, None, None]
        seqs_at = (seq_at ^ jnp.arange(seqs))[None, :, None]
        row_pos = (
            (seqs_at * shards + shard_at) * rows + halves_at * half + jnp.arange(half)[None, None]
        ).reshape(-1)
        row_angles = row_pos.astype(F32)[:, None] * frequency[None]
        units = proj_cols // (2 * rot_half)
        unit_at = seq_at * units + jnp.arange(units)
        head_units = head_cols // (2 * rot_half)
        turned = (unit_at % 2 == 0) & (first | (unit_at < head_units))
        unit_scale = jnp.where(unit_at < head_units, scale, 1.0)[None, :, None]
        turned = turned[None, :, None]
        row_cos = jnp.where(turned, jnp.cos(row_angles)[:, None], 1.0) * unit_scale
        row_sin = jnp.where(turned, jnp.sin(row_angles)[:, None], 0.0) * unit_scale
        proj = rotate(proj.reshape(-1, units, 2 * rot_half), row_cos, row_sin)
    proj = proj.astype(BF16).reshape(2 * seqs * half, proj_cols)
    if square and rotate_first:
        proj_here = trade(proj, False, 5)
    else:
        proj = proj.reshape(2, seqs, half, proj_cols)
        proj = jnp.where(first, proj, proj[::-1])
        proj_parts = [proj[:, 0].reshape(rows, proj_cols)] + [
            exchange(proj[:, at].reshape(rows, proj_cols), at) for at in range(1, seqs)
        ]
        proj_here = jnp.concatenate(order_cols(proj_parts), axis=1)
    queries = proj_here[:, :head_cols]
    pair_here = proj_here[:, head_cols:]
    if not rotate_first:
        queries = queries.reshape(rows, heads_here, head_size).astype(F32)
        queries = (rotate(queries, cosine[:, None], sine[:, None]) * scale).astype(BF16)
        queries = queries.reshape(rows, head_cols)
        pair_here = jnp.where(first, rotate(pair_here.astype(F32), cosine, sine), pair_here)
        pair_here = pair_here.astype(BF16)

    earlier = seq_shift(pair_here, 1)
    slots = [
        lax.ppermute(
            jnp.where(shard_at >= at, earlier, pair_here),
            "fsdp", [(source_at, (source_at - at) % shards) for source_at in range(shards)],
        )
        for at in range(1, shards)
    ]
    window_here = jnp.concatenate([earlier] + slots + [pair_here], axis=0)
    window_here, *out_pieces = lax.optimization_barrier((window_here, *plane_gather(out_quarter)))
    window_other = swap(window_here)
    key_rows = jnp.where(first, window_here, window_other)
    value_rows = jnp.where(first, window_other, window_here)

    out_weight = jnp.zeros((head_cols, width), BF16)
    for at, piece in enumerate(out_pieces):
        out_weight = lax.dynamic_update_slice_in_dim(
            out_weight, piece, (seq_at ^ at) * out_rows, 0
        )

    head_outputs, log_total = attend(first_pos, queries, key_rows, value_rows)

    out_part = jnp.dot(head_outputs, out_weight, preferred_element_type=F32)
    hidden_in = source + my_half(out_part) + swap(other_half(out_part))
    inverse_two = inverse_rms(hidden_in)
    unit_two = (hidden_in * inverse_two * gains[1]).astype(BF16)
    rows_two = gather_rows(unit_two, 2) if square else plane_rows(unit_two)
    cot_later = after(cotangent, out_weight)
    rows_cot = plane_rows(my_half(cot_later), other_half(cot_later))

    if kernels:
        activation, gate_factor, up_factor = ffn(rows_two, in_weight)
        down_term = rows_product(rows_cot, activation).astype(BF16)
        gate_factor, proj_later, _ = lax.optimization_barrier(
            (gate_factor, proj_weight, down_term)
        )
        grad_in, back_part = ffn_back(rows_cot, down_weight, gate_factor, up_factor, in_weight)
    else:
        in_proj = jnp.dot(rows_two, in_weight, preferred_element_type=F32)
        gate_pre, up_proj = in_proj[:, :hidden], in_proj[:, hidden:]
        activation = gated_unit(gate_pre, up_proj).astype(BF16)
        down_term = rows_product(rows_cot, activation).astype(BF16)
        grad_activation = times_transpose(rows_cot, down_weight)
        grad_gate, grad_up = jax.vjp(gated_unit, gate_pre, up_proj)[1](grad_activation)
        grad_in = jnp.concatenate([grad_gate.astype(BF16), grad_up.astype(BF16)], axis=1)
        back_part = times_transpose(grad_in, in_weight)
        proj_later = after(proj_weight, down_term)
    grad_in, proj_near = lax.optimization_barrier((grad_in, gather_near(proj_later)))
    proj_pieces = gather_far(proj_later, proj_near)
    in_term = rows_product(rows_two, grad_in).astype(BF16)
    back_part, proj_pieces, in_term = lax.optimization_barrier((back_part, proj_pieces, in_term))
    grad_unit_two = scatter_rows(back_part, 3) if square else plane_sum(back_part)
    grad_hidden = my_half(cotangent).astype(F32) + norm_pull(
        hidden_in, inverse_two, grad_unit_two * gains[1]
    )
    down_shard = lax.psum_scatter(down_term, "fsdp", scatter_dimension=0, tiled=True).T
    in_shard = lax.psum_scatter(in_term, "fsdp", scatter_dimension=0, tiled=True)

    grad_attn_out = whole_rows(grad_hidden.astype(BF16))
    out_term = rows_product(head_outputs, grad_attn_out).astype(BF16)
    grad_attn_out, down_shard, out_term = lax.optimization_barrier(
        (grad_attn_out, down_shard, out_term)
    )
    grad_heads = times_transpose(grad_attn_out, out_weight).astype(BF16)
    out_parts = [part_of(out_term, seq_at ^ at, out_rows, 0) for at in range(seqs)]
    out_near = scatter_near(out_parts)
    grad_query_proj, pair_keep, pair_sent = attend_back(
        first_pos, core, queries, grad_heads, key_rows, value_rows, log_total,
        jnp.concatenate([cosine, cosine], axis=1), jnp.concatenate([sine, -sine], axis=1),
    )
    pair_sent, down_near = lax.optimization_barrier((pair_sent, gather_near(down_shard)))
    count = seqs * half
    activation = after(activation, pair_sent)
    ffn_other = jnp.dot(activation[count:], down_weight, preferred_element_type=F32)
    ffn_other, out_near = lax.optimization_barrier((ffn_other, out_near))
    ffn_part = jnp.dot(
        after(activation[:count], ffn_other), down_weight, preferred_element_type=F32
    )
    ffn_part = (ffn_part + swap(ffn_other.astype(BF16)).astype(F32)).astype(BF16)
    ffn_cores = [ffn_part[j * half : (j + 1) * half] for j in range(seqs)]
    ffn_near = scatter_near(ffn_cores)
    pair_keep, pair_sent, _ = lax.optimization_barrier((pair_keep, pair_sent, ffn_part))
    out_sum, out_far = scatter_far(out_parts, out_near, not square)
    if square:
        down_cut = down_shard.shape[0] // 2
        extras = [*out_far, down_near[1][:down_cut], down_near[0][down_cut:]]
        own_total, out_top, out_low, down_top, down_low = return_pairs(
            pair_keep, pair_sent, extras, (2, 1, 1, 2), rows, shards, 7
        )
        out_far = [out_top, out_low]
        down_parts = [down_shard, *down_near, jnp.concatenate([down_top, down_low], axis=0)]
    else:
        pair_grads = pair_keep + swap(pair_sent).astype(F32)
        own_total = pair_grads[shards * rows :]
        earlier_total = pair_grads[:rows]
        for at in range(1, shards):
            piece = lax.ppermute(
                pair_grads[at * rows : (at + 1) * rows].astype(BF16),
                "fsdp",
                [((source_at - at) % shards, source_at) for source_at in range(shards)],
            ).astype(F32)
            own_total = own_total + jnp.where(shard_at >= at, 0.0, piece)
            earlier_total = earlier_total + jnp.where(shard_at >= at, piece, 0.0)
        own_total = own_total + seq_shift(earlier_total.astype(BF16), -1).astype(F32)
        down_parts = gather_far(down_shard, down_near)
    own_total, ffn_near = lax.optimization_barrier((own_total, ffn_near))
    grad_pair = jnp.where(first, rotate(own_total, cosine, -sine), own_total).astype(BF16)
    grad_pair, in_shard = lax.optimization_barrier((grad_pair, in_shard))
    grad_proj = jnp.concatenate([grad_query_proj, grad_pair], axis=1)
    if square:
        grad_rows = trade(grad_proj, True, 6)
    else:
        grad_parts = [part_of(grad_proj, seq_at, proj_cols, 1)] + [
            exchange(part_of(grad_proj, seq_at ^ at, proj_cols, 1), at) for at in range(1, seqs)
        ]
        grad_rows = jnp.stack(grad_parts).reshape(seqs, 2, half, proj_cols).swapaxes(0, 1)
        grad_rows = jnp.where(first, grad_rows, grad_rows[::-1])
        grad_rows = grad_rows.reshape(2 * seqs * half, proj_cols)
    proj_term = rows_product(rows_one, grad_rows).astype(BF16)

    out_sum = scatter_end(out_sum, after(out_far, proj_term))
    last_term = jnp.concatenate([proj_term, out_sum.astype(BF16).T], axis=1)
    last_sum = lax.psum_scatter(last_term, "fsdp", scatter_dimension=0, tiled=True)
    in_near = gather_near(after(in_shard, grad_rows))
    grad_proj = after(grad_proj, proj_term)
    if square:
        unit_part = unit_grads(seq_at, grad_proj, proj_pieces)
    else:
        unit_part = sum(
            times_transpose(part_of(grad_proj, seq_at ^ at, proj_cols, 1), proj_pieces[at])
            for at in range(seqs)
        )
    down_grad = order_rows(after(down_parts, grad_rows))
    ffn_sum, ffn_far = scatter_far(ffn_cores, after(ffn_near, proj_term))
    in_near, unit_part, down_grad = lax.optimization_barrier((in_near, unit_part, down_grad))
    in_parts = gather_far(in_shard, in_near)
    grad_unit_one = my_half(unit_part) + swap(other_half(unit_part))
    layer_half = (hidden_in + scatter_end(ffn_sum, ffn_far)).astype(BF16)
    grad_half = grad_hidden + norm_pull(source, inverse_one, grad_unit_one * gains[0])
    in_parts, grad_half, last_near = lax.optimization_barrier(
        (in_parts, grad_half, gather_near(last_sum))
    )
    last_parts = gather_far(last_sum, last_near)
    layer_out, grad_input = whole_rows(layer_half), whole_rows(grad_half)
    if kernels and square:
        gate_grad, up_grad, gain_two_half = join_columns(seq_at, in_parts, w_gate, w_up)
    else:
        in_parts = order_cols(in_parts)
        rest = hidden - main
        gate_grad, up_grad = (
            jnp.concatenate(
                [
                    piece[:, first_at : first_at + count]
                    for piece in in_parts
                    for first_at, count in spans
                    if count
                ],
                axis=1,
            ).astype(F32)
            for spans in (((0, main), (2 * main, rest)), ((main, main), (2 * main + rest, rest)))
        )
        gain_two_half = jnp.sum(
            gate_grad * w_gate.astype(F32) + up_grad * w_up.astype(F32), axis=1
        )
    gain_two_half = gain_two_half / gain_two[:, 0]
    last_parts = after(last_parts, gate_grad)
    out_grad = order_rows([piece[:, proj_cols:].T for piece in last_parts])
    proj_grad = jnp.concatenate(
        order_cols([piece[:, :proj_cols] for piece in last_parts]), axis=1
    ).astype(F32)
    gain_one_half = jnp.sum(proj_grad * proj_shard.astype(F32), axis=1) / gain_one[:, 0]
    query_grad = proj_grad[:, :head_cols]
    pair_grad = proj_grad[:, head_cols:]
    pair_other = swap(pair_grad)
    gain_grads = jnp.stack([gain_one_half, gain_two_half])
    gain_grads = gain_grads + swap(gain_grads)
    return (
        layer_out,
        grad_input,
        gain_grads[0],
        gain_grads[1],
        query_grad,
        jnp.where(first, pair_grad, pair_other),
        jnp.where(first, pair_other, pair_grad),
        out_grad,
        gate_grad,
        up_grad,
        down_grad,
    )


def solution(mesh):
    rows = P(("seq", "fsdp"), None)
    specs = (
        P("fsdp"),
        P("fsdp"),
        P("fsdp", "tensor"),
        P("fsdp", None),
        P("fsdp", None),
        P("tensor", "fsdp"),
        P("fsdp", "tensor"),
        P("fsdp", "tensor"),
        P("tensor", "fsdp"),
    )
    return jax.shard_map(
        local, mesh=mesh, in_specs=(rows, rows) + specs, out_specs=(rows, rows) + specs,
        check_vma=False,
    )
```

```python
import functools

import jax
import jax.numpy as jnp
from jax import lax
from jax.experimental import pallas as pl
from jax.experimental.pallas import tpu as pltpu
from jax.sharding import PartitionSpec as P

WINDOW = 2048
EPSILON = 1e-06
F32 = jnp.float32
BF16 = jnp.bfloat16


def exchange(value, step):
    count = lax.axis_size("seq")
    return lax.ppermute(value, "seq", [(at, at ^ step) for at in range(count)])


def swap(value):
    return lax.ppermute(value, "tensor", [(0, 1), (1, 0)])


def seq_shift(value, steps):
    count = lax.axis_size("seq")
    leading, last = (max(0, -steps), min(count, count - steps))
    return lax.ppermute(value, "seq", [(at, at + steps) for at in range(leading, last)])


def gather_near(value):
    count = lax.axis_size("seq")
    steps = (1, 2) if count == 4 else range(1, count)
    return [exchange(value, step) for step in steps]


def gather_far(value, near):
    if lax.axis_size("seq") != 4:
        return [value, *near]
    half = value.shape[0] // 2
    far = jnp.concatenate([exchange(near[1][:half], 1), exchange(near[0][half:], 2)], axis=0)
    return [value, *near, far]


def plane_gather(value):
    return gather_far(value, gather_near(value))


def scatter_near(parts):
    if len(parts) != 4:
        return [exchange(part.astype(BF16), step) for step, part in enumerate(parts[1:], 1)]
    cut = parts[0].shape[0] // 2
    by_one = jnp.concatenate([parts[1][:cut], parts[3][:cut]]).astype(BF16)
    by_two = jnp.concatenate([parts[2][cut:], parts[3][cut:]]).astype(BF16)
    return [exchange(by_one, 1), exchange(by_two, 2)]


def scatter_far(parts, near, send_on=True):
    if len(parts) != 4:
        return sum((part.astype(F32) for part in near), parts[0].astype(F32)), []
    cut = parts[0].shape[0] // 2
    by_one, by_two = near
    last_top = (parts[2][:cut].astype(F32) + by_one[cut:].astype(F32)).astype(BF16)
    last_low = (parts[1][cut:].astype(F32) + by_two[cut:].astype(F32)).astype(BF16)
    total = parts[0].astype(F32) + jnp.concatenate([by_one[:cut], by_two[:cut]]).astype(F32)
    if not send_on:
        return total, [last_top, last_low]
    return total, [exchange(last_top, 2), exchange(last_low, 1)]


def scatter_end(total, far):
    return total + jnp.concatenate(far).astype(F32) if far else total


def times_transpose(left, right):
    return lax.dot_general(left, right, (((1,), (1,)), ((), ())), preferred_element_type=F32)


def rows_product(left, right):
    return lax.dot_general(left, right, (((0,), (0,)), ((), ())), preferred_element_type=F32)


def rotate(values, cosine, sine):
    half = cosine.shape[-1]
    first_part = values[..., :half]
    second_part = values[..., half : 2 * half]
    return jnp.concatenate(
        [
            first_part * cosine - second_part * sine,
            second_part * cosine + first_part * sine,
            values[..., 2 * half :],
        ],
        axis=-1,
    )


def inverse_rms(values):
    return lax.rsqrt(jnp.mean(values * values, axis=-1, keepdims=True) + EPSILON)


def norm_pull(values, inverse, grad):
    unit = values * inverse
    return inverse * (grad - unit * jnp.mean(grad * unit, axis=-1, keepdims=True))


def gated_unit(gate_pre, up_proj):
    return jax.nn.gelu(gate_pre) * up_proj


def pick(stacked, at):
    return lax.dynamic_index_in_dim(stacked, at, 0, keepdims=False)


def after(value, *others):
    return lax.optimization_barrier((value, *others))[0]


def part_of(value, at, size, axis):
    return lax.dynamic_slice_in_dim(value, at * size, size, axis)


MESH = pl.DeviceIdType.MESH


def greet(partners):
    barrier = pltpu.get_barrier_semaphore()
    for partner in partners:
        pl.semaphore_signal(barrier, inc=1, device_id=partner, device_id_type=MESH)
    pl.semaphore_wait(barrier, len(partners))


def plane_partners():
    seq_at, core = lax.axis_index("seq"), lax.axis_index("tensor")
    return {"seq": seq_at ^ 1}, {"seq": seq_at ^ 2}, {"tensor": 1 - core}


def send(source, target, sems, at, partner):
    copy = pltpu.make_async_remote_copy(
        src_ref=source, dst_ref=target, send_sem=sems.at[0, at], recv_sem=sems.at[1, at],
        device_id=partner, device_id_type=MESH,
    )
    copy.start()
    return copy


def rows_kernel(own_ref, out_ref, sems, local_sem):
    half = own_ref.shape[0]
    one, two, core = plane_partners()
    greet((one, two, core))

    def block(at, first=0, count=half):
        return out_ref.at[pl.ds(at * half + first, count), :]

    here = pltpu.make_async_copy(own_ref, block(0), local_sem)
    here.start()
    from_one = send(own_ref, block(1), sems, 0, one)
    from_two = send(own_ref, block(2), sems, 1, two)
    copies = [from_one, from_two, send(own_ref, block(4), sems, 2, core)]
    cut = half // 2
    from_one.wait_recv()
    far_low = send(block(1, cut, cut), block(3, cut, cut), sems, 3, two)
    copies.append(send(block(1), block(5), sems, 4, core))
    from_two.wait_recv()
    far_top = send(block(2, 0, cut), block(3, 0, cut), sems, 5, one)
    copies.append(send(block(2), block(6), sems, 6, core))
    far_low.wait_recv()
    far_top.wait_recv()
    copies.append(send(block(3), block(7), sems, 7, core))
    for copy in copies[2:]:
        copy.wait_recv()
    for copy in copies + [far_low, far_top]:
        copy.wait_send()
    here.wait()


def gather_rows(own, collective_id):
    half, width = own.shape
    return pl.pallas_call(
        rows_kernel,
        out_shape=jax.ShapeDtypeStruct((8 * half, width), own.dtype),
        in_specs=[pl.BlockSpec(memory_space=pl.ANY)],
        out_specs=pl.BlockSpec(memory_space=pl.ANY),
        scratch_shapes=[pltpu.SemaphoreType.DMA((2, 8)), pltpu.SemaphoreType.DMA],
        compiler_params=pltpu.CompilerParams(collective_id=collective_id, has_side_effects=True),
        cost_estimate=pl.CostEstimate(flops=1000, bytes_accessed=1000, transcendentals=0),
        name="gather_rows",
    )(own)


def unit_kernel(seq_ref, grad_ref, *refs):
    weights, out_ref = refs[:-1], refs[-1]
    cols = weights[0].shape[1]
    for at, weight_ref in enumerate(weights):
        part = pl.ds(pl.multiple_of((seq_ref[0] ^ at) * cols, 128), cols)
        term = lax.dot_general(
            grad_ref[:, part], weight_ref[...], NT, preferred_element_type=F32
        )
        if at:
            out_ref[...] += term
        else:
            out_ref[...] = term


def unit_grads(seq_at, grads, weights):
    vmem = pl.BlockSpec(memory_space=pltpu.VMEM)
    return pl.pallas_call(
        unit_kernel,
        out_shape=jax.ShapeDtypeStruct((grads.shape[0], weights[0].shape[0]), F32),
        in_specs=[pl.BlockSpec(memory_space=pltpu.SMEM), vmem] + [vmem] * len(weights),
        out_specs=vmem,
        compiler_params=pltpu.CompilerParams(vmem_limit_bytes=40 * 2**20),
        cost_estimate=pl.CostEstimate(flops=1000, bytes_accessed=1000, transcendentals=0),
        name="unit_grads",
    )(seq_at.reshape(1), grads, *weights)


def return_kernel(steps, keep_ref, sent_ref, *refs):
    extras, (out_ref, *refs) = refs[: len(steps)], refs[len(steps) :]
    extra_outs, refs = refs[: len(steps)], refs[len(steps) :]
    land_ref, pass_ref, ring_ref, early_ref, back_ref, sems, extra_sems = refs
    seqs, shards = lax.axis_size("seq"), lax.axis_size("fsdp")
    seq_at, shard_at = lax.axis_index("seq"), lax.axis_index("fsdp")
    rows = out_ref.shape[0]
    core = {"tensor": 1 - lax.axis_index("tensor")}
    behind = {"seq": lax.rem(seq_at + seqs - 1, seqs)}
    ring = [{"fsdp": lax.rem(shard_at + at, shards)} for at in range(1, shards)]
    greet([core, *({"seq": seq_at ^ step} for step in range(1, 4)), *ring])
    slots = [pl.ds(at * rows, rows) for at in range(shards + 1)]
    lands = {
        at: send(sent_ref.at[slots[at], :], land_ref.at[slots[at], :], sems, at, core)
        for at in (*range(1, shards), 0, shards)
    }

    traded = [
        send(source, target, extra_sems, at, {"seq": seq_at ^ step})
        for at, (source, target, step) in enumerate(zip(extras, extra_outs, steps))
    ]

    def chip_sum(at):
        lands[at].wait_recv()
        return keep_ref[slots[at], :] + land_ref[slots[at], :].astype(F32)

    rings = []
    for at in range(1, shards):
        pass_ref[at - 1] = chip_sum(at).astype(BF16)
        rings.append(send(pass_ref.at[at - 1], ring_ref.at[at - 1], sems, shards + at, ring[at - 1]))
    early, own = chip_sum(0), chip_sum(shards)
    for at, copy in enumerate(rings, 1):
        copy.wait_recv()
        piece = ring_ref[at - 1].astype(F32)
        share = jnp.where(shard_at >= at, 1.0, 0.0).astype(F32)
        early = early + piece * share
        own = own + piece * (1.0 - share)
    early_ref[...] = early.astype(BF16)
    shift = send(early_ref, back_ref, sems, 2 * shards, behind)
    shift.wait_recv()
    share = jnp.where(seq_at < seqs - 1, 1.0, 0.0).astype(F32)
    out_ref[...] = own + back_ref[...].astype(F32) * share
    for copy in (*lands.values(), *rings, shift):
        copy.wait_send()
    for copy in traded:
        copy.wait()


def return_pairs(keep, sent, extras, steps, rows, shards, collective_id):
    size = keep.shape[1]
    any_place = [pl.BlockSpec(memory_space=pl.ANY)] * len(steps)
    vmem = pl.BlockSpec(memory_space=pltpu.VMEM)
    return pl.pallas_call(
        functools.partial(return_kernel, steps),
        out_shape=[jax.ShapeDtypeStruct((rows, size), F32)]
        + [jax.ShapeDtypeStruct(value.shape, value.dtype) for value in extras],
        in_specs=[vmem, vmem] + any_place,
        out_specs=[vmem] + any_place,
        scratch_shapes=[
            pltpu.VMEM(sent.shape, BF16),
            pltpu.VMEM((shards - 1, rows, size), BF16),
            pltpu.VMEM((shards - 1, rows, size), BF16),
            pltpu.VMEM((rows, size), BF16),
            pltpu.VMEM((rows, size), BF16),
            pltpu.SemaphoreType.DMA((2, 2 * shards + 1)),
            pltpu.SemaphoreType.DMA((2, len(steps))),
        ],
        compiler_params=pltpu.CompilerParams(
            collective_id=collective_id, has_side_effects=True, vmem_limit_bytes=24 * 2**20
        ),
        cost_estimate=pl.CostEstimate(flops=1000, bytes_accessed=1000, transcendentals=0),
        name="return_pairs",
    )(keep, sent, *extras)


def trade_kernel(to_rows, value_ref, out_ref, sems, local_sems):
    seq_at, core = lax.axis_index("seq"), lax.axis_index("tensor")
    plane_ref, chip_ref = (out_ref, value_ref) if to_rows else (value_ref, out_ref)
    cols, half = plane_ref.shape[1], plane_ref.shape[0] // 8
    greet([{"seq": seq_at ^ step} for step in range(1, 4)])
    copies = []
    for step in (3, 1, 2, 0):
        for at in range(2):
            plane = plane_ref.at[pl.ds((at * 4 + step) * half, half), :]
            rows = pl.ds(pl.multiple_of((core if at == 0 else 1 - core) * half, half), half)
            owner = seq_at ^ step if to_rows else seq_at
            chip = chip_ref.at[rows, pl.ds(pl.multiple_of(owner * cols, 128), cols)]
            source, target = (chip, plane) if to_rows else (plane, chip)
            if step:
                sem_at = 2 * (step - 1) + at
                copies.append(send(source, target, sems, sem_at, {"seq": seq_at ^ step}))
            else:
                here = pltpu.make_async_copy(source, target, local_sems.at[at])
                here.start()
                copies.append(here)
    for copy in copies:
        copy.wait()


def trade(value, to_rows, collective_id):
    rows, cols = value.shape
    return pl.pallas_call(
        functools.partial(trade_kernel, to_rows),
        out_shape=jax.ShapeDtypeStruct(
            (rows * 4, cols // 4) if to_rows else (rows // 4, cols * 4), value.dtype
        ),
        in_specs=[pl.BlockSpec(memory_space=pl.ANY)],
        out_specs=pl.BlockSpec(memory_space=pl.ANY),
        scratch_shapes=[pltpu.SemaphoreType.DMA((2, 6)), pltpu.SemaphoreType.DMA((2,))],
        compiler_params=pltpu.CompilerParams(collective_id=collective_id, has_side_effects=True),
        cost_estimate=pl.CostEstimate(flops=1000, bytes_accessed=1000, transcendentals=0),
        name="trade",
    )(value)


def sum_kernel(
    part_ref, out_ref, own_ref, land_ref, total_ref, near_ref, sems, local_sems
):
    half = out_ref.shape[0]
    cut = half // 2
    chunk = 32
    one, two, core = plane_partners()
    greet((one, two, core))
    order = (3, 1, 2, 0)
    loads, lands = {}, {}
    for at in order:
        loads[at] = pltpu.make_async_copy(
            part_ref.at[pl.ds(at * half, half), :], own_ref.at[at], local_sems.at[at]
        )
        loads[at].start()
        lands[at] = send(
            part_ref.at[pl.ds((4 + at) * half, half), :], land_ref.at[at], sems, at, core
        )
    sent = []
    for at in order:
        loads[at].wait()
        lands[at].wait_recv()

        @pl.loop(0, half // chunk)
        def _(step):
            rows = pl.ds(pl.multiple_of(step * chunk, chunk), chunk)
            value = own_ref[at, rows, :].astype(F32) + land_ref[at, rows, :].astype(F32)
            if at:
                total_ref[at - 1, rows, :] = value.astype(BF16)
            else:
                out_ref[rows, :] = value

        top, low = (total_ref.at[at - 1, pl.ds(first, cut), :] for first in (0, cut))
        if at == 3:
            far_top = send(top, near_ref.at[1], sems, 4, one)
            far_low = send(low, near_ref.at[3], sems, 5, two)
        if at == 1:
            near_top = send(top, near_ref.at[0], sems, 6, one)
        if at == 2:
            near_low = send(low, near_ref.at[2], sems, 7, two)

    def add_in(at, first, from_at):
        @pl.loop(0, cut // chunk)
        def _(step):
            rows = pl.ds(pl.multiple_of(step * chunk, chunk), chunk)
            there = pl.ds(pl.multiple_of(first + step * chunk, chunk), chunk)
            value = total_ref[at, there, :].astype(F32) + near_ref[from_at, rows, :].astype(F32)
            total_ref[at, there, :] = value.astype(BF16)

    far_top.wait_recv()
    add_in(1, 0, 1)
    last_top = send(total_ref.at[1, pl.ds(0, cut), :], near_ref.at[4], sems, 8, two)
    far_low.wait_recv()
    add_in(0, cut, 3)
    last_low = send(total_ref.at[0, pl.ds(cut, cut), :], near_ref.at[5], sems, 9, one)

    for first, near, last, near_at, last_at in (
        (0, near_top, last_top, 0, 4), (cut, near_low, last_low, 2, 5),
    ):
        near.wait_recv()
        last.wait_recv()

        @pl.loop(0, cut // chunk)
        def _(step):
            rows = pl.ds(pl.multiple_of(step * chunk, chunk), chunk)
            there = pl.ds(pl.multiple_of(first + step * chunk, chunk), chunk)
            out_ref[there, :] += near_ref[near_at, rows, :].astype(F32) + near_ref[
                last_at, rows, :
            ].astype(F32)

    for copy in (*lands.values(), far_top, far_low, near_top, near_low, last_top, last_low):
        copy.wait_send()


def scatter_rows(part, collective_id):
    count, width = part.shape
    half = count // 8
    return pl.pallas_call(
        sum_kernel,
        out_shape=jax.ShapeDtypeStruct((half, width), F32),
        in_specs=[pl.BlockSpec(memory_space=pl.ANY)],
        out_specs=pl.BlockSpec(memory_space=pltpu.VMEM),
        scratch_shapes=[
            pltpu.VMEM((4, half, width), BF16),
            pltpu.VMEM((4, half, width), BF16),
            pltpu.VMEM((3, half, width), BF16),
            pltpu.VMEM((6, half // 2, width), BF16),
            pltpu.SemaphoreType.DMA((2, 10)),
            pltpu.SemaphoreType.DMA((4,)),
        ],
        compiler_params=pltpu.CompilerParams(
            collective_id=collective_id, has_side_effects=True, vmem_limit_bytes=40 * 2**20
        ),
        cost_estimate=pl.CostEstimate(flops=1000, bytes_accessed=1000, transcendentals=0),
        name="scatter_rows",
    )(part)


TILE = 256
NT = (((1,), (1,)), ((), ()))
LOWEST = -1e30


def masked_tile(scores, at, tiles, shift):
    scores = scores + shift
    if at in (0, tiles - 1):
        key_at = lax.broadcasted_iota(jnp.int32, scores.shape, 0)
        query_at = lax.broadcasted_iota(jnp.int32, scores.shape, 1)
        allowed = key_at > query_at if at == 0 else key_at <= query_at
        scores = jnp.where(allowed, scores, LOWEST)
    return scores

def tile_shifts(pos_ref, start, tiles):
    return [
        jnp.where(pos_ref[0] - WINDOW + start + at * TILE >= 0, 0.0, LOWEST).astype(F32)
        for at in range(tiles)
    ]

def attend_kernel(pos_ref, q_ref, k_ref, v_ref, out_ref, log_ref, turned_ref, score_ref):
    tiles = WINDOW // TILE + 1

    @pl.when(pl.program_id(0) == 0)
    def _():
        turned_ref[...] = v_ref[...].T

    for start in range(0, q_ref.shape[0], TILE):
        shifts = tile_shifts(pos_ref, start, tiles)
        queries = q_ref[start : start + TILE, :]
        top = jnp.full((1, TILE), LOWEST, F32)
        for at in range(tiles):
            keys = k_ref[start + at * TILE : start + (at + 1) * TILE, :]
            scores = lax.dot_general(keys, queries, NT, preferred_element_type=F32)
            scores = masked_tile(scores, at, tiles, shifts[at])
            score_ref[at] = scores
            top = jnp.maximum(top, jnp.max(scores, axis=0, keepdims=True))
        total = jnp.zeros((1, TILE), F32)
        for at in range(tiles):
            expon = jnp.exp(score_ref[at] - top)
            score_ref[at] = expon
            total = total + jnp.sum(expon, axis=0, keepdims=True)
        inverse = 1.0 / total
        attended = jnp.zeros((v_ref.shape[1], TILE), F32)
        for at in range(tiles):
            probability = (score_ref[at] * inverse).astype(BF16)
            values = turned_ref[:, start + at * TILE : start + (at + 1) * TILE]
            attended = attended + jnp.dot(values, probability, preferred_element_type=F32)
        out_ref[start : start + TILE, :] = attended.T.astype(BF16)
        log_ref[0, :, start : start + TILE] = top + jnp.log(total)

def attend(first_pos, queries, key_rows, value_rows):
    rows, cols = queries.shape
    span, size = key_rows.shape
    heads = cols // size
    return pl.pallas_call(
        attend_kernel,
        out_shape=(
            jax.ShapeDtypeStruct((rows, cols), BF16),
            jax.ShapeDtypeStruct((heads, 1, rows), F32),
        ),
        grid=(heads,),
        in_specs=[
            pl.BlockSpec(memory_space=pltpu.SMEM),
            pl.BlockSpec((rows, size), lambda head: (0, head)),
            pl.BlockSpec((span, size), lambda head: (0, 0)),
            pl.BlockSpec((span, size), lambda head: (0, 0)),
        ],
        out_specs=(
            pl.BlockSpec((rows, size), lambda head: (0, head)),
            pl.BlockSpec((1, 1, rows), lambda head: (head, 0, 0)),
        ),
        scratch_shapes=[
            pltpu.VMEM((size, span), BF16),
            pltpu.VMEM((WINDOW // TILE + 1, TILE, TILE), F32),
        ],
        compiler_params=pltpu.CompilerParams(vmem_limit_bytes=40 * 2**20),
        cost_estimate=pl.CostEstimate(flops=1000, bytes_accessed=1000, transcendentals=0),
        name="attend",
    )(first_pos.reshape(1), queries, key_rows, value_rows)

def attend_back_kernel(
    pos_ref, q_ref, g_ref, k_ref, v_ref, log_ref, cos_ref, sin_ref,
    q_grad_ref, keep_ref, sent_ref, turned_ref, p_ref, gp_ref, k_grad_ref, v_grad_ref,
):
    tiles = WINDOW // TILE + 1
    size = k_ref.shape[1]

    @pl.when(pl.program_id(0) == 0)
    def _():
        turned_ref[...] = k_ref[...].T
        k_grad_ref[...] = jnp.zeros_like(k_grad_ref)
        v_grad_ref[...] = jnp.zeros_like(v_grad_ref)

    for start in range(0, q_ref.shape[0], TILE):
        shifts = tile_shifts(pos_ref, start, tiles)
        block = slice(start, start + TILE)
        queries, grads = q_ref[block, :], g_ref[block, :]
        log_total = log_ref[0, :, block]
        inner = jnp.zeros((1, TILE), F32)
        for at in range(tiles):
            span = slice(start + at * TILE, start + (at + 1) * TILE)
            scores = lax.dot_general(k_ref[span, :], queries, NT, preferred_element_type=F32)
            scores = masked_tile(scores, at, tiles, shifts[at])
            probability = jnp.exp(scores - log_total)
            grad = lax.dot_general(v_ref[span, :], grads, NT, preferred_element_type=F32)
            inner = inner + jnp.sum(probability * grad, axis=0, keepdims=True)
            p_ref[at] = probability
            gp_ref[at] = grad
        query_grad = jnp.zeros((size, TILE), F32)
        for at in range(tiles):
            span = slice(start + at * TILE, start + (at + 1) * TILE)
            probability = p_ref[at]
            score_grad = (probability * (gp_ref[at] - inner)).astype(BF16)
            k_grad_ref[span, :] += jnp.dot(score_grad, queries, preferred_element_type=F32)
            v_grad_ref[span, :] += jnp.dot(
                probability.astype(BF16), grads, preferred_element_type=F32
            )
            query_grad = query_grad + jnp.dot(
                turned_ref[:, span], score_grad, preferred_element_type=F32
            )
        query_grad = query_grad.T * size ** (-0.5)
        turn = cos_ref.shape[1]
        rotated = query_grad[:, :turn]
        rotated = (
            rotated * cos_ref[block, :] + pltpu.roll(rotated, turn // 2, 1) * sin_ref[block, :]
        )
        q_grad_ref[block, :turn] = rotated.astype(BF16)
        q_grad_ref[block, turn:] = query_grad[:, turn:].astype(BF16)

    @pl.when(pl.program_id(0) == pl.num_programs(0) - 1)
    def _():
        first = pos_ref[1] == 0
        for start in range(0, k_ref.shape[0], TILE):
            block = slice(start, start + TILE)
            k_grad, v_grad = k_grad_ref[block, :], v_grad_ref[block, :]
            keep_ref[block, :] = jnp.where(first, k_grad, v_grad)
            sent_ref[block, :] = jnp.where(first, v_grad, k_grad).astype(BF16)


def attend_back(first_pos, core, queries, grads, key_rows, value_rows, log_total, cosine, sine):
    rows, cols = queries.shape
    span, size = key_rows.shape
    heads = cols // size
    by_head = pl.BlockSpec((rows, size), lambda head: (0, head))
    whole = pl.BlockSpec((span, size), lambda head: (0, 0))
    tile_shape = (WINDOW // TILE + 1, TILE, TILE)
    return pl.pallas_call(
        attend_back_kernel,
        out_shape=(
            jax.ShapeDtypeStruct((rows, cols), BF16),
            jax.ShapeDtypeStruct((span, size), F32),
            jax.ShapeDtypeStruct((span, size), BF16),
        ),
        grid=(heads,),
        in_specs=[
            pl.BlockSpec(memory_space=pltpu.SMEM), by_head, by_head, whole, whole,
            pl.BlockSpec((1, 1, rows), lambda head: (head, 0, 0)),
            pl.BlockSpec(cosine.shape, lambda head: (0, 0)),
            pl.BlockSpec(sine.shape, lambda head: (0, 0)),
        ],
        out_specs=(by_head, whole, whole),
        scratch_shapes=[
            pltpu.VMEM((size, span), BF16),
            pltpu.VMEM(tile_shape, F32),
            pltpu.VMEM(tile_shape, F32),
            pltpu.VMEM((span, size), F32),
            pltpu.VMEM((span, size), F32),
        ],
        compiler_params=pltpu.CompilerParams(vmem_limit_bytes=48 * 2**20),
        cost_estimate=pl.CostEstimate(flops=1000, bytes_accessed=1000, transcendentals=0),
        name="attend_back",
    )(jnp.stack([first_pos, core]), queries, grads, key_rows, value_rows, log_total, cosine, sine)

def gelu_parts(gate):
    root = 0.7978845608028654
    square = gate * gate
    tanh = jnp.tanh(root * gate * (1.0 + 0.044715 * square))
    half = 0.5 * (1.0 + tanh)
    slope = half + 0.5 * gate * (1.0 - tanh * tanh) * root * (1.0 + 3 * 0.044715 * square)
    return gate * half, slope

def ffn_kernel(x_ref, w_ref, act_ref, a_ref, b_ref, total_ref):
    steps = 5
    depth = w_ref.shape[0] // steps
    total_ref[...] = jnp.dot(x_ref[:, :depth], w_ref[:depth, :], preferred_element_type=F32)
    for step in range(1, steps):
        part = slice(step * depth, (step + 1) * depth)
        total_ref[...] += jnp.dot(x_ref[:, part], w_ref[part, :], preferred_element_type=F32)
    hidden = act_ref.shape[1]
    main = hidden // 128 * 128
    for start in range(0, main, 128):
        cols = slice(start, start + 128)
        gate, up = total_ref[:, cols], total_ref[:, main + start : main + start + 128]
        gelu, slope = gelu_parts(gate)
        act_ref[:, cols] = (gelu * up).astype(BF16)
        a_ref[:, cols] = (slope * up).astype(BF16)
        b_ref[:, cols] = gelu.astype(BF16)
    last = total_ref[:, 2 * main :]
    up = pltpu.roll(last, 64, 1)
    gelu, slope = gelu_parts(last)
    act_ref[:, main:] = (gelu * up)[:, :64].astype(BF16)
    a_ref[:, main:] = (slope * up)[:, :64].astype(BF16)
    b_ref[:, main:] = gelu[:, :64].astype(BF16)

def ffn(x, w, rows=512):
    count, width = x.shape
    hidden = w.shape[1] // 2
    tile = pl.BlockSpec((rows, hidden), lambda i: (i, 0))
    return pl.pallas_call(
        ffn_kernel,
        out_shape=(jax.ShapeDtypeStruct((count, hidden), BF16),) * 3,
        grid=(count // rows,),
        in_specs=[
            pl.BlockSpec((rows, width), lambda i: (i, 0)),
            pl.BlockSpec(w.shape, lambda i: (0, 0), pipeline_mode=pl.Buffered(1)),
        ],
        out_specs=(tile,) * 3,
        scratch_shapes=[pltpu.VMEM((rows, 2 * hidden), F32)],
        compiler_params=pltpu.CompilerParams(vmem_limit_bytes=56 * 2**20),
        cost_estimate=pl.CostEstimate(flops=1000, bytes_accessed=1000, transcendentals=0),
        name="ffn",
    )(x, w)

def ffn_back_kernel(c_ref, d_ref, a_ref, b_ref, w_ref, g_ref, out_ref):
    hidden = a_ref.shape[1]
    main = hidden // 128 * 128
    act_grad = lax.dot_general(c_ref[...], d_ref[...], NT, preferred_element_type=F32)
    g_ref[:, :main] = (act_grad[:, :main] * a_ref[:, :main].astype(F32)).astype(BF16)
    g_ref[:, main : 2 * main] = (act_grad[:, :main] * b_ref[:, :main].astype(F32)).astype(BF16)
    last = act_grad[:, main:]
    g_ref[:, 2 * main :] = jnp.concatenate(
        [last * a_ref[:, main:].astype(F32), last * b_ref[:, main:].astype(F32)], axis=1
    ).astype(BF16)
    out_ref[...] = lax.dot_general(
        g_ref[...], w_ref[...], NT, preferred_element_type=F32
    ).astype(BF16)

def ffn_back(cot, down, a, b, w, rows=256):
    count, width = cot.shape
    hidden = a.shape[1]
    by_rows = lambda cols: pl.BlockSpec((rows, cols), lambda i: (i, 0))
    once = lambda v: pl.BlockSpec(v.shape, lambda i: (0, 0), pipeline_mode=pl.Buffered(1))
    return pl.pallas_call(
        ffn_back_kernel,
        out_shape=(
            jax.ShapeDtypeStruct((count, 2 * hidden), BF16),
            jax.ShapeDtypeStruct((count, width), BF16),
        ),
        grid=(count // rows,),
        in_specs=[by_rows(width), once(down), by_rows(hidden), by_rows(hidden), once(w)],
        out_specs=(by_rows(2 * hidden), by_rows(width)),
        compiler_params=pltpu.CompilerParams(vmem_limit_bytes=56 * 2**20),
        cost_estimate=pl.CostEstimate(flops=1000, bytes_accessed=1000, transcendentals=0),
        name="ffn_back",
    )(cot, down, a, b, w)


def join_kernel(seq_ref, *refs):
    pieces, (gate_w_ref, up_w_ref, gate_ref, up_ref, gain_ref) = refs[:4], refs[4:]
    hidden = pieces[0].shape[1] // 2
    main, rest = hidden // 128 * 128, hidden % 128
    for seq_at in range(4):

        @pl.when(seq_ref[0] == seq_at)
        def _():
            gain = jnp.zeros((gate_ref.shape[0], 1), F32)
            for out_ref, w_ref, spans in (
                (gate_ref, gate_w_ref, ((0, main), (2 * main, rest))),
                (up_ref, up_w_ref, ((main, main), (2 * main + rest, rest))),
            ):
                grad = jnp.concatenate(
                    [
                        pieces[at ^ seq_at][:, start : start + count].astype(F32)
                        for at in range(4)
                        for start, count in spans
                    ],
                    axis=1,
                )
                out_ref[...] = grad
                gain += jnp.sum(grad * w_ref[...].astype(F32), axis=1, keepdims=True)
            gain_ref[...] = gain


def join_columns(seq_at, pieces, w_gate, w_up):
    rows, cols = w_gate.shape
    tile = 64
    by_rows = lambda width: pl.BlockSpec((tile, width), lambda i: (i, 0))
    whole = jax.ShapeDtypeStruct((rows, cols), F32)
    gate, up, gain = pl.pallas_call(
        join_kernel,
        out_shape=(whole, whole, jax.ShapeDtypeStruct((rows, 1), F32)),
        grid=(rows // tile,),
        in_specs=[pl.BlockSpec(memory_space=pltpu.SMEM)]
        + [by_rows(pieces[0].shape[1])] * 4 + [by_rows(cols)] * 2,
        out_specs=(by_rows(cols), by_rows(cols), by_rows(1)),
        compiler_params=pltpu.CompilerParams(vmem_limit_bytes=40 * 2**20),
        cost_estimate=pl.CostEstimate(flops=1000, bytes_accessed=1000, transcendentals=0),
        name="join_columns",
    )(seq_at.reshape(1), *pieces, w_gate, w_up)
    return gate, up, gain[:, 0]


def local(
    inputs, cotangent, gain_attn, gain_ffn, w_query, w_key, w_value, w_out, w_gate, w_up, w_down
):
    rows, width = inputs.shape
    half = rows // 2
    head_size = w_key.shape[1]
    head_cols = w_query.shape[1]
    heads_here = head_cols // head_size
    seqs, shards = lax.axis_size("seq"), lax.axis_size("fsdp")
    assert rows * shards == WINDOW and lax.axis_size("tensor") == 2
    seq_at, shard_at, core = (lax.axis_index(name) for name in ("seq", "fsdp", "tensor"))
    first = core == 0
    key_span = rows + WINDOW
    first_pos = (seq_at * shards + shard_at) * rows
    scale = head_size ** (-0.5)
    rot_half = head_size // 4
    frequency = 10000.0 ** (-(jnp.arange(rot_half, dtype=F32) * 2.0) / (2 * rot_half))
    angles = (first_pos + jnp.arange(rows, dtype=jnp.int32)).astype(F32)[:, None] * frequency[None]
    cosine, sine = jnp.cos(angles), jnp.sin(angles)

    def my_half(value):
        return part_of(value, core, half, 0)

    def other_half(value):
        return part_of(value, 1 - core, half, 0)

    def whole_rows(own):
        other = swap(own)
        return jnp.where(first, jnp.stack([own, other]), jnp.stack([other, own])).reshape(
            rows, own.shape[1]
        )

    def plane_rows(own, other=None):
        near = plane_gather(own)
        far = [swap(piece) if at or other is None else other for at, piece in enumerate(near)]
        return jnp.concatenate(near + far, axis=0)

    def core_sum(partial):
        count = seqs * half
        cores = partial[:count].astype(F32) + swap(partial[count:].astype(BF16)).astype(F32)
        return [cores[j * half : (j + 1) * half] for j in range(seqs)]

    def plane_sum(partial):
        parts = core_sum(partial)
        return scatter_end(*scatter_far(parts, scatter_near(parts)))

    def order_cols(pieces):
        stacked = jnp.stack(pieces)
        return [pick(stacked, seq_at ^ at) for at in range(seqs)]

    def order_rows(pieces):
        count, width = pieces[0].shape
        rows_all = jnp.zeros((seqs * count, width), F32)
        for at, piece in enumerate(pieces):
            rows_all = lax.dynamic_update_slice_in_dim(
                rows_all, piece.astype(F32), (seq_at ^ at) * count, 0
            )
        return rows_all

    gain_one, gain_two = gain_attn.astype(F32)[:, None], gain_ffn.astype(F32)[:, None]
    gains = jnp.stack([gain_attn, gain_ffn])
    gains = jnp.stack(
        [gains]
        + [
            lax.ppermute(gains, "fsdp", [((at + by) % shards, at) for at in range(shards)])
            for by in range(1, shards)
        ]
    )
    gains = jnp.concatenate(
        [pick(gains, (at - shard_at) % shards) for at in range(shards)], axis=1
    ).astype(F32)
    pair_shard = jnp.where(first, w_key, w_value)
    proj_shard = jnp.concatenate([w_query, pair_shard], axis=1)
    proj_cols = proj_shard.shape[1] // seqs
    out_rows = head_cols // seqs
    proj_weight = lax.all_gather(
        part_of(proj_shard, seq_at, proj_cols, 1), "fsdp", axis=0, tiled=True
    )
    hidden = w_gate.shape[1] // seqs
    kernels = hidden % 128 == 64
    main = hidden // 128 * 128 if kernels else hidden
    gate_mine, up_mine = (part_of(value, seq_at, hidden, 1) for value in (w_gate, w_up))
    pair_in = jnp.concatenate(
        [gate_mine[:, :main], up_mine[:, :main], gate_mine[:, main:], up_mine[:, main:]], axis=1
    )
    in_weight = lax.all_gather(pair_in, "fsdp", axis=0, tiled=True)
    down_weight = lax.all_gather(
        part_of(w_down, seq_at, hidden, 0), "fsdp", axis=1, tiled=True
    )

    source = my_half(inputs).astype(F32)
    inverse_one = inverse_rms(source)
    unit_one = (source * inverse_one * gains[0]).astype(BF16)
    square = seqs == 4
    out_quarter = lax.all_gather(
        part_of(w_out, seq_at, out_rows, 0), "fsdp", axis=1, tiled=True
    )
    rows_one = gather_rows(unit_one, 1) if square else plane_rows(unit_one)
    proj = jnp.dot(rows_one, proj_weight, preferred_element_type=F32)
    rotate_first = proj_cols % (2 * rot_half) == 0
    if rotate_first:
        halves_at = jnp.where(first, jnp.arange(2), 1 - jnp.arange(2))[:, None, None]
        seqs_at = (seq_at ^ jnp.arange(seqs))[None, :, None]
        row_pos = (
            (seqs_at * shards + shard_at) * rows + halves_at * half + jnp.arange(half)[None, None]
        ).reshape(-1)
        row_angles = row_pos.astype(F32)[:, None] * frequency[None]
        units = proj_cols // (2 * rot_half)
        unit_at = seq_at * units + jnp.arange(units)
        head_units = head_cols // (2 * rot_half)
        turned = (unit_at % 2 == 0) & (first | (unit_at < head_units))
        unit_scale = jnp.where(unit_at < head_units, scale, 1.0)[None, :, None]
        turned = turned[None, :, None]
        row_cos = jnp.where(turned, jnp.cos(row_angles)[:, None], 1.0) * unit_scale
        row_sin = jnp.where(turned, jnp.sin(row_angles)[:, None], 0.0) * unit_scale
        proj = rotate(proj.reshape(-1, units, 2 * rot_half), row_cos, row_sin)
    proj = proj.astype(BF16).reshape(2 * seqs * half, proj_cols)
    if square and rotate_first:
        proj_here = trade(proj, False, 5)
    else:
        proj = proj.reshape(2, seqs, half, proj_cols)
        proj = jnp.where(first, proj, proj[::-1])
        proj_parts = [proj[:, 0].reshape(rows, proj_cols)] + [
            exchange(proj[:, at].reshape(rows, proj_cols), at) for at in range(1, seqs)
        ]
        proj_here = jnp.concatenate(order_cols(proj_parts), axis=1)
    queries = proj_here[:, :head_cols]
    pair_here = proj_here[:, head_cols:]
    if not rotate_first:
        queries = queries.reshape(rows, heads_here, head_size).astype(F32)
        queries = (rotate(queries, cosine[:, None], sine[:, None]) * scale).astype(BF16)
        queries = queries.reshape(rows, head_cols)
        pair_here = jnp.where(first, rotate(pair_here.astype(F32), cosine, sine), pair_here)
        pair_here = pair_here.astype(BF16)

    earlier = seq_shift(pair_here, 1)
    slots = [
        lax.ppermute(
            jnp.where(shard_at >= at, earlier, pair_here),
            "fsdp", [(source_at, (source_at - at) % shards) for source_at in range(shards)],
        )
        for at in range(1, shards)
    ]
    window_here = jnp.concatenate([earlier] + slots + [pair_here], axis=0)
    window_here, *out_pieces = lax.optimization_barrier((window_here, *plane_gather(out_quarter)))
    window_other = swap(window_here)
    key_rows = jnp.where(first, window_here, window_other)
    value_rows = jnp.where(first, window_other, window_here)

    out_weight = jnp.zeros((head_cols, width), BF16)
    for at, piece in enumerate(out_pieces):
        out_weight = lax.dynamic_update_slice_in_dim(
            out_weight, piece, (seq_at ^ at) * out_rows, 0
        )

    head_outputs, log_total = attend(first_pos, queries, key_rows, value_rows)

    out_part = jnp.dot(head_outputs, out_weight, preferred_element_type=F32)
    hidden_in = source + my_half(out_part) + swap(other_half(out_part))
    inverse_two = inverse_rms(hidden_in)
    unit_two = (hidden_in * inverse_two * gains[1]).astype(BF16)
    rows_two = gather_rows(unit_two, 2) if square else plane_rows(unit_two)
    cot_later = after(cotangent, out_weight)
    rows_cot = plane_rows(my_half(cot_later), other_half(cot_later))

    if kernels:
        activation, gate_factor, up_factor = ffn(rows_two, in_weight)
        down_term = rows_product(rows_cot, activation).astype(BF16)
        gate_factor, proj_later, _ = lax.optimization_barrier(
            (gate_factor, proj_weight, down_term)
        )
        grad_in, back_part = ffn_back(rows_cot, down_weight, gate_factor, up_factor, in_weight)
    else:
        in_proj = jnp.dot(rows_two, in_weight, preferred_element_type=F32)
        gate_pre, up_proj = in_proj[:, :hidden], in_proj[:, hidden:]
        activation = gated_unit(gate_pre, up_proj).astype(BF16)
        down_term = rows_product(rows_cot, activation).astype(BF16)
        grad_activation = times_transpose(rows_cot, down_weight)
        grad_gate, grad_up = jax.vjp(gated_unit, gate_pre, up_proj)[1](grad_activation)
        grad_in = jnp.concatenate([grad_gate.astype(BF16), grad_up.astype(BF16)], axis=1)
        back_part = times_transpose(grad_in, in_weight)
        proj_later = after(proj_weight, down_term)
    grad_in, proj_near = lax.optimization_barrier((grad_in, gather_near(proj_later)))
    proj_pieces = gather_far(proj_later, proj_near)
    in_term = rows_product(rows_two, grad_in).astype(BF16)
    back_part, proj_pieces, in_term = lax.optimization_barrier((back_part, proj_pieces, in_term))
    grad_unit_two = scatter_rows(back_part, 3) if square else plane_sum(back_part)
    grad_hidden = my_half(cotangent).astype(F32) + norm_pull(
        hidden_in, inverse_two, grad_unit_two * gains[1]
    )
    down_shard = lax.psum_scatter(down_term, "fsdp", scatter_dimension=0, tiled=True).T
    in_shard = lax.psum_scatter(in_term, "fsdp", scatter_dimension=0, tiled=True)

    grad_attn_out = whole_rows(grad_hidden.astype(BF16))
    out_term = rows_product(head_outputs, grad_attn_out).astype(BF16)
    grad_attn_out, down_shard, out_term = lax.optimization_barrier(
        (grad_attn_out, down_shard, out_term)
    )
    grad_heads = times_transpose(grad_attn_out, out_weight).astype(BF16)
    out_parts = [part_of(out_term, seq_at ^ at, out_rows, 0) for at in range(seqs)]
    out_near = scatter_near(out_parts)
    grad_query_proj, pair_keep, pair_sent = attend_back(
        first_pos, core, queries, grad_heads, key_rows, value_rows, log_total,
        jnp.concatenate([cosine, cosine], axis=1), jnp.concatenate([sine, -sine], axis=1),
    )
    pair_sent, down_near = lax.optimization_barrier((pair_sent, gather_near(down_shard)))
    count = seqs * half
    activation = after(activation, pair_sent)
    ffn_other = jnp.dot(activation[count:], down_weight, preferred_element_type=F32)
    ffn_other, out_near = lax.optimization_barrier((ffn_other, out_near))
    ffn_part = jnp.dot(
        after(activation[:count], ffn_other), down_weight, preferred_element_type=F32
    )
    ffn_part, ffn_other = lax.optimization_barrier(
        (ffn_part.astype(BF16), swap(ffn_other.astype(BF16)))
    )
    ffn_part = (ffn_part.astype(F32) + ffn_other.astype(F32)).astype(BF16)
    ffn_cores = [ffn_part[j * half : (j + 1) * half] for j in range(seqs)]
    ffn_near = scatter_near(ffn_cores)
    pair_keep, pair_sent, _ = lax.optimization_barrier((pair_keep, pair_sent, ffn_part))
    out_sum, out_far = scatter_far(out_parts, out_near, not square)
    if square:
        down_cut = down_shard.shape[0] // 2
        extras = [*out_far, down_near[1][:down_cut], down_near[0][down_cut:]]
        own_total, out_top, out_low, down_top, down_low = return_pairs(
            pair_keep, pair_sent, extras, (2, 1, 1, 2), rows, shards, 7
        )
        out_far = [out_top, out_low]
        down_parts = [down_shard, *down_near, jnp.concatenate([down_top, down_low], axis=0)]
    else:
        pair_grads = pair_keep + swap(pair_sent).astype(F32)
        own_total = pair_grads[shards * rows :]
        earlier_total = pair_grads[:rows]
        for at in range(1, shards):
            piece = lax.ppermute(
                pair_grads[at * rows : (at + 1) * rows].astype(BF16),
                "fsdp",
                [((source_at - at) % shards, source_at) for source_at in range(shards)],
            ).astype(F32)
            own_total = own_total + jnp.where(shard_at >= at, 0.0, piece)
            earlier_total = earlier_total + jnp.where(shard_at >= at, piece, 0.0)
        own_total = own_total + seq_shift(earlier_total.astype(BF16), -1).astype(F32)
        down_parts = gather_far(down_shard, down_near)
    own_total, ffn_near = lax.optimization_barrier((own_total, ffn_near))
    grad_pair = jnp.where(first, rotate(own_total, cosine, -sine), own_total).astype(BF16)
    grad_pair, in_shard = lax.optimization_barrier((grad_pair, in_shard))
    grad_proj = jnp.concatenate([grad_query_proj, grad_pair], axis=1)
    if square:
        grad_rows = trade(grad_proj, True, 6)
    else:
        grad_parts = [part_of(grad_proj, seq_at, proj_cols, 1)] + [
            exchange(part_of(grad_proj, seq_at ^ at, proj_cols, 1), at) for at in range(1, seqs)
        ]
        grad_rows = jnp.stack(grad_parts).reshape(seqs, 2, half, proj_cols).swapaxes(0, 1)
        grad_rows = jnp.where(first, grad_rows, grad_rows[::-1])
        grad_rows = grad_rows.reshape(2 * seqs * half, proj_cols)
    proj_term = rows_product(rows_one, grad_rows).astype(BF16)

    out_sum = scatter_end(out_sum, after(out_far, proj_term))
    last_term = jnp.concatenate([proj_term, out_sum.astype(BF16).T], axis=1)
    last_sum = lax.psum_scatter(last_term, "fsdp", scatter_dimension=0, tiled=True)
    in_near = gather_near(after(in_shard, grad_rows))
    grad_proj = after(grad_proj, proj_term)
    if square:
        unit_part = unit_grads(seq_at, grad_proj, proj_pieces)
    else:
        unit_part = sum(
            times_transpose(part_of(grad_proj, seq_at ^ at, proj_cols, 1), proj_pieces[at])
            for at in range(seqs)
        )
    down_grad = order_rows(after(down_parts, grad_rows))
    ffn_sum, ffn_far = scatter_far(ffn_cores, after(ffn_near, proj_term))
    in_near, unit_part, down_grad = lax.optimization_barrier((in_near, unit_part, down_grad))
    in_parts = gather_far(in_shard, in_near)
    grad_unit_one = my_half(unit_part) + swap(other_half(unit_part))
    layer_half = (hidden_in + scatter_end(ffn_sum, ffn_far)).astype(BF16)
    grad_half = grad_hidden + norm_pull(source, inverse_one, grad_unit_one * gains[0])
    in_parts, grad_half, last_near = lax.optimization_barrier(
        (in_parts, grad_half, gather_near(last_sum))
    )
    last_parts = gather_far(last_sum, last_near)
    layer_out, grad_input = whole_rows(layer_half), whole_rows(grad_half)
    if kernels and square:
        gate_grad, up_grad, gain_two_half = join_columns(seq_at, in_parts, w_gate, w_up)
    else:
        in_parts = order_cols(in_parts)
        rest = hidden - main
        gate_grad, up_grad = (
            jnp.concatenate(
                [
                    piece[:, first_at : first_at + count]
                    for piece in in_parts
                    for first_at, count in spans
                    if count
                ],
                axis=1,
            ).astype(F32)
            for spans in (((0, main), (2 * main, rest)), ((main, main), (2 * main + rest, rest)))
        )
        gain_two_half = jnp.sum(
            gate_grad * w_gate.astype(F32) + up_grad * w_up.astype(F32), axis=1
        )
    gain_two_half = gain_two_half / gain_two[:, 0]
    last_parts = after(last_parts, gate_grad)
    out_grad = order_rows([piece[:, proj_cols:].T for piece in last_parts])
    proj_grad = jnp.concatenate(
        order_cols([piece[:, :proj_cols] for piece in last_parts]), axis=1
    ).astype(F32)
    gain_one_half = jnp.sum(proj_grad * proj_shard.astype(F32), axis=1) / gain_one[:, 0]
    query_grad = proj_grad[:, :head_cols]
    pair_grad = proj_grad[:, head_cols:]
    pair_other = swap(pair_grad)
    gain_grads = jnp.stack([gain_one_half, gain_two_half])
    gain_grads = gain_grads + swap(gain_grads)
    return (
        layer_out,
        grad_input,
        gain_grads[0],
        gain_grads[1],
        query_grad,
        jnp.where(first, pair_grad, pair_other),
        jnp.where(first, pair_other, pair_grad),
        out_grad,
        gate_grad,
        up_grad,
        down_grad,
    )


def solution(mesh):
    rows = P(("seq", "fsdp"), None)
    specs = (
        P("fsdp"),
        P("fsdp"),
        P("fsdp", "tensor"),
        P("fsdp", None),
        P("fsdp", None),
        P("tensor", "fsdp"),
        P("fsdp", "tensor"),
        P("fsdp", "tensor"),
        P("tensor", "fsdp"),
    )
    return jax.shard_map(
        local, mesh=mesh, in_specs=(rows, rows) + specs, out_specs=(rows, rows) + specs,
        check_vma=False,
    )
```

```python
import functools

import jax
import jax.numpy as jnp
from jax import lax
from jax.experimental import pallas as pl
from jax.experimental.pallas import tpu as pltpu
from jax.sharding import PartitionSpec as P

WINDOW = 2048
EPSILON = 1e-06
F32 = jnp.float32
BF16 = jnp.bfloat16


def exchange(value, step):
    count = lax.axis_size("seq")
    return lax.ppermute(value, "seq", [(at, at ^ step) for at in range(count)])


def swap(value):
    return lax.ppermute(value, "tensor", [(0, 1), (1, 0)])


def seq_shift(value, steps):
    count = lax.axis_size("seq")
    leading, last = (max(0, -steps), min(count, count - steps))
    return lax.ppermute(value, "seq", [(at, at + steps) for at in range(leading, last)])


def gather_near(value):
    count = lax.axis_size("seq")
    steps = (1, 2) if count == 4 else range(1, count)
    return [exchange(value, step) for step in steps]


def gather_far(value, near):
    if lax.axis_size("seq") != 4:
        return [value, *near]
    half = value.shape[0] // 2
    far = jnp.concatenate([exchange(near[1][:half], 1), exchange(near[0][half:], 2)], axis=0)
    return [value, *near, far]


def plane_gather(value):
    return gather_far(value, gather_near(value))


def scatter_near(parts):
    if len(parts) != 4:
        return [exchange(part.astype(BF16), step) for step, part in enumerate(parts[1:], 1)]
    cut = parts[0].shape[0] // 2
    by_one = jnp.concatenate([parts[1][:cut], parts[3][:cut]]).astype(BF16)
    by_two = jnp.concatenate([parts[2][cut:], parts[3][cut:]]).astype(BF16)
    return [exchange(by_one, 1), exchange(by_two, 2)]


def scatter_far(parts, near, send_on=True):
    if len(parts) != 4:
        return sum((part.astype(F32) for part in near), parts[0].astype(F32)), []
    cut = parts[0].shape[0] // 2
    by_one, by_two = near
    last_top = (parts[2][:cut].astype(F32) + by_one[cut:].astype(F32)).astype(BF16)
    last_low = (parts[1][cut:].astype(F32) + by_two[cut:].astype(F32)).astype(BF16)
    total = parts[0].astype(F32) + jnp.concatenate([by_one[:cut], by_two[:cut]]).astype(F32)
    if not send_on:
        return total, [last_top, last_low]
    return total, [exchange(last_top, 2), exchange(last_low, 1)]


def scatter_end(total, far):
    return total + jnp.concatenate(far).astype(F32) if far else total


def times_transpose(left, right):
    return lax.dot_general(left, right, (((1,), (1,)), ((), ())), preferred_element_type=F32)


def rows_product(left, right):
    return lax.dot_general(left, right, (((0,), (0,)), ((), ())), preferred_element_type=F32)


def rotate(values, cosine, sine):
    half = cosine.shape[-1]
    first_part = values[..., :half]
    second_part = values[..., half : 2 * half]
    return jnp.concatenate(
        [
            first_part * cosine - second_part * sine,
            second_part * cosine + first_part * sine,
            values[..., 2 * half :],
        ],
        axis=-1,
    )


def inverse_rms(values):
    return lax.rsqrt(jnp.mean(values * values, axis=-1, keepdims=True) + EPSILON)


def norm_pull(values, inverse, grad):
    unit = values * inverse
    return inverse * (grad - unit * jnp.mean(grad * unit, axis=-1, keepdims=True))


def gated_unit(gate_pre, up_proj):
    return jax.nn.gelu(gate_pre) * up_proj


def pick(stacked, at):
    return lax.dynamic_index_in_dim(stacked, at, 0, keepdims=False)


def after(value, *others):
    return lax.optimization_barrier((value, *others))[0]


def part_of(value, at, size, axis):
    return lax.dynamic_slice_in_dim(value, at * size, size, axis)


MESH = pl.DeviceIdType.MESH


def greet(partners):
    barrier = pltpu.get_barrier_semaphore()
    for partner in partners:
        pl.semaphore_signal(barrier, inc=1, device_id=partner, device_id_type=MESH)
    pl.semaphore_wait(barrier, len(partners))


def plane_partners():
    seq_at, core = lax.axis_index("seq"), lax.axis_index("tensor")
    return {"seq": seq_at ^ 1}, {"seq": seq_at ^ 2}, {"tensor": 1 - core}


def send(source, target, sems, at, partner):
    copy = pltpu.make_async_remote_copy(
        src_ref=source, dst_ref=target, send_sem=sems.at[0, at], recv_sem=sems.at[1, at],
        device_id=partner, device_id_type=MESH,
    )
    copy.start()
    return copy


def rows_kernel(own_ref, out_ref, sems, local_sem):
    half = own_ref.shape[0]
    one, two, core = plane_partners()
    greet((one, two, core))

    def block(at, first=0, count=half):
        return out_ref.at[pl.ds(at * half + first, count), :]

    here = pltpu.make_async_copy(own_ref, block(0), local_sem)
    here.start()
    from_one = send(own_ref, block(1), sems, 0, one)
    from_two = send(own_ref, block(2), sems, 1, two)
    copies = [from_one, from_two, send(own_ref, block(4), sems, 2, core)]
    cut = half // 2
    from_one.wait_recv()
    far_low = send(block(1, cut, cut), block(3, cut, cut), sems, 3, two)
    copies.append(send(block(1), block(5), sems, 4, core))
    from_two.wait_recv()
    far_top = send(block(2, 0, cut), block(3, 0, cut), sems, 5, one)
    copies.append(send(block(2), block(6), sems, 6, core))
    far_low.wait_recv()
    far_top.wait_recv()
    copies.append(send(block(3), block(7), sems, 7, core))
    for copy in copies[2:]:
        copy.wait_recv()
    for copy in copies + [far_low, far_top]:
        copy.wait_send()
    here.wait()


def gather_rows(own, collective_id):
    half, width = own.shape
    return pl.pallas_call(
        rows_kernel,
        out_shape=jax.ShapeDtypeStruct((8 * half, width), own.dtype),
        in_specs=[pl.BlockSpec(memory_space=pl.ANY)],
        out_specs=pl.BlockSpec(memory_space=pl.ANY),
        scratch_shapes=[pltpu.SemaphoreType.DMA((2, 8)), pltpu.SemaphoreType.DMA],
        compiler_params=pltpu.CompilerParams(collective_id=collective_id, has_side_effects=True),
        cost_estimate=pl.CostEstimate(flops=1000, bytes_accessed=1000, transcendentals=0),
        name="gather_rows",
    )(own)


def unit_kernel(seq_ref, grad_ref, *refs):
    weights, out_ref = refs[:-1], refs[-1]
    cols = weights[0].shape[1]
    for at, weight_ref in enumerate(weights):
        part = pl.ds(pl.multiple_of((seq_ref[0] ^ at) * cols, 128), cols)
        term = lax.dot_general(
            grad_ref[:, part], weight_ref[...], NT, preferred_element_type=F32
        )
        if at:
            out_ref[...] += term
        else:
            out_ref[...] = term


def unit_grads(seq_at, grads, weights):
    vmem = pl.BlockSpec(memory_space=pltpu.VMEM)
    return pl.pallas_call(
        unit_kernel,
        out_shape=jax.ShapeDtypeStruct((grads.shape[0], weights[0].shape[0]), F32),
        in_specs=[pl.BlockSpec(memory_space=pltpu.SMEM), vmem] + [vmem] * len(weights),
        out_specs=vmem,
        compiler_params=pltpu.CompilerParams(vmem_limit_bytes=40 * 2**20),
        cost_estimate=pl.CostEstimate(flops=1000, bytes_accessed=1000, transcendentals=0),
        name="unit_grads",
    )(seq_at.reshape(1), grads, *weights)


def return_kernel(steps, keep_ref, sent_ref, *refs):
    extras, (out_ref, *refs) = refs[: len(steps)], refs[len(steps) :]
    extra_outs, refs = refs[: len(steps)], refs[len(steps) :]
    land_ref, pass_ref, ring_ref, early_ref, back_ref, sems, extra_sems = refs
    seqs, shards = lax.axis_size("seq"), lax.axis_size("fsdp")
    seq_at, shard_at = lax.axis_index("seq"), lax.axis_index("fsdp")
    rows = out_ref.shape[0]
    core = {"tensor": 1 - lax.axis_index("tensor")}
    behind = {"seq": lax.rem(seq_at + seqs - 1, seqs)}
    ring = [{"fsdp": lax.rem(shard_at + at, shards)} for at in range(1, shards)]
    greet([core, *({"seq": seq_at ^ step} for step in range(1, 4)), *ring])
    slots = [pl.ds(at * rows, rows) for at in range(shards + 1)]
    lands = {
        at: send(sent_ref.at[slots[at], :], land_ref.at[slots[at], :], sems, at, core)
        for at in (*range(1, shards), 0, shards)
    }

    traded = [
        send(source, target, extra_sems, at, {"seq": seq_at ^ step})
        for at, (source, target, step) in enumerate(zip(extras, extra_outs, steps))
    ]

    def chip_sum(at):
        lands[at].wait_recv()
        return keep_ref[slots[at], :] + land_ref[slots[at], :].astype(F32)

    rings = []
    for at in range(1, shards):
        pass_ref[at - 1] = chip_sum(at).astype(BF16)
        rings.append(send(pass_ref.at[at - 1], ring_ref.at[at - 1], sems, shards + at, ring[at - 1]))
    early, own = chip_sum(0), chip_sum(shards)
    for at, copy in enumerate(rings, 1):
        copy.wait_recv()
        piece = ring_ref[at - 1].astype(F32)
        share = jnp.where(shard_at >= at, 1.0, 0.0).astype(F32)
        early = early + piece * share
        own = own + piece * (1.0 - share)
    early_ref[...] = early.astype(BF16)
    shift = send(early_ref, back_ref, sems, 2 * shards, behind)
    shift.wait_recv()
    share = jnp.where(seq_at < seqs - 1, 1.0, 0.0).astype(F32)
    out_ref[...] = own + back_ref[...].astype(F32) * share
    for copy in (*lands.values(), *rings, shift):
        copy.wait_send()
    for copy in traded:
        copy.wait()


def return_pairs(keep, sent, extras, steps, rows, shards, collective_id):
    size = keep.shape[1]
    any_place = [pl.BlockSpec(memory_space=pl.ANY)] * len(steps)
    vmem = pl.BlockSpec(memory_space=pltpu.VMEM)
    return pl.pallas_call(
        functools.partial(return_kernel, steps),
        out_shape=[jax.ShapeDtypeStruct((rows, size), F32)]
        + [jax.ShapeDtypeStruct(value.shape, value.dtype) for value in extras],
        in_specs=[vmem, vmem] + any_place,
        out_specs=[vmem] + any_place,
        scratch_shapes=[
            pltpu.VMEM(sent.shape, BF16),
            pltpu.VMEM((shards - 1, rows, size), BF16),
            pltpu.VMEM((shards - 1, rows, size), BF16),
            pltpu.VMEM((rows, size), BF16),
            pltpu.VMEM((rows, size), BF16),
            pltpu.SemaphoreType.DMA((2, 2 * shards + 1)),
            pltpu.SemaphoreType.DMA((2, len(steps))),
        ],
        compiler_params=pltpu.CompilerParams(
            collective_id=collective_id, has_side_effects=True, vmem_limit_bytes=24 * 2**20
        ),
        cost_estimate=pl.CostEstimate(flops=1000, bytes_accessed=1000, transcendentals=0),
        name="return_pairs",
    )(keep, sent, *extras)


def trade_kernel(to_rows, value_ref, out_ref, sems, local_sems):
    seq_at, core = lax.axis_index("seq"), lax.axis_index("tensor")
    plane_ref, chip_ref = (out_ref, value_ref) if to_rows else (value_ref, out_ref)
    cols, half = plane_ref.shape[1], plane_ref.shape[0] // 8
    greet([{"seq": seq_at ^ step} for step in range(1, 4)])
    copies = []
    for step in (3, 1, 2, 0):
        for at in range(2):
            plane = plane_ref.at[pl.ds((at * 4 + step) * half, half), :]
            rows = pl.ds(pl.multiple_of((core if at == 0 else 1 - core) * half, half), half)
            owner = seq_at ^ step if to_rows else seq_at
            chip = chip_ref.at[rows, pl.ds(pl.multiple_of(owner * cols, 128), cols)]
            source, target = (chip, plane) if to_rows else (plane, chip)
            if step:
                sem_at = 2 * (step - 1) + at
                copies.append(send(source, target, sems, sem_at, {"seq": seq_at ^ step}))
            else:
                here = pltpu.make_async_copy(source, target, local_sems.at[at])
                here.start()
                copies.append(here)
    for copy in copies:
        copy.wait()


def trade(value, to_rows, collective_id):
    rows, cols = value.shape
    return pl.pallas_call(
        functools.partial(trade_kernel, to_rows),
        out_shape=jax.ShapeDtypeStruct(
            (rows * 4, cols // 4) if to_rows else (rows // 4, cols * 4), value.dtype
        ),
        in_specs=[pl.BlockSpec(memory_space=pl.ANY)],
        out_specs=pl.BlockSpec(memory_space=pl.ANY),
        scratch_shapes=[pltpu.SemaphoreType.DMA((2, 6)), pltpu.SemaphoreType.DMA((2,))],
        compiler_params=pltpu.CompilerParams(collective_id=collective_id, has_side_effects=True),
        cost_estimate=pl.CostEstimate(flops=1000, bytes_accessed=1000, transcendentals=0),
        name="trade",
    )(value)


def sum_kernel(
    part_ref, out_ref, own_ref, land_ref, total_ref, near_ref, sems, local_sems
):
    half = out_ref.shape[0]
    cut = half // 2
    chunk = 32
    one, two, core = plane_partners()
    greet((one, two, core))
    order = (3, 1, 2, 0)
    loads, lands = {}, {}
    for at in order:
        loads[at] = pltpu.make_async_copy(
            part_ref.at[pl.ds(at * half, half), :], own_ref.at[at], local_sems.at[at]
        )
        loads[at].start()
        lands[at] = send(
            part_ref.at[pl.ds((4 + at) * half, half), :], land_ref.at[at], sems, at, core
        )
    sent = []
    for at in order:
        loads[at].wait()
        lands[at].wait_recv()

        @pl.loop(0, half // chunk)
        def _(step):
            rows = pl.ds(pl.multiple_of(step * chunk, chunk), chunk)
            value = own_ref[at, rows, :].astype(F32) + land_ref[at, rows, :].astype(F32)
            if at:
                total_ref[at - 1, rows, :] = value.astype(BF16)
            else:
                out_ref[rows, :] = value

        top, low = (total_ref.at[at - 1, pl.ds(first, cut), :] for first in (0, cut))
        if at == 3:
            far_top = send(top, near_ref.at[1], sems, 4, one)
            far_low = send(low, near_ref.at[3], sems, 5, two)
        if at == 1:
            near_top = send(top, near_ref.at[0], sems, 6, one)
        if at == 2:
            near_low = send(low, near_ref.at[2], sems, 7, two)

    def add_in(at, first, from_at):
        @pl.loop(0, cut // chunk)
        def _(step):
            rows = pl.ds(pl.multiple_of(step * chunk, chunk), chunk)
            there = pl.ds(pl.multiple_of(first + step * chunk, chunk), chunk)
            value = total_ref[at, there, :].astype(F32) + near_ref[from_at, rows, :].astype(F32)
            total_ref[at, there, :] = value.astype(BF16)

    far_top.wait_recv()
    add_in(1, 0, 1)
    last_top = send(total_ref.at[1, pl.ds(0, cut), :], near_ref.at[4], sems, 8, two)
    far_low.wait_recv()
    add_in(0, cut, 3)
    last_low = send(total_ref.at[0, pl.ds(cut, cut), :], near_ref.at[5], sems, 9, one)

    for first, near, last, near_at, last_at in (
        (0, near_top, last_top, 0, 4), (cut, near_low, last_low, 2, 5),
    ):
        near.wait_recv()
        last.wait_recv()

        @pl.loop(0, cut // chunk)
        def _(step):
            rows = pl.ds(pl.multiple_of(step * chunk, chunk), chunk)
            there = pl.ds(pl.multiple_of(first + step * chunk, chunk), chunk)
            out_ref[there, :] += near_ref[near_at, rows, :].astype(F32) + near_ref[
                last_at, rows, :
            ].astype(F32)

    for copy in (*lands.values(), far_top, far_low, near_top, near_low, last_top, last_low):
        copy.wait_send()


def scatter_rows(part, collective_id):
    count, width = part.shape
    half = count // 8
    return pl.pallas_call(
        sum_kernel,
        out_shape=jax.ShapeDtypeStruct((half, width), F32),
        in_specs=[pl.BlockSpec(memory_space=pl.ANY)],
        out_specs=pl.BlockSpec(memory_space=pltpu.VMEM),
        scratch_shapes=[
            pltpu.VMEM((4, half, width), BF16),
            pltpu.VMEM((4, half, width), BF16),
            pltpu.VMEM((3, half, width), BF16),
            pltpu.VMEM((6, half // 2, width), BF16),
            pltpu.SemaphoreType.DMA((2, 10)),
            pltpu.SemaphoreType.DMA((4,)),
        ],
        compiler_params=pltpu.CompilerParams(
            collective_id=collective_id, has_side_effects=True, vmem_limit_bytes=40 * 2**20
        ),
        cost_estimate=pl.CostEstimate(flops=1000, bytes_accessed=1000, transcendentals=0),
        name="scatter_rows",
    )(part)


TILE = 256
NT = (((1,), (1,)), ((), ()))
LOWEST = -1e30


def masked_tile(scores, at, tiles, shift):
    scores = scores + shift
    if at in (0, tiles - 1):
        key_at = lax.broadcasted_iota(jnp.int32, scores.shape, 0)
        query_at = lax.broadcasted_iota(jnp.int32, scores.shape, 1)
        allowed = key_at > query_at if at == 0 else key_at <= query_at
        scores = jnp.where(allowed, scores, LOWEST)
    return scores

def tile_shifts(pos_ref, start, tiles):
    return [
        jnp.where(pos_ref[0] - WINDOW + start + at * TILE >= 0, 0.0, LOWEST).astype(F32)
        for at in range(tiles)
    ]

def attend_kernel(pos_ref, q_ref, k_ref, v_ref, out_ref, log_ref, turned_ref, score_ref):
    tiles = WINDOW // TILE + 1

    @pl.when(pl.program_id(0) == 0)
    def _():
        turned_ref[...] = v_ref[...].T

    for start in range(0, q_ref.shape[0], TILE):
        shifts = tile_shifts(pos_ref, start, tiles)
        queries = q_ref[start : start + TILE, :]
        top = jnp.full((1, TILE), LOWEST, F32)
        for at in range(tiles):
            keys = k_ref[start + at * TILE : start + (at + 1) * TILE, :]
            scores = lax.dot_general(keys, queries, NT, preferred_element_type=F32)
            scores = masked_tile(scores, at, tiles, shifts[at])
            score_ref[at] = scores
            top = jnp.maximum(top, jnp.max(scores, axis=0, keepdims=True))
        total = jnp.zeros((1, TILE), F32)
        for at in range(tiles):
            expon = jnp.exp(score_ref[at] - top)
            score_ref[at] = expon
            total = total + jnp.sum(expon, axis=0, keepdims=True)
        inverse = 1.0 / total
        attended = jnp.zeros((v_ref.shape[1], TILE), F32)
        for at in range(tiles):
            probability = (score_ref[at] * inverse).astype(BF16)
            values = turned_ref[:, start + at * TILE : start + (at + 1) * TILE]
            attended = attended + jnp.dot(values, probability, preferred_element_type=F32)
        out_ref[start : start + TILE, :] = attended.T.astype(BF16)
        log_ref[0, :, start : start + TILE] = top + jnp.log(total)

def attend(first_pos, queries, key_rows, value_rows):
    rows, cols = queries.shape
    span, size = key_rows.shape
    heads = cols // size
    return pl.pallas_call(
        attend_kernel,
        out_shape=(
            jax.ShapeDtypeStruct((rows, cols), BF16),
            jax.ShapeDtypeStruct((heads, 1, rows), F32),
        ),
        grid=(heads,),
        in_specs=[
            pl.BlockSpec(memory_space=pltpu.SMEM),
            pl.BlockSpec((rows, size), lambda head: (0, head)),
            pl.BlockSpec((span, size), lambda head: (0, 0)),
            pl.BlockSpec((span, size), lambda head: (0, 0)),
        ],
        out_specs=(
            pl.BlockSpec((rows, size), lambda head: (0, head)),
            pl.BlockSpec((1, 1, rows), lambda head: (head, 0, 0)),
        ),
        scratch_shapes=[
            pltpu.VMEM((size, span), BF16),
            pltpu.VMEM((WINDOW // TILE + 1, TILE, TILE), F32),
        ],
        compiler_params=pltpu.CompilerParams(vmem_limit_bytes=40 * 2**20),
        cost_estimate=pl.CostEstimate(flops=1000, bytes_accessed=1000, transcendentals=0),
        name="attend",
    )(first_pos.reshape(1), queries, key_rows, value_rows)

def attend_back_kernel(
    pos_ref, q_ref, g_ref, k_ref, v_ref, log_ref, cos_ref, sin_ref,
    q_grad_ref, keep_ref, sent_ref, turned_ref, p_ref, gp_ref, k_grad_ref, v_grad_ref,
):
    tiles = WINDOW // TILE + 1
    size = k_ref.shape[1]

    @pl.when(pl.program_id(0) == 0)
    def _():
        turned_ref[...] = k_ref[...].T
        k_grad_ref[...] = jnp.zeros_like(k_grad_ref)
        v_grad_ref[...] = jnp.zeros_like(v_grad_ref)

    for start in range(0, q_ref.shape[0], TILE):
        shifts = tile_shifts(pos_ref, start, tiles)
        block = slice(start, start + TILE)
        queries, grads = q_ref[block, :], g_ref[block, :]
        log_total = log_ref[0, :, block]
        inner = jnp.zeros((1, TILE), F32)
        for at in range(tiles):
            span = slice(start + at * TILE, start + (at + 1) * TILE)
            scores = lax.dot_general(k_ref[span, :], queries, NT, preferred_element_type=F32)
            scores = masked_tile(scores, at, tiles, shifts[at])
            probability = jnp.exp(scores - log_total)
            grad = lax.dot_general(v_ref[span, :], grads, NT, preferred_element_type=F32)
            inner = inner + jnp.sum(probability * grad, axis=0, keepdims=True)
            p_ref[at] = probability
            gp_ref[at] = grad
        query_grad = jnp.zeros((size, TILE), F32)
        for at in range(tiles):
            span = slice(start + at * TILE, start + (at + 1) * TILE)
            probability = p_ref[at]
            score_grad = (probability * (gp_ref[at] - inner)).astype(BF16)
            k_grad_ref[span, :] += jnp.dot(score_grad, queries, preferred_element_type=F32)
            v_grad_ref[span, :] += jnp.dot(
                probability.astype(BF16), grads, preferred_element_type=F32
            )
            query_grad = query_grad + jnp.dot(
                turned_ref[:, span], score_grad, preferred_element_type=F32
            )
        query_grad = query_grad.T * size ** (-0.5)
        turn = cos_ref.shape[1]
        rotated = query_grad[:, :turn]
        rotated = (
            rotated * cos_ref[block, :] + pltpu.roll(rotated, turn // 2, 1) * sin_ref[block, :]
        )
        q_grad_ref[block, :turn] = rotated.astype(BF16)
        q_grad_ref[block, turn:] = query_grad[:, turn:].astype(BF16)

    @pl.when(pl.program_id(0) == pl.num_programs(0) - 1)
    def _():
        first = pos_ref[1] == 0
        for start in range(0, k_ref.shape[0], TILE):
            block = slice(start, start + TILE)
            k_grad, v_grad = k_grad_ref[block, :], v_grad_ref[block, :]
            keep_ref[block, :] = jnp.where(first, k_grad, v_grad)
            sent_ref[block, :] = jnp.where(first, v_grad, k_grad).astype(BF16)


def attend_back(first_pos, core, queries, grads, key_rows, value_rows, log_total, cosine, sine):
    rows, cols = queries.shape
    span, size = key_rows.shape
    heads = cols // size
    by_head = pl.BlockSpec((rows, size), lambda head: (0, head))
    whole = pl.BlockSpec((span, size), lambda head: (0, 0))
    tile_shape = (WINDOW // TILE + 1, TILE, TILE)
    return pl.pallas_call(
        attend_back_kernel,
        out_shape=(
            jax.ShapeDtypeStruct((rows, cols), BF16),
            jax.ShapeDtypeStruct((span, size), F32),
            jax.ShapeDtypeStruct((span, size), BF16),
        ),
        grid=(heads,),
        in_specs=[
            pl.BlockSpec(memory_space=pltpu.SMEM), by_head, by_head, whole, whole,
            pl.BlockSpec((1, 1, rows), lambda head: (head, 0, 0)),
            pl.BlockSpec(cosine.shape, lambda head: (0, 0)),
            pl.BlockSpec(sine.shape, lambda head: (0, 0)),
        ],
        out_specs=(by_head, whole, whole),
        scratch_shapes=[
            pltpu.VMEM((size, span), BF16),
            pltpu.VMEM(tile_shape, F32),
            pltpu.VMEM(tile_shape, F32),
            pltpu.VMEM((span, size), F32),
            pltpu.VMEM((span, size), F32),
        ],
        compiler_params=pltpu.CompilerParams(vmem_limit_bytes=48 * 2**20),
        cost_estimate=pl.CostEstimate(flops=1000, bytes_accessed=1000, transcendentals=0),
        name="attend_back",
    )(jnp.stack([first_pos, core]), queries, grads, key_rows, value_rows, log_total, cosine, sine)

def gelu_parts(gate):
    root = 0.7978845608028654
    square = gate * gate
    tanh = jnp.tanh(root * gate * (1.0 + 0.044715 * square))
    half = 0.5 * (1.0 + tanh)
    slope = half + 0.5 * gate * (1.0 - tanh * tanh) * root * (1.0 + 3 * 0.044715 * square)
    return gate * half, slope

def ffn_kernel(x_ref, w_ref, act_ref, a_ref, b_ref, total_ref):
    steps = 5
    depth = w_ref.shape[0] // steps
    total_ref[...] = jnp.dot(x_ref[:, :depth], w_ref[:depth, :], preferred_element_type=F32)
    for step in range(1, steps):
        part = slice(step * depth, (step + 1) * depth)
        total_ref[...] += jnp.dot(x_ref[:, part], w_ref[part, :], preferred_element_type=F32)
    hidden = act_ref.shape[1]
    main = hidden // 128 * 128
    for start in range(0, main, 128):
        cols = slice(start, start + 128)
        gate, up = total_ref[:, cols], total_ref[:, main + start : main + start + 128]
        gelu, slope = gelu_parts(gate)
        act_ref[:, cols] = (gelu * up).astype(BF16)
        a_ref[:, cols] = (slope * up).astype(BF16)
        b_ref[:, cols] = gelu.astype(BF16)
    last = total_ref[:, 2 * main :]
    up = pltpu.roll(last, 64, 1)
    gelu, slope = gelu_parts(last)
    act_ref[:, main:] = (gelu * up)[:, :64].astype(BF16)
    a_ref[:, main:] = (slope * up)[:, :64].astype(BF16)
    b_ref[:, main:] = gelu[:, :64].astype(BF16)

def ffn(x, w, rows=512):
    count, width = x.shape
    hidden = w.shape[1] // 2
    tile = pl.BlockSpec((rows, hidden), lambda i: (i, 0))
    return pl.pallas_call(
        ffn_kernel,
        out_shape=(jax.ShapeDtypeStruct((count, hidden), BF16),) * 3,
        grid=(count // rows,),
        in_specs=[
            pl.BlockSpec((rows, width), lambda i: (i, 0)),
            pl.BlockSpec(w.shape, lambda i: (0, 0), pipeline_mode=pl.Buffered(1)),
        ],
        out_specs=(tile,) * 3,
        scratch_shapes=[pltpu.VMEM((rows, 2 * hidden), F32)],
        compiler_params=pltpu.CompilerParams(vmem_limit_bytes=56 * 2**20),
        cost_estimate=pl.CostEstimate(flops=1000, bytes_accessed=1000, transcendentals=0),
        name="ffn",
    )(x, w)

def ffn_back_kernel(c_ref, d_ref, a_ref, b_ref, w_ref, g_ref, out_ref):
    hidden = a_ref.shape[1]
    main = hidden // 128 * 128
    act_grad = lax.dot_general(c_ref[...], d_ref[...], NT, preferred_element_type=F32)
    g_ref[:, :main] = (act_grad[:, :main] * a_ref[:, :main].astype(F32)).astype(BF16)
    g_ref[:, main : 2 * main] = (act_grad[:, :main] * b_ref[:, :main].astype(F32)).astype(BF16)
    last = act_grad[:, main:]
    g_ref[:, 2 * main :] = jnp.concatenate(
        [last * a_ref[:, main:].astype(F32), last * b_ref[:, main:].astype(F32)], axis=1
    ).astype(BF16)
    out_ref[...] = lax.dot_general(
        g_ref[...], w_ref[...], NT, preferred_element_type=F32
    ).astype(BF16)

def ffn_back(cot, down, a, b, w, rows=256):
    count, width = cot.shape
    hidden = a.shape[1]
    by_rows = lambda cols: pl.BlockSpec((rows, cols), lambda i: (i, 0))
    once = lambda v: pl.BlockSpec(v.shape, lambda i: (0, 0), pipeline_mode=pl.Buffered(1))
    return pl.pallas_call(
        ffn_back_kernel,
        out_shape=(
            jax.ShapeDtypeStruct((count, 2 * hidden), BF16),
            jax.ShapeDtypeStruct((count, width), BF16),
        ),
        grid=(count // rows,),
        in_specs=[by_rows(width), once(down), by_rows(hidden), by_rows(hidden), once(w)],
        out_specs=(by_rows(2 * hidden), by_rows(width)),
        compiler_params=pltpu.CompilerParams(vmem_limit_bytes=56 * 2**20),
        cost_estimate=pl.CostEstimate(flops=1000, bytes_accessed=1000, transcendentals=0),
        name="ffn_back",
    )(cot, down, a, b, w)


def join_kernel(seq_ref, *refs):
    pieces, (gate_w_ref, up_w_ref, gate_ref, up_ref, gain_ref) = refs[:4], refs[4:]
    hidden = pieces[0].shape[1] // 2
    main, rest = hidden // 128 * 128, hidden % 128
    for seq_at in range(4):

        @pl.when(seq_ref[0] == seq_at)
        def _():
            gain = jnp.zeros((gate_ref.shape[0], 1), F32)
            for out_ref, w_ref, spans in (
                (gate_ref, gate_w_ref, ((0, main), (2 * main, rest))),
                (up_ref, up_w_ref, ((main, main), (2 * main + rest, rest))),
            ):
                grad = jnp.concatenate(
                    [
                        pieces[at ^ seq_at][:, start : start + count].astype(F32)
                        for at in range(4)
                        for start, count in spans
                    ],
                    axis=1,
                )
                out_ref[...] = grad
                gain += jnp.sum(grad * w_ref[...].astype(F32), axis=1, keepdims=True)
            gain_ref[...] = gain


def join_columns(seq_at, pieces, w_gate, w_up):
    rows, cols = w_gate.shape
    tile = 64
    by_rows = lambda width: pl.BlockSpec((tile, width), lambda i: (i, 0))
    whole = jax.ShapeDtypeStruct((rows, cols), F32)
    gate, up, gain = pl.pallas_call(
        join_kernel,
        out_shape=(whole, whole, jax.ShapeDtypeStruct((rows, 1), F32)),
        grid=(rows // tile,),
        in_specs=[pl.BlockSpec(memory_space=pltpu.SMEM)]
        + [by_rows(pieces[0].shape[1])] * 4 + [by_rows(cols)] * 2,
        out_specs=(by_rows(cols), by_rows(cols), by_rows(1)),
        compiler_params=pltpu.CompilerParams(vmem_limit_bytes=40 * 2**20),
        cost_estimate=pl.CostEstimate(flops=1000, bytes_accessed=1000, transcendentals=0),
        name="join_columns",
    )(seq_at.reshape(1), *pieces, w_gate, w_up)
    return gate, up, gain[:, 0]


def local(
    inputs, cotangent, gain_attn, gain_ffn, w_query, w_key, w_value, w_out, w_gate, w_up, w_down
):
    rows, width = inputs.shape
    half = rows // 2
    head_size = w_key.shape[1]
    head_cols = w_query.shape[1]
    heads_here = head_cols // head_size
    seqs, shards = lax.axis_size("seq"), lax.axis_size("fsdp")
    assert rows * shards == WINDOW and lax.axis_size("tensor") == 2
    seq_at, shard_at, core = (lax.axis_index(name) for name in ("seq", "fsdp", "tensor"))
    first = core == 0
    key_span = rows + WINDOW
    first_pos = (seq_at * shards + shard_at) * rows
    scale = head_size ** (-0.5)
    rot_half = head_size // 4
    frequency = 10000.0 ** (-(jnp.arange(rot_half, dtype=F32) * 2.0) / (2 * rot_half))
    angles = (first_pos + jnp.arange(rows, dtype=jnp.int32)).astype(F32)[:, None] * frequency[None]
    cosine, sine = jnp.cos(angles), jnp.sin(angles)

    def my_half(value):
        return part_of(value, core, half, 0)

    def other_half(value):
        return part_of(value, 1 - core, half, 0)

    def whole_rows(own):
        other = swap(own)
        return jnp.where(first, jnp.stack([own, other]), jnp.stack([other, own])).reshape(
            rows, own.shape[1]
        )

    def plane_rows(own, other=None):
        near = plane_gather(own)
        far = [swap(piece) if at or other is None else other for at, piece in enumerate(near)]
        return jnp.concatenate(near + far, axis=0)

    def core_sum(partial):
        count = seqs * half
        cores = partial[:count].astype(F32) + swap(partial[count:].astype(BF16)).astype(F32)
        return [cores[j * half : (j + 1) * half] for j in range(seqs)]

    def plane_sum(partial):
        parts = core_sum(partial)
        return scatter_end(*scatter_far(parts, scatter_near(parts)))

    def order_cols(pieces):
        stacked = jnp.stack(pieces)
        return [pick(stacked, seq_at ^ at) for at in range(seqs)]

    def order_rows(pieces):
        count, width = pieces[0].shape
        rows_all = jnp.zeros((seqs * count, width), F32)
        for at, piece in enumerate(pieces):
            rows_all = lax.dynamic_update_slice_in_dim(
                rows_all, piece.astype(F32), (seq_at ^ at) * count, 0
            )
        return rows_all

    gain_one, gain_two = gain_attn.astype(F32)[:, None], gain_ffn.astype(F32)[:, None]
    gains = jnp.stack([gain_attn, gain_ffn])
    gains = jnp.stack(
        [gains]
        + [
            lax.ppermute(gains, "fsdp", [((at + by) % shards, at) for at in range(shards)])
            for by in range(1, shards)
        ]
    )
    gains = jnp.concatenate(
        [pick(gains, (at - shard_at) % shards) for at in range(shards)], axis=1
    ).astype(F32)
    pair_shard = jnp.where(first, w_key, w_value)
    proj_shard = jnp.concatenate([w_query, pair_shard], axis=1)
    proj_cols = proj_shard.shape[1] // seqs
    out_rows = head_cols // seqs
    proj_weight = lax.all_gather(
        part_of(proj_shard, seq_at, proj_cols, 1), "fsdp", axis=0, tiled=True
    )
    hidden = w_gate.shape[1] // seqs
    kernels = hidden % 128 == 64
    main = hidden // 128 * 128 if kernels else hidden
    gate_mine, up_mine = (part_of(value, seq_at, hidden, 1) for value in (w_gate, w_up))
    pair_in = jnp.concatenate(
        [gate_mine[:, :main], up_mine[:, :main], gate_mine[:, main:], up_mine[:, main:]], axis=1
    )
    in_weight = lax.all_gather(pair_in, "fsdp", axis=0, tiled=True)
    down_weight = lax.all_gather(
        part_of(w_down, seq_at, hidden, 0), "fsdp", axis=1, tiled=True
    )

    source = my_half(inputs).astype(F32)
    inverse_one = inverse_rms(source)
    unit_one = (source * inverse_one * gains[0]).astype(BF16)
    square = seqs == 4
    out_quarter = lax.all_gather(
        part_of(w_out, seq_at, out_rows, 0), "fsdp", axis=1, tiled=True
    )
    rows_one = gather_rows(unit_one, 1) if square else plane_rows(unit_one)
    proj = jnp.dot(rows_one, proj_weight, preferred_element_type=F32)
    rotate_first = proj_cols % (2 * rot_half) == 0
    if rotate_first:
        halves_at = jnp.where(first, jnp.arange(2), 1 - jnp.arange(2))[:, None, None]
        seqs_at = (seq_at ^ jnp.arange(seqs))[None, :, None]
        row_pos = (
            (seqs_at * shards + shard_at) * rows + halves_at * half + jnp.arange(half)[None, None]
        ).reshape(-1)
        row_angles = row_pos.astype(F32)[:, None] * frequency[None]
        units = proj_cols // (2 * rot_half)
        unit_at = seq_at * units + jnp.arange(units)
        head_units = head_cols // (2 * rot_half)
        turned = (unit_at % 2 == 0) & (first | (unit_at < head_units))
        unit_scale = jnp.where(unit_at < head_units, scale, 1.0)[None, :, None]
        turned = turned[None, :, None]
        row_cos = jnp.where(turned, jnp.cos(row_angles)[:, None], 1.0) * unit_scale
        row_sin = jnp.where(turned, jnp.sin(row_angles)[:, None], 0.0) * unit_scale
        proj = rotate(proj.reshape(-1, units, 2 * rot_half), row_cos, row_sin)
    proj = proj.astype(BF16).reshape(2 * seqs * half, proj_cols)
    if square and rotate_first:
        proj_here = trade(proj, False, 5)
    else:
        proj = proj.reshape(2, seqs, half, proj_cols)
        proj = jnp.where(first, proj, proj[::-1])
        proj_parts = [proj[:, 0].reshape(rows, proj_cols)] + [
            exchange(proj[:, at].reshape(rows, proj_cols), at) for at in range(1, seqs)
        ]
        proj_here = jnp.concatenate(order_cols(proj_parts), axis=1)
    queries = proj_here[:, :head_cols]
    pair_here = proj_here[:, head_cols:]
    if not rotate_first:
        queries = queries.reshape(rows, heads_here, head_size).astype(F32)
        queries = (rotate(queries, cosine[:, None], sine[:, None]) * scale).astype(BF16)
        queries = queries.reshape(rows, head_cols)
        pair_here = jnp.where(first, rotate(pair_here.astype(F32), cosine, sine), pair_here)
        pair_here = pair_here.astype(BF16)

    earlier = seq_shift(pair_here, 1)
    slots = [
        lax.ppermute(
            jnp.where(shard_at >= at, earlier, pair_here),
            "fsdp", [(source_at, (source_at - at) % shards) for source_at in range(shards)],
        )
        for at in range(1, shards)
    ]
    window_here = jnp.concatenate([earlier] + slots + [pair_here], axis=0)
    window_here, *out_pieces = lax.optimization_barrier((window_here, *plane_gather(out_quarter)))
    window_other = swap(window_here)
    key_rows = jnp.where(first, window_here, window_other)
    value_rows = jnp.where(first, window_other, window_here)

    out_weight = jnp.zeros((head_cols, width), BF16)
    for at, piece in enumerate(out_pieces):
        out_weight = lax.dynamic_update_slice_in_dim(
            out_weight, piece, (seq_at ^ at) * out_rows, 0
        )

    head_outputs, log_total = attend(first_pos, queries, key_rows, value_rows)

    out_part = jnp.dot(head_outputs, out_weight, preferred_element_type=F32)
    hidden_in = source + my_half(out_part) + swap(other_half(out_part))
    inverse_two = inverse_rms(hidden_in)
    unit_two = (hidden_in * inverse_two * gains[1]).astype(BF16)
    rows_two = gather_rows(unit_two, 2) if square else plane_rows(unit_two)
    cot_later = after(cotangent, out_weight)
    rows_cot = plane_rows(my_half(cot_later), other_half(cot_later))

    if kernels:
        activation, gate_factor, up_factor = ffn(rows_two, in_weight)
        down_term = rows_product(rows_cot, activation).astype(BF16)
        gate_factor, proj_later, _ = lax.optimization_barrier(
            (gate_factor, proj_weight, down_term)
        )
        grad_in, back_part = ffn_back(rows_cot, down_weight, gate_factor, up_factor, in_weight)
    else:
        in_proj = jnp.dot(rows_two, in_weight, preferred_element_type=F32)
        gate_pre, up_proj = in_proj[:, :hidden], in_proj[:, hidden:]
        activation = gated_unit(gate_pre, up_proj).astype(BF16)
        down_term = rows_product(rows_cot, activation).astype(BF16)
        grad_activation = times_transpose(rows_cot, down_weight)
        grad_gate, grad_up = jax.vjp(gated_unit, gate_pre, up_proj)[1](grad_activation)
        grad_in = jnp.concatenate([grad_gate.astype(BF16), grad_up.astype(BF16)], axis=1)
        back_part = times_transpose(grad_in, in_weight)
        proj_later = after(proj_weight, down_term)
    grad_in, proj_near = lax.optimization_barrier((grad_in, gather_near(proj_later)))
    proj_pieces = gather_far(proj_later, proj_near)
    in_term = rows_product(rows_two, grad_in).astype(BF16)
    back_part, proj_pieces, in_term = lax.optimization_barrier((back_part, proj_pieces, in_term))
    grad_unit_two = scatter_rows(back_part, 3) if square else plane_sum(back_part)
    grad_hidden = my_half(cotangent).astype(F32) + norm_pull(
        hidden_in, inverse_two, grad_unit_two * gains[1]
    )
    down_shard = lax.psum_scatter(down_term, "fsdp", scatter_dimension=0, tiled=True).T
    in_shard = lax.psum_scatter(in_term, "fsdp", scatter_dimension=0, tiled=True)

    grad_attn_out = whole_rows(grad_hidden.astype(BF16))
    out_term = rows_product(head_outputs, grad_attn_out).astype(BF16)
    grad_attn_out, down_shard, out_term = lax.optimization_barrier(
        (grad_attn_out, down_shard, out_term)
    )
    grad_heads = times_transpose(grad_attn_out, out_weight).astype(BF16)
    out_parts = [part_of(out_term, seq_at ^ at, out_rows, 0) for at in range(seqs)]
    out_near = scatter_near(out_parts)
    grad_query_proj, pair_keep, pair_sent = attend_back(
        first_pos, core, queries, grad_heads, key_rows, value_rows, log_total,
        jnp.concatenate([cosine, cosine], axis=1), jnp.concatenate([sine, -sine], axis=1),
    )
    pair_sent, down_near = lax.optimization_barrier((pair_sent, gather_near(down_shard)))
    count = seqs * half
    activation = after(activation, pair_sent)
    ffn_other = jnp.dot(activation[count:], down_weight, preferred_element_type=F32)
    ffn_other, out_near = lax.optimization_barrier((ffn_other, out_near))
    ffn_part = jnp.dot(
        after(activation[:count], ffn_other), down_weight, preferred_element_type=F32
    )
    ffn_part, ffn_other = lax.optimization_barrier(
        (ffn_part.astype(BF16), swap(ffn_other.astype(BF16)))
    )
    ffn_part = (ffn_part.astype(F32) + ffn_other.astype(F32)).astype(BF16)
    ffn_cores = [ffn_part[j * half : (j + 1) * half] for j in range(seqs)]
    ffn_near = scatter_near(ffn_cores)
    pair_keep, pair_sent, _ = lax.optimization_barrier((pair_keep, pair_sent, ffn_part))
    out_sum, out_far = scatter_far(out_parts, out_near, not square)
    if square:
        down_cut = down_shard.shape[0] // 2
        extras = [*out_far, down_near[1][:down_cut], down_near[0][down_cut:]]
        own_total, out_top, out_low, down_top, down_low = return_pairs(
            pair_keep, pair_sent, extras, (2, 1, 1, 2), rows, shards, 7
        )
        out_far = [out_top, out_low]
        down_parts = [down_shard, *down_near, jnp.concatenate([down_top, down_low], axis=0)]
    else:
        pair_grads = pair_keep + swap(pair_sent).astype(F32)
        own_total = pair_grads[shards * rows :]
        earlier_total = pair_grads[:rows]
        for at in range(1, shards):
            piece = lax.ppermute(
                pair_grads[at * rows : (at + 1) * rows].astype(BF16),
                "fsdp",
                [((source_at - at) % shards, source_at) for source_at in range(shards)],
            ).astype(F32)
            own_total = own_total + jnp.where(shard_at >= at, 0.0, piece)
            earlier_total = earlier_total + jnp.where(shard_at >= at, piece, 0.0)
        own_total = own_total + seq_shift(earlier_total.astype(BF16), -1).astype(F32)
        down_parts = gather_far(down_shard, down_near)
    own_total, ffn_near = lax.optimization_barrier((own_total, ffn_near))
    grad_pair = jnp.where(first, rotate(own_total, cosine, -sine), own_total).astype(BF16)
    grad_pair, in_shard = lax.optimization_barrier((grad_pair, in_shard))
    grad_proj = jnp.concatenate([grad_query_proj, grad_pair], axis=1)
    if square:
        grad_rows = trade(grad_proj, True, 6)
    else:
        grad_parts = [part_of(grad_proj, seq_at, proj_cols, 1)] + [
            exchange(part_of(grad_proj, seq_at ^ at, proj_cols, 1), at) for at in range(1, seqs)
        ]
        grad_rows = jnp.stack(grad_parts).reshape(seqs, 2, half, proj_cols).swapaxes(0, 1)
        grad_rows = jnp.where(first, grad_rows, grad_rows[::-1])
        grad_rows = grad_rows.reshape(2 * seqs * half, proj_cols)
    proj_term = rows_product(rows_one, grad_rows).astype(BF16)

    out_sum = scatter_end(out_sum, after(out_far, proj_term))
    last_term = jnp.concatenate([proj_term, out_sum.astype(BF16).T], axis=1)
    last_sum = lax.psum_scatter(last_term, "fsdp", scatter_dimension=0, tiled=True)
    in_near = gather_near(after(in_shard, grad_rows))
    grad_proj = after(grad_proj, proj_term)
    if square:
        unit_part = unit_grads(seq_at, grad_proj, proj_pieces)
    else:
        unit_part = sum(
            times_transpose(part_of(grad_proj, seq_at ^ at, proj_cols, 1), proj_pieces[at])
            for at in range(seqs)
        )
    down_grad = order_rows(after(down_parts, grad_rows))
    ffn_sum, ffn_far = scatter_far(ffn_cores, after(ffn_near, proj_term))
    in_near, unit_part, down_grad = lax.optimization_barrier((in_near, unit_part, down_grad))
    in_parts = gather_far(in_shard, in_near)
    grad_unit_one = my_half(unit_part) + swap(other_half(unit_part))
    layer_half = (hidden_in + scatter_end(ffn_sum, ffn_far)).astype(BF16)
    grad_half = grad_hidden + norm_pull(source, inverse_one, grad_unit_one * gains[0])
    in_parts, last_near = lax.optimization_barrier((in_parts, gather_near(last_sum)))
    last_parts = gather_far(last_sum, last_near)
    layer_out, grad_input = whole_rows(layer_half), whole_rows(grad_half)
    if kernels and square:
        gate_grad, up_grad, gain_two_half = join_columns(seq_at, in_parts, w_gate, w_up)
    else:
        in_parts = order_cols(in_parts)
        rest = hidden - main
        gate_grad, up_grad = (
            jnp.concatenate(
                [
                    piece[:, first_at : first_at + count]
                    for piece in in_parts
                    for first_at, count in spans
                    if count
                ],
                axis=1,
            ).astype(F32)
            for spans in (((0, main), (2 * main, rest)), ((main, main), (2 * main + rest, rest)))
        )
        gain_two_half = jnp.sum(
            gate_grad * w_gate.astype(F32) + up_grad * w_up.astype(F32), axis=1
        )
    gain_two_half = gain_two_half / gain_two[:, 0]
    last_parts = after(last_parts, gate_grad)
    out_grad = order_rows([piece[:, proj_cols:].T for piece in last_parts])
    proj_grad = jnp.concatenate(
        order_cols([piece[:, :proj_cols] for piece in last_parts]), axis=1
    ).astype(F32)
    gain_one_half = jnp.sum(proj_grad * proj_shard.astype(F32), axis=1) / gain_one[:, 0]
    query_grad = proj_grad[:, :head_cols]
    pair_grad = proj_grad[:, head_cols:]
    pair_other = swap(pair_grad)
    gain_grads = jnp.stack([gain_one_half, gain_two_half])
    gain_grads = gain_grads + swap(gain_grads)
    return (
        layer_out,
        grad_input,
        gain_grads[0],
        gain_grads[1],
        query_grad,
        jnp.where(first, pair_grad, pair_other),
        jnp.where(first, pair_other, pair_grad),
        out_grad,
        gate_grad,
        up_grad,
        down_grad,
    )


def solution(mesh):
    rows = P(("seq", "fsdp"), None)
    specs = (
        P("fsdp"),
        P("fsdp"),
        P("fsdp", "tensor"),
        P("fsdp", None),
        P("fsdp", None),
        P("tensor", "fsdp"),
        P("fsdp", "tensor"),
        P("fsdp", "tensor"),
        P("tensor", "fsdp"),
    )
    return jax.shard_map(
        local, mesh=mesh, in_specs=(rows, rows) + specs, out_specs=(rows, rows) + specs,
        check_vma=False,
    )
```
